32 devices in a mesh: seq: 8 (over y, x, core), head: 4 (over z).
Axes of the slice: x: 2, y: 2, z: 4, core: 2. Of those that a mesh axis runs over, the one named last changes fastest.
Arguments:
- inputs: bfloat16 [8192, 2048], P(('seq', 'head')), may hold values from -6 to 6
- out_grad: bfloat16 [8192, 2048], P(('seq', 'head')), may hold values from -6 to 6
- q_weight: bfloat16 [2048, 2048], P('seq', 'head'), may hold values from -0.125 to 0.125
- q_bias: bfloat16 [2048], P(('seq', 'head')), may hold values from -4 to 4
- kv_weight: bfloat16 [2048, 512], P(('seq', 'head')), may hold values from -0.125 to 0.125
- kv_bias: bfloat16 [512], P(('seq', 'head')), may hold values from -4 to 4
- out_weight: bfloat16 [2048, 2048], P('head', 'seq'), may hold values from -0.75 to 0.75
- attn_gain: bfloat16 [2048], P(('seq', 'head')), may hold values from 0.5 to 1.5
- ffn_gain: bfloat16 [2048], P(('seq', 'head')), may hold values from 0.5 to 1.5
- gate_weight: bfloat16 [2048, 11008], P('seq', 'head'), may hold values from -0.125 to 0.125
- up_weight: bfloat16 [2048, 11008], P('seq', 'head'), may hold values from -0.125 to 0.125
- down_weight: bfloat16 [11008, 2048], P('head', 'seq'), may hold values from -0.0546875 to 0.0546875
- block_order: int32 [16], replicated, may hold values from 0 to 15, as said below
- long_docs: int32 [8], replicated, may hold values from 1 to 3584, 7168 in all
- short_docs: int32 [4], replicated, may hold values from 1 to 512, 1024 in all
Outputs:
- output: float32 [8192, 2048], P(('seq', 'head'))
- input_grad: float32 [8192, 2048], P(('seq', 'head'))
- q_weight_grad: float32 [2048, 2048], P('seq', 'head')
- q_bias_grad: float32 [2048], P(('seq', 'head'))
- kv_weight_grad: float32 [2048, 512], P(('seq', 'head'))
- kv_bias_grad: float32 [512], P(('seq', 'head'))
- out_weight_grad: float32 [2048, 2048], P('head', 'seq')
- attn_gain_grad: float32 [2048], P(('seq', 'head'))
- ffn_gain_grad: float32 [2048], P(('seq', 'head'))
- gate_weight_grad: float32 [2048, 11008], P('seq', 'head')
- up_weight_grad: float32 [2048, 11008], P('seq', 'head')
- down_weight_grad: float32 [11008, 2048], P('head', 'seq')
The draws below stay inside these ranges and needn't reach their ends.
Inputs may be any that keep to these rules, and one draw needn't show every extreme that they name: `block_order`: a permutation of the blocks in which storage blocks 2k and 2k + 1 hold a block b < 8 and the block 15 - b. `long_docs`: lay the first row end to end; the largest is 3584. `short_docs`: lay the second row end to end; the largest is 512.
All inputs are finite; a program needn't handle non-finite values.
Results may differ from the reference program's by a relative error of at most 0.023.
Values may be sent and summed in bfloat16 or wider, within the bound.
No kernel may reach another device: no remote copies, remote signals or barrier semaphores. Data moves between devices by JAX's collectives and lax.ppermute only.
A program may use at most 256 MiB of HBM per device.

```python
import math
import jax
import jax.numpy as jnp
import numpy as np
from jax import lax

D = 2048
HEADS = 16
KV = 2
HD = 128
FF = 11008
BLK = 512
DOCS_LONG = 8
DOCS_SHORT = 4
QW = 2048
KVW = 512
NB = 16
TOTAL = 8192
SHORT = 1024
LONG = 7168


def draw_block_order(key, part):
    lower_half = jax.random.permutation(key, NB // 2).astype(jnp.int32)
    mirrored = NB - 1 - lower_half
    return jnp.stack([lower_half, mirrored], axis=1).reshape(NB).astype(jnp.int32)


def level_of(key, extent, split, low, top_value):
    def one(axis_at, blocks):
        steps = jax.random.uniform(jax.random.fold_in(jax.random.fold_in(key, 6), axis_at), (blocks,), jnp.float32, low / len(split), top_value / len(split))
        return jnp.repeat(jnp.exp(steps), extent[axis_at] // blocks).reshape((-1,) + (1,) * (len(extent) - axis_at - 1))

    gain = one(*split[0])
    for cut in split[1:]:
        gain = gain * one(*cut)
    return gain


def split_up(count, total, limit, slope):
    loads = [(1 << 20) // math.isqrt(rank ** slope) + 1 for rank in range(2, count + 1)]
    rest, given = total - limit - (count - 1), [1] * (count - 1)
    while rest > 0:
        candidates = [i for i in range(count - 1) if given[i] < limit]
        pool, remaining = sum([loads[i] for i in candidates]), rest
        for i in candidates:
            extra = min(limit - given[i], max(1, remaining * loads[i] // pool), rest)
            given[i] = given[i] + extra
            rest = rest - extra
    return np.array([limit] + given)


def ragged_sizes(rng, count, total, most, lean):
    if count == 2:
        one = jax.random.randint(rng, (), max(1, total - most), min(most, total - 1) + 1)
        return jnp.stack([one, total - one])
    tallies = jnp.asarray(split_up(count, total, most, lean), jnp.int32)
    twos = (count - 1) // 2
    giver, taker = tallies[1:1 + 2 * twos:2], tallies[2:2 + 2 * twos:2]
    slack = jnp.minimum(giver - 1, most - taker)
    moved = jax.random.randint(jax.random.fold_in(rng, 1), (twos,), 0, 1 << 20) % (slack + 1)
    tallies = tallies.at[1:1 + 2 * twos:2].set(giver - moved).at[2:2 + 2 * twos:2].set(taker + moved)
    return tallies[jax.random.permutation(jax.random.fold_in(rng, 2), count)]


def normal_values(rng, shape, scale, bound, shards=(), held_as=jnp.bfloat16):
    factor_of = level_of(rng, shape, shards, -0.22, 0.18) if shards else 1.0
    array = jax.random.normal(rng, shape, jnp.float32) * scale * factor_of
    return jnp.minimum(jnp.maximum(array, -bound), bound).astype(held_as)


def setup_inputs(seed: int = 0) -> dict:
    key_list = jax.random.split(jax.random.key(seed), 16)
    return {
        "inputs": normal_values(key_list[0], (TOTAL, D), 1.0, 6.0, ((0, 32),)),
        "out_grad": normal_values(key_list[1], (TOTAL, D), 1.0, 6.0, ((0, 32),)),
        "q_weight": normal_values(key_list[2], (D, QW), D ** -0.5, 0.125, ((0, 8), (1, 4))),
        "q_bias": normal_values(key_list[3], (QW,), 0.3, 4.0, ((0, 32),)),
        "kv_weight": normal_values(key_list[4], (D, KVW), D ** -0.5, 0.125, ((0, 32),)),
        "kv_bias": normal_values(key_list[5], (KVW,), 0.3, 4.0, ((0, 32),)),
        "out_weight": normal_values(key_list[6], (QW, D), (QW // 32) ** -0.5, 0.75, ((0, 4), (1, 8))),
        "attn_gain": jnp.clip(1.0 + 0.1 * jax.random.normal(key_list[7], (D,), jnp.float32), 0.5, 1.5).astype(jnp.bfloat16),
        "ffn_gain": jnp.clip(1.0 + 0.1 * jax.random.normal(key_list[8], (D,), jnp.float32), 0.5, 1.5).astype(jnp.bfloat16),
        "gate_weight": normal_values(key_list[9], (D, FF), D ** -0.5, 0.125, ((0, 8), (1, 4))),
        "up_weight": normal_values(key_list[10], (D, FF), D ** -0.5, 0.125, ((0, 8), (1, 4))),
        "down_weight": normal_values(key_list[11], (FF, D), FF ** -0.5, 0.0546875, ((0, 4), (1, 8))),
        "block_order": draw_block_order(jax.random.fold_in(key_list[15], 71), 0),
        "long_docs": ragged_sizes(key_list[13], DOCS_LONG, LONG, LONG // 2, 2).astype(jnp.int32),
        "short_docs": ragged_sizes(key_list[14], DOCS_SHORT, SHORT, SHORT // 2, 2).astype(jnp.int32),
    }


EPSILON = 1e-06
ROPE_BASE = 1000000.0
NEGATIVE = -1e+30
HIGHEST = lax.Precision.HIGHEST

@jax.custom_vjp
def low(v):
    return lax.optimization_barrier(v.astype(jnp.bfloat16)).astype(jnp.float32)

@jax.custom_vjp
def low_back(v):
    return v

def low_keep(v):
    return (low(v), None)

def low_pass(kept, grad):
    return (grad,)

def back_keep(v):
    return (v, None)

def back_low(kept, grad):
    return (low(grad),)
low.defvjp(low_keep, low_pass)
low_back.defvjp(back_keep, back_low)

def stream_layout(block_order, long_docs, short_docs):
    within = jnp.arange(BLK, dtype=jnp.int32)
    stream_index = (block_order[:, None] * BLK + within[None, :]).reshape(-1).astype(jnp.int32)
    long_ends = jnp.cumsum(long_docs).astype(jnp.int32)
    short_ends = jnp.cumsum(short_docs).astype(jnp.int32)
    long_total = long_ends[-1]
    second_row = stream_index >= long_total
    position = jnp.where(second_row, stream_index - long_total, stream_index)
    first_doc = lax.optimization_barrier(jnp.sum((position[:, None] >= long_ends[None, :]).astype(jnp.int32), axis=1))
    second_doc = lax.optimization_barrier(jnp.sum((position[:, None] >= short_ends[None, :]).astype(jnp.int32), axis=1)) + long_docs.shape[0]
    document = jnp.where(second_row, second_doc, first_doc).astype(jnp.int32)
    return (stream_index, position, document)

def rope_tables(position):
    half_width = HD // 2
    inverse = ROPE_BASE ** (-(jnp.arange(half_width, dtype=jnp.float32) * 2.0 / HD))
    angles = position.astype(jnp.float32)[:, None] * inverse[None, :]
    angles = jnp.concatenate([angles, angles], axis=1)
    return (jnp.cos(angles), jnp.sin(angles))

def rotate(values, cosine, sine_table):
    half_width = values.shape[-1] // 2
    turned = jnp.concatenate([-values[..., half_width:], values[..., :half_width]], axis=-1)
    return values * cosine + turned * sine_table

def norm_apply(values, gain_vector):
    rms_scale = lax.rsqrt(lax.optimization_barrier(jnp.mean(values * values, axis=1, keepdims=True)) + EPSILON)
    return values * rms_scale * gain_vector

def reference(inputs, out_grad, q_weight, q_bias, kv_weight, kv_bias, out_weight, attn_gain, ffn_gain, gate_weight, up_weight, down_weight, block_order, long_docs, short_docs):
    stream_index, position, document = stream_layout(block_order, long_docs, short_docs)
    cosine, sine_table = rope_tables(position)
    group_size = HEADS // KV
    factor = HD ** (-0.5)

    def attend_block(key_rows, value_rows, portion):
        block_queries, block_stream, block_doc = portion
        raw_scores = jnp.einsum('bkgd,tkd->kgbt', block_queries, key_rows, precision=HIGHEST)
        scores = low_back(raw_scores) * factor
        allowed = (block_doc[:, None] == document[None, :]) & (stream_index[None, :] <= block_stream[:, None])
        masked = jnp.where(allowed[None, None], scores, NEGATIVE)
        row_top = lax.optimization_barrier(jnp.max(masked, axis=3, keepdims=True))
        exponent = jnp.where(allowed[None, None], jnp.exp(masked - row_top), 0.0)
        probabilities = low(exponent / lax.optimization_barrier(jnp.sum(exponent, axis=3, keepdims=True)))
        return jnp.einsum('kgbt,tkd->bkgd', probabilities, value_rows, precision=HIGHEST)
    checkpointed = jax.checkpoint(attend_block)

    def layer(inputs32, q_weight32, q_bias32, kv_weight32, kv_bias32, out_weight32, attn_gain32, ffn_gain32, gate32, up32, down32):
        normed = low(norm_apply(inputs32, attn_gain32))
        query_raw = low_back(jnp.dot(normed, q_weight32, precision=HIGHEST) + q_bias32)
        queries = low(rotate(query_raw.reshape(TOTAL, HEADS, HD), cosine[:, None, :], sine_table[:, None, :]))
        kv_raw = low_back(jnp.dot(normed, kv_weight32, precision=HIGHEST) + kv_bias32)
        key_rows = low(rotate(kv_raw[:, :KV * HD].reshape(TOTAL, KV, HD), cosine[:, None, :], sine_table[:, None, :]))
        value_rows = low(kv_raw[:, KV * HD:].reshape(TOTAL, KV, HD))
        grouped = queries.reshape(NB, BLK, KV, group_size, HD)
        mixed_heads = lax.map(lambda portion: checkpointed(key_rows, value_rows, portion), (grouped, stream_index.reshape(NB, BLK), document.reshape(NB, BLK)))
        mixed_heads = low(low_back(mixed_heads.reshape(TOTAL, HEADS * HD)))
        hidden = inputs32 + low_back(jnp.dot(mixed_heads, out_weight32, precision=HIGHEST))
        normed2 = low(norm_apply(hidden, ffn_gain32))
        gate_value = low_back(jnp.dot(normed2, gate32, precision=HIGHEST))
        up_value = low_back(jnp.dot(normed2, up32, precision=HIGHEST))
        activation = low(jax.nn.silu(gate_value) * up_value)
        return hidden + jnp.dot(activation, down32, precision=HIGHEST)
    floats = (inputs, q_weight, q_bias, kv_weight, kv_bias, out_weight, attn_gain, ffn_gain, gate_weight, up_weight, down_weight)
    floats = tuple((item.astype(jnp.float32) for item in floats))
    output, backward = jax.vjp(layer, *floats)
    grads = backward(out_grad.astype(jnp.float32))
    return (output, grads[0], grads[1], grads[2], grads[3], grads[4], grads[5], grads[6], grads[7], grads[8], grads[9], grads[10])
```

```python
import functools

import jax
import jax.numpy as jnp
from jax import lax
from jax.experimental import pallas as pl
from jax.experimental.pallas import tpu as pltpu
from jax.sharding import PartitionSpec as P

HEADS = 16
KV = 2
HD = 128
BLK = 512
GROUP = HEADS // KV
TILE = 512
BATCH = 8

EPSILON = 1e-06
ROPE_BASE = 1000000.0
NEGATIVE = -1e30
SCALE = HD**-0.5
LOG2E = 1.4426950408889634

F32 = jnp.float32
BF16 = jnp.bfloat16

RELATIVE = (0, 2, 4, 6, 1, 3, 5, 7)
SLOTS = ((0, 1, 2, 3), (1, 0, 2, 3), (2, 3, 1, 0), (3, 2, 1, 0))


def contract(left_side, right_side, left_dim, right_dim):
    return lax.dot_general(
        left_side,
        right_side,
        (((left_dim,), (right_dim,)), ((), ())),
        preferred_element_type=F32,
    )


class SeqAxis:
    def __init__(self):
        self.size = lax.axis_size("seq")
        self.me = lax.axis_index("seq")
        self.fast = self.size == 8

    def owner(self, position):
        return self.me ^ RELATIVE[position] if self.fast else position

    def swap(self, value, bit):
        return lax.ppermute(value, "seq", [(i, i ^ bit) for i in range(self.size)])

    def gather(self, value):
        if not self.fast:
            whole = lax.all_gather(value, "seq", axis=0, tiled=False)
            return [whole[i] for i in range(self.size)]
        half = value.shape[0] // 2
        along_x = self.swap(value, 2)
        along_y = self.swap(value, 4)
        corner = jnp.concatenate(
            [self.swap(along_y[:half], 2), self.swap(along_x[half:], 4)], axis=0
        )
        chip = [value, along_x, along_y, corner]
        return chip + [self.swap(item, 1) for item in chip]

    def reduce(self, even, odd, axis):
        if not self.fast:
            whole = jnp.concatenate([even, odd], axis=axis).astype(BF16)
            return lax.psum_scatter(whole, "seq", scatter_dimension=axis, tiled=True).astype(F32)
        width = even.shape[axis] // 4
        chip = (even + self.swap(odd.astype(BF16), 1).astype(F32)).astype(BF16)
        here, to_x, to_y, corner = (
            lax.slice_in_dim(chip, i * width, (i + 1) * width, axis=axis) for i in range(4)
        )
        half = corner.shape[0] // 2
        for_y = self.swap(corner[:half], 2)
        for_x = self.swap(corner[half:], 4)
        to_x = jnp.concatenate([to_x[:half], to_x[half:] + for_x], axis=0)
        to_y = jnp.concatenate([to_y[:half] + for_y, to_y[half:]], axis=0)
        return here.astype(F32) + self.swap(to_x, 2).astype(F32) + self.swap(to_y, 4).astype(F32)


class HeadAxis:
    def __init__(self):
        self.size = lax.axis_size("head")
        self.me = lax.axis_index("head")
        self.fast = self.size == 4
        self.inner = (self.me == 1) | (self.me == 2)

    def owners(self):
        if self.fast:
            return jnp.array(SLOTS, jnp.int32)[self.me]
        return jnp.arange(self.size, dtype=jnp.int32)

    def send(self, value, pairs):
        return lax.ppermute(value, "head", pairs)

    def gather(self, value):
        if not self.fast:
            whole = lax.all_gather(value, "head", axis=0, tiled=False)
            return [whole[i] for i in range(self.size)]
        pair = [(0, 1), (1, 0), (2, 3), (3, 2)]
        middle = [(1, 2), (2, 1)]
        outward = [(1, 0), (2, 3)]
        slot1 = self.send(value, pair)
        near = self.send(value, middle)
        far = self.send(slot1, middle)
        slot2 = jnp.where(self.inner, near, self.send(near, outward))
        slot3 = jnp.where(self.inner, far, self.send(far, outward))
        return [value, slot1, slot2, slot3]

    def reduce(self, pieces):
        if not self.fast:
            whole = jnp.stack(pieces).astype(BF16)
            return lax.psum_scatter(whole, "head", scatter_dimension=0, tiled=False).astype(F32)
        pair = [(0, 1), (1, 0), (2, 3), (3, 2)]
        middle = [(1, 2), (2, 1)]
        inward = [(0, 1), (3, 2)]
        own, slot1, slot2, slot3 = pieces
        far = slot3 + self.send(slot3.astype(BF16), inward)
        near = slot2 + self.send(slot2.astype(BF16), inward)
        next_door = slot1 + self.send(far.astype(BF16), middle)
        return (
            own.astype(F32)
            + self.send(next_door.astype(BF16), pair).astype(F32)
            + self.send(near.astype(BF16), middle).astype(F32)
        )


def place(pieces, owners, axis):
    width = pieces[0].shape[axis]
    shape = list(pieces[0].shape)
    shape[axis] = width * len(pieces)
    whole = jnp.zeros(shape, pieces[0].dtype)
    for slot, item in enumerate(pieces):
        whole = lax.dynamic_update_slice_in_dim(whole, item, owners[slot] * width, axis)
    return whole


def take(whole, owners, axis):
    count = owners.shape[0]
    width = whole.shape[axis] // count
    return [
        lax.dynamic_slice_in_dim(whole, owners[slot] * width, width, axis) for slot in range(count)
    ]


def vmem():
    return pl.BlockSpec(memory_space=pltpu.VMEM)


def smem():
    return pl.BlockSpec(memory_space=pltpu.SMEM)


def shuffle_kernel(order_ref, in_ref, out_ref):
    out_ref[...] = in_ref[...]


def shuffle(values, order):
    count = order.shape[0]
    rows, width = values.shape[0], values.shape[1] // count
    return pl.pallas_call(
        shuffle_kernel,
        out_shape=jax.ShapeDtypeStruct(values.shape, values.dtype),
        grid_spec=pltpu.PrefetchScalarGridSpec(
            num_scalar_prefetch=1,
            grid=(count,),
            in_specs=[pl.BlockSpec((rows, width), lambda i, order_ref: (0, order_ref[i]))],
            out_specs=pl.BlockSpec((rows, width), lambda i, order_ref: (0, i)),
        ),
        cost_estimate=pl.CostEstimate(flops=0, transcendentals=0, bytes_accessed=2 * values.nbytes if hasattr(values, "nbytes") else 0),
        name="shuffle",
    )(order, values)


def turn(values, cosine, sine):
    return values * cosine + pltpu.roll(values, HD // 2, 1) * sine


def allowed_bias(tile, stream, first, shape):
    key = tile * TILE + lax.broadcasted_iota(jnp.int32, shape, 0)
    return jnp.where((key >= first) & (key <= stream), 0.0, NEGATIVE)


def forward_kernel(
    offset_ref, bound_ref, raw_ref, cos_ref, sin_ref, stream_ref, first_ref, kv_ref,
    query_ref, mixed_ref, lse_ref,
    top_ref, total_ref, sum_ref, bias_ref, turned_ref,
):
    rows = raw_ref.shape[0]
    cosine, sine = cos_ref[...], sin_ref[...]
    for h in range(HEADS):
        query_ref[h] = turn(raw_ref[:, h * HD : (h + 1) * HD], cosine, sine).astype(BF16)
    top_ref[...] = jnp.full(top_ref.shape, NEGATIVE, F32)
    total_ref[...] = jnp.zeros(total_ref.shape, F32)
    sum_ref[...] = jnp.zeros(sum_ref.shape, F32)

    def visit(tile, carry):
        start = pl.multiple_of(offset_ref[tile], TILE)
        bias_ref[...] = allowed_bias(tile, stream_ref[...], first_ref[...], bias_ref.shape)
        for g in range(KV):
            turned_ref[g] = kv_ref[pl.ds(start, TILE), (KV + g) * HD : (KV + g + 1) * HD].T
        for g in range(KV):
            keys = kv_ref[pl.ds(start, TILE), g * HD : (g + 1) * HD]

            def some(i, carry):
                heads = [g * GROUP + i * BATCH + b for b in range(BATCH)]
                old = [top_ref[h] for h in heads]
                total = [total_ref[h] for h in heads]
                summed = [sum_ref[h] for h in heads]
                scores = [contract(keys, query_ref[h], 1, 1) for h in heads]
                bias = bias_ref[...]
                turned = turned_ref[g]
                new, fresh, fades = [], [], []
                for b in range(BATCH):
                    score = scores[b] * (SCALE * LOG2E) + bias
                    peak = jnp.maximum(old[b], jnp.max(score, axis=0, keepdims=True))
                    weights = jnp.exp2(score - peak)
                    fade = jnp.exp2(old[b] - peak)
                    new.append(peak)
                    fades.append(fade)
                    total[b] = total[b] * fade + jnp.sum(weights, axis=0, keepdims=True)
                    fresh.append(contract(turned, weights.astype(BF16), 1, 0))
                for b, h in enumerate(heads):
                    top_ref[h] = new[b]
                    total_ref[h] = total[b]
                    sum_ref[h] = summed[b] * fades[b] + fresh[b]
                return carry

            lax.fori_loop(0, GROUP // BATCH, some, 0)
        return carry

    lax.fori_loop(bound_ref[0], bound_ref[1] + 1, visit, 0)
    for h in range(HEADS):
        lse_ref[h] = top_ref[h] + jnp.log2(total_ref[h])
        mixed_ref[:, h * HD : (h + 1) * HD] = (sum_ref[h] / total_ref[h]).T.astype(BF16)


def attention_forward(offsets, bounds, query_raw, cosine, sine, stream, first, kv_all):
    rows = query_raw.shape[0]
    return pl.pallas_call(
        forward_kernel,
        out_shape=(
            jax.ShapeDtypeStruct((HEADS, rows, HD), BF16),
            jax.ShapeDtypeStruct((rows, HEADS * HD), BF16),
            jax.ShapeDtypeStruct((HEADS, 1, rows), F32),
        ),
        in_specs=[smem(), smem()] + [vmem()] * 6,
        out_specs=[vmem()] * 3,
        scratch_shapes=[
            pltpu.VMEM((HEADS, 1, rows), F32),
            pltpu.VMEM((HEADS, 1, rows), F32),
            pltpu.VMEM((HEADS, HD, rows), F32),
            pltpu.VMEM((TILE, rows), F32),
            pltpu.VMEM((KV, HD, TILE), BF16),
        ],
        compiler_params=pltpu.CompilerParams(vmem_limit_bytes=48 << 20),
        cost_estimate=pl.CostEstimate(
            flops=4 * HEADS * rows * HD * 2048,
            transcendentals=HEADS * rows * 2048,
            bytes_accessed=kv_all.size * 2 + query_raw.size * 8,
        ),
        name="attention_forward",
    )(offsets, bounds, query_raw, cosine, sine, stream, first, kv_all)


def backward_kernel(
    offset_ref, bound_ref, query_ref, cos_ref, sin_ref, stream_ref, first_ref, kv_ref,
    mixed_ref, grad_ref, lse_ref,
    d_query_ref, d_kv_ref,
    delta_ref, head_grad_ref, sum_ref, bias_ref, turned_ref, d_tile_ref,
):
    rows = mixed_ref.shape[0]
    for h in range(HEADS):
        part = grad_ref[:, h * HD : (h + 1) * HD]
        head_grad_ref[h] = part
        product = part.astype(F32) * mixed_ref[:, h * HD : (h + 1) * HD].astype(F32)
        delta_ref[h] = lax.dot_general(
            jnp.ones((8, HD), F32),
            product,
            (((1,), (1,)), ((), ())),
            precision=lax.Precision.HIGHEST,
            preferred_element_type=F32,
        )[:1]
    sum_ref[...] = jnp.zeros(sum_ref.shape, F32)
    d_kv_ref[...] = jnp.zeros(d_kv_ref.shape, BF16)

    def visit(tile, carry):
        start = pl.multiple_of(offset_ref[tile], TILE)
        bias_ref[...] = allowed_bias(tile, stream_ref[...], first_ref[...], bias_ref.shape)
        d_tile_ref[...] = jnp.zeros(d_tile_ref.shape, F32)
        for g in range(KV):
            turned_ref[g] = kv_ref[pl.ds(start, TILE), g * HD : (g + 1) * HD].T
        for g in range(KV):
            keys = kv_ref[pl.ds(start, TILE), g * HD : (g + 1) * HD]
            values = kv_ref[pl.ds(start, TILE), (KV + g) * HD : (KV + g + 1) * HD]

            def some(i, carry):
                heads = [g * GROUP + i * BATCH + b for b in range(BATCH)]
                query = [query_ref[h] for h in heads]
                head_grad = [head_grad_ref[h] for h in heads]
                summed = [sum_ref[h] for h in heads]
                bias = bias_ref[...]
                turned = turned_ref[g]
                d_keys, d_values = d_tile_ref[g], d_tile_ref[KV + g]
                for b, h in enumerate(heads):
                    scores = contract(keys, query[b], 1, 1) * (SCALE * LOG2E) + bias
                    weights = jnp.exp2(scores - lse_ref[h])
                    d_weights = contract(values, head_grad[b], 1, 1)
                    d_scores = (weights * (d_weights - delta_ref[h])).astype(BF16)
                    d_keys += contract(d_scores, query[b], 1, 0)
                    d_values += contract(weights.astype(BF16), head_grad[b], 1, 0)
                    summed[b] += contract(turned, d_scores, 1, 0)
                for b, h in enumerate(heads):
                    sum_ref[h] = summed[b]
                d_tile_ref[g] = d_keys
                d_tile_ref[KV + g] = d_values
                return carry

            lax.fori_loop(0, GROUP // BATCH, some, 0)
        for g in range(KV):
            d_kv_ref[pl.ds(start, TILE), g * HD : (g + 1) * HD] = (
                d_tile_ref[g] * SCALE
            ).astype(BF16)
            d_kv_ref[pl.ds(start, TILE), (KV + g) * HD : (KV + g + 1) * HD] = d_tile_ref[
                KV + g
            ].astype(BF16)
        return carry

    lax.fori_loop(bound_ref[0], bound_ref[1] + 1, visit, 0)
    cosine, sine = cos_ref[...], -sin_ref[...]
    for h in range(HEADS):
        d_query_ref[:, h * HD : (h + 1) * HD] = turn(
            sum_ref[h].T * SCALE, cosine, sine
        ).astype(BF16)


def attention_backward(
    offsets, bounds, queries, cosine, sine, stream, first, kv_all, mixed, d_mixed, lse
):
    rows = mixed.shape[0]
    return pl.pallas_call(
        backward_kernel,
        out_shape=(
            jax.ShapeDtypeStruct((rows, HEADS * HD), BF16),
            jax.ShapeDtypeStruct(kv_all.shape, BF16),
        ),
        in_specs=[smem(), smem()] + [vmem()] * 9,
        out_specs=[vmem()] * 2,
        scratch_shapes=[
            pltpu.VMEM((HEADS, 1, rows), F32),
            pltpu.VMEM((HEADS, rows, HD), BF16),
            pltpu.VMEM((HEADS, HD, rows), F32),
            pltpu.VMEM((TILE, rows), F32),
            pltpu.VMEM((KV, HD, TILE), BF16),
            pltpu.VMEM((2 * KV, TILE, HD), F32),
        ],
        compiler_params=pltpu.CompilerParams(vmem_limit_bytes=56 << 20),
        cost_estimate=pl.CostEstimate(
            flops=10 * HEADS * rows * HD * 2048,
            transcendentals=HEADS * rows * 2048,
            bytes_accessed=kv_all.size * 4 + mixed.size * 8,
        ),
        name="attention_backward",
    )(offsets, bounds, queries, cosine, sine, stream, first, kv_all, mixed, d_mixed, lse)


def ffn_kernel(normed_ref, grad_ref, gate_ref, up_ref, down_ref, act_ref, d_gate_ref, d_up_ref):
    step = 256

    def chunk(i, carry):
        at = pl.ds(pl.multiple_of(i * step, step), step)
        normed = normed_ref[at, :]
        gate = contract(normed, gate_ref[...], 1, 0)
        up = contract(normed, up_ref[...], 1, 0)
        d_act = contract(grad_ref[at, :], down_ref[...], 1, 1)
        sigmoid = jax.nn.sigmoid(gate)
        silu = gate * sigmoid
        act_ref[at, :] = (silu * up).astype(BF16)
        d_up_ref[at, :] = (d_act * silu).astype(BF16)
        d_gate_ref[at, :] = (d_act * up * (sigmoid + silu * (1.0 - sigmoid))).astype(BF16)
        return carry

    lax.fori_loop(0, normed_ref.shape[0] // step, chunk, 0)


def ffn_middle(normed, grad, gate, up, down):
    rows, depth = normed.shape
    units = gate.shape[1]
    width = 256
    whole = pl.BlockSpec((rows, depth), lambda i: (0, 0), pipeline_mode=pl.Buffered(1))
    columns = pl.BlockSpec((depth, width), lambda i: (0, i))
    out = pl.BlockSpec((rows, width), lambda i: (0, i))
    return pl.pallas_call(
        ffn_kernel,
        out_shape=(jax.ShapeDtypeStruct((rows, units), BF16),) * 3,
        grid=(pl.cdiv(units, width),),
        in_specs=[whole, whole, columns, columns, pl.BlockSpec((width, depth), lambda i: (i, 0))],
        out_specs=[out] * 3,
        compiler_params=pltpu.CompilerParams(vmem_limit_bytes=48 << 20),
        cost_estimate=pl.CostEstimate(
            flops=6 * rows * depth * units,
            transcendentals=rows * units,
            bytes_accessed=2 * (3 * depth * units + 3 * rows * units + 2 * rows * depth),
        ),
        name="ffn_middle",
    )(normed, grad, gate, up, down)


def back_kernel(d_gate_ref, d_up_ref, gate_ref, up_ref, out_ref):
    out_ref[...] = (
        contract(d_gate_ref[...], gate_ref[...], 1, 1) + contract(d_up_ref[...], up_ref[...], 1, 1)
    ).astype(BF16)


def ffn_back(d_gate, d_up, gate, up):
    rows, units = d_gate.shape
    depth = gate.shape[0]
    width = 256
    whole = pl.BlockSpec((rows, units), lambda i: (0, 0), pipeline_mode=pl.Buffered(1))
    part = pl.BlockSpec((width, units), lambda i: (i, 0))
    return pl.pallas_call(
        back_kernel,
        out_shape=jax.ShapeDtypeStruct((rows, depth), BF16),
        grid=(depth // width,),
        in_specs=[whole, whole, part, part],
        out_specs=pl.BlockSpec((rows, width), lambda i: (0, i)),
        compiler_params=pltpu.CompilerParams(vmem_limit_bytes=48 << 20),
        cost_estimate=pl.CostEstimate(
            flops=4 * rows * depth * units,
            transcendentals=0,
            bytes_accessed=2 * (2 * depth * units + 2 * rows * units + rows * depth),
        ),
        name="ffn_back",
    )(d_gate, d_up, gate, up)


def rope_tables(position):
    half_width = HD // 2
    inverse = ROPE_BASE ** (-(jnp.arange(half_width, dtype=F32) * 2.0 / HD))
    angles = position.astype(F32)[:, None] * inverse[None, :]
    cosine, sine = jnp.cos(angles), jnp.sin(angles)
    return (
        jnp.concatenate([cosine, cosine], axis=1),
        jnp.concatenate([-sine, sine], axis=1),
    )


def rotate(values, cosine, sine):
    half_width = values.shape[-1] // 2
    swapped = jnp.concatenate([values[..., half_width:], values[..., :half_width]], axis=-1)
    return values * cosine + swapped * sine


def norm_forward(values, gain_vector):
    rms_scale = lax.rsqrt(jnp.mean(values * values, axis=1, keepdims=True) + EPSILON)
    return (values * rms_scale * gain_vector, rms_scale)


def norm_backward(values, rms_scale, gain_vector, gradient):
    weighted = gradient * gain_vector
    gain_grad = jnp.sum(gradient * values * rms_scale, axis=0)
    inner_mean = jnp.mean(weighted * values, axis=1, keepdims=True)
    return (rms_scale * weighted - values * rms_scale**3 * inner_mean, gain_grad)


def local(
    inputs,
    out_grad,
    q_weight,
    q_bias,
    kv_weight,
    kv_bias,
    out_weight,
    attn_gain,
    ffn_gain,
    gate_weight,
    up_weight,
    down_weight,
    block_order,
    long_docs,
    short_docs,
):
    seq, head = SeqAxis(), HeadAxis()
    owners = head.owners()
    local_rows, depth = inputs.shape
    span_rows = local_rows * head.size
    block_count = block_order.shape[0]
    wide = KV * HD * 2
    seq_order = jnp.stack([jnp.asarray(seq.owner(p), jnp.int32) for p in range(seq.size)])
    seq_place = jnp.argsort(seq_order).astype(jnp.int32)

    kv_rows_each = kv_weight.shape[0]
    sizes = [q_bias.shape[0], kv_bias.shape[0], attn_gain.shape[0], ffn_gain.shape[0]]
    padded = -(-(kv_rows_each + 1) // 16) * 16
    strip = jnp.concatenate([q_bias, kv_bias, attn_gain, ffn_gain])
    strip = jnp.pad(strip, (0, wide - strip.shape[0]))[None, :]
    pack = jnp.concatenate(
        [kv_weight, strip, jnp.zeros((padded - kv_rows_each - 1, wide), BF16)], axis=0
    )
    pack_span = place(head.gather(pack), owners, 0)
    pack_all = jnp.stack(seq.gather(pack_span)).reshape(seq.size, head.size, padded, wide)
    kv_full = pack_all[:, :, :kv_rows_each].reshape(depth, wide)
    strips = pack_all[:, :, kv_rows_each].astype(F32)

    def part_of(i):
        start = sum(sizes[:i])
        return strips[:, :, start : start + sizes[i]].reshape(seq.size, -1)

    q_bias_full = part_of(0)[seq_place].reshape(1, -1)
    kv_bias_full = part_of(1)[seq_place].reshape(1, -1)
    attn_gain32 = part_of(2).reshape(1, -1)
    ffn_gain32 = part_of(3).reshape(1, -1)

    q_full = jnp.concatenate(seq.gather(place(head.gather(q_weight), owners, 1)), axis=0)

    starts = jnp.concatenate(
        [
            jnp.cumsum(long_docs) - long_docs,
            jnp.sum(long_docs) + jnp.cumsum(short_docs) - short_docs,
        ]
    )
    row_start = (seq.me * head.size + head.me) * local_rows
    stream = (
        block_order[row_start // BLK] * BLK
        + row_start % BLK
        + jnp.arange(local_rows, dtype=jnp.int32)
    )
    long_total = jnp.sum(long_docs)
    position = jnp.where(stream >= long_total, stream - long_total, stream)
    first = jnp.max(jnp.where(starts[None, :] <= stream[:, None], starts[None, :], 0), axis=1)
    cosine, sine = rope_tables(position)
    storage = jnp.argsort(block_order).astype(jnp.int32)
    span_blocks = span_rows // BLK
    base = seq_place[storage // span_blocks] * span_rows + storage % span_blocks * BLK
    per_block = BLK // TILE
    offsets = (base[:, None] + jnp.arange(per_block, dtype=jnp.int32)[None, :] * TILE).reshape(-1)
    bounds = jnp.stack([first[0] // TILE, stream[-1] // TILE]).astype(jnp.int32)
    stream_row, first_row = stream[None, :], first[None, :]

    residual = shuffle(inputs, seq_order).astype(F32)
    cotangent16 = shuffle(out_grad, seq_order)
    normed32, attn_scale = norm_forward(residual, attn_gain32)
    normed = normed32.astype(BF16)
    kv_raw = jnp.dot(normed, kv_full, preferred_element_type=F32) + kv_bias_full
    key_part = rotate(
        kv_raw[:, : KV * HD].reshape(local_rows, KV, HD), cosine[:, None, :], sine[:, None, :]
    )
    kv_rows = jnp.concatenate(
        [key_part.reshape(local_rows, KV * HD), kv_raw[:, KV * HD :]], axis=1
    ).astype(BF16)
    kv_all = jnp.concatenate(seq.gather(place(head.gather(kv_rows), owners, 0)), axis=0)
    query_raw = jnp.dot(normed, q_full, preferred_element_type=F32) + q_bias_full
    queries, mixed, lse = attention_forward(
        offsets, bounds, query_raw, cosine, sine, stream_row, first_row, kv_all
    )
    out_full = jnp.concatenate(seq.gather(place(head.gather(out_weight), owners, 0)), axis=1)
    hidden = residual + jnp.dot(mixed, out_full, preferred_element_type=F32)
    normed2_32, ffn_scale = norm_forward(hidden, ffn_gain32)
    normed2 = normed2_32.astype(BF16)

    gate_full = jnp.concatenate(seq.gather(gate_weight), axis=0)
    up_full = jnp.concatenate(seq.gather(up_weight), axis=0)
    down_full = jnp.concatenate(seq.gather(down_weight), axis=1)
    grad_all = jnp.concatenate(head.gather(cotangent16), axis=0)
    normed2_all = jnp.concatenate(head.gather(normed2), axis=0)
    act, d_gate, d_up = ffn_middle(normed2_all, grad_all, gate_full, up_full, down_full)

    def slots(whole):
        return [whole[i * local_rows : (i + 1) * local_rows] for i in range(head.size)]

    d_normed2 = head.reduce(slots(ffn_back(d_gate, d_up, gate_full, up_full)))
    ffn_terms = jnp.dot(act, down_full, preferred_element_type=F32).astype(BF16)
    output = hidden + head.reduce(slots(ffn_terms))
    output = shuffle(output, seq_place)
    half = depth // 2
    gate_grad = seq.reduce(
        contract(normed2_all[:, :half], d_gate, 0, 0),
        contract(normed2_all[:, half:], d_gate, 0, 0),
        0,
    )
    up_grad = seq.reduce(
        contract(normed2_all[:, :half], d_up, 0, 0),
        contract(normed2_all[:, half:], d_up, 0, 0),
        0,
    )
    down_grad = seq.reduce(
        contract(act, grad_all[:, :half], 0, 0), contract(act, grad_all[:, half:], 0, 0), 1
    )

    cotangent = cotangent16.astype(F32)
    d_hidden_norm, ffn_gain_grad = norm_backward(hidden, ffn_scale, ffn_gain32, d_normed2)
    d_hidden = cotangent + d_hidden_norm
    d_attn = d_hidden.astype(BF16)
    d_mixed = contract(d_attn, out_full, 1, 1).astype(BF16)
    d_queries, d_kv_all = attention_backward(
        offsets, bounds, queries, cosine, sine, stream_row, first_row, kv_all, mixed, d_mixed, lse
    )
    middle = d_kv_all.shape[0] // 2
    d_kv_span = seq.reduce(d_kv_all[:middle].astype(F32), d_kv_all[middle:], 0).astype(BF16)
    d_kv_own = head.reduce(take(d_kv_span, owners, 0))
    key_back = rotate(
        d_kv_own[:, : KV * HD].reshape(local_rows, KV, HD), cosine[:, None, :], -sine[:, None, :]
    )
    d_kv = jnp.concatenate(
        [key_back.reshape(local_rows, KV * HD), d_kv_own[:, KV * HD :]], axis=1
    ).astype(BF16)
    d_normed = contract(d_queries, q_full, 1, 1) + contract(d_kv, kv_full, 1, 1)
    d_input_norm, attn_gain_grad = norm_backward(residual, attn_scale, attn_gain32, d_normed)
    input_grad = shuffle(d_hidden + d_input_norm, seq_place)

    def head_sum(value, axis):
        return head.reduce(take(value.astype(BF16), owners, axis))

    out_weight_grad = head_sum(
        seq.reduce(
            contract(mixed, d_attn[:, :half], 0, 0), contract(mixed, d_attn[:, half:], 0, 0), 1
        ),
        0,
    )
    q_weight_grad = head_sum(
        seq.reduce(
            contract(normed[:, :half], d_queries, 0, 0),
            contract(normed[:, half:], d_queries, 0, 0),
            0,
        ),
        1,
    )
    kv_part = contract(normed, d_kv, 0, 0).reshape(seq.size, head.size, kv_rows_each, wide)
    q_bias_part = jnp.sum(d_queries.astype(F32), axis=0).reshape(seq.size, -1)[seq_order]
    kv_bias_part = jnp.sum(d_kv.astype(F32), axis=0).reshape(seq.size, -1)[seq_order]
    strips = jnp.concatenate(
        [
            item.reshape(seq.size, head.size, 1, -1)
            for item in (q_bias_part, kv_bias_part, attn_gain_grad, ffn_gain_grad)
        ],
        axis=3,
    )
    strips = jnp.pad(
        strips,
        ((0, 0), (0, 0), (0, padded - kv_rows_each - 1), (0, wide - strips.shape[3])),
    )
    small = jnp.concatenate([kv_part, strips], axis=2).reshape(-1, wide)
    middle = small.shape[0] // 2
    small = head_sum(seq.reduce(small[:middle], small[middle:], 0), 0)
    kv_weight_grad = small[:kv_rows_each]
    tail = small[kv_rows_each]
    cuts = [sum(sizes[:i]) for i in range(5)]
    q_bias_grad, kv_bias_grad, attn_grad, ffn_grad = (
        tail[cuts[i] : cuts[i + 1]] for i in range(4)
    )
    return (
        output,
        input_grad,
        q_weight_grad,
        q_bias_grad,
        kv_weight_grad,
        kv_bias_grad,
        out_weight_grad,
        attn_grad,
        ffn_grad,
        gate_grad,
        up_grad,
        down_grad,
    )


def solution(mesh):
    in_specs = (
        P(("seq", "head"), None),
        P(("seq", "head"), None),
        P("seq", "head"),
        P(("seq", "head")),
        P(("seq", "head"), None),
        P(("seq", "head")),
        P("head", "seq"),
        P(("seq", "head")),
        P(("seq", "head")),
        P("seq", "head"),
        P("seq", "head"),
        P("head", "seq"),
        P(),
        P(),
        P(),
    )
    out_specs = (
        P(("seq", "head"), None),
        P(("seq", "head"), None),
        P("seq", "head"),
        P(("seq", "head")),
        P(("seq", "head"), None),
        P(("seq", "head")),
        P("head", "seq"),
        P(("seq", "head")),
        P(("seq", "head")),
        P("seq", "head"),
        P("seq", "head"),
        P("head", "seq"),
    )
    return jax.shard_map(local, mesh=mesh, in_specs=in_specs, out_specs=out_specs, check_vma=False)
```

```python
import functools

import jax
import jax.numpy as jnp
from jax import lax
from jax.experimental import pallas as pl
from jax.experimental.pallas import tpu as pltpu
from jax.sharding import PartitionSpec as P

HEADS = 16
KV = 2
HD = 128
BLK = 512
GROUP = HEADS // KV
TILE = 512
BATCH = 8
ROWS = 1024
UNITS = 256
GRAD_UNITS = 512

EPSILON = 1e-06
ROPE_BASE = 1000000.0
NEGATIVE = -1e30
SCALE = HD**-0.5
LOG2E = 1.4426950408889634

F32 = jnp.float32
BF16 = jnp.bfloat16

ORDER = ((0, 2, 4, 6, 1, 5, 3, 7), (0, 4, 2, 6, 1, 3, 5, 7))
RELAY = ((0, 1, 2, 3), (1, 0, 2, 3), (2, 3, 1, 0), (3, 2, 1, 0))


def contract(left_side, right_side, left_dim, right_dim):
    return lax.dot_general(
        left_side,
        right_side,
        (((left_dim,), (right_dim,)), ((), ())),
        preferred_element_type=F32,
    )


def after(value, *others):
    return lax.optimization_barrier((value, *others))[0]


class Lane:
    def __init__(self, depth):
        self.depth = depth
        self.done = []

    def __call__(self, send, value):
        if len(self.done) >= self.depth:
            value = after(value, self.done[-self.depth])
        self.done.append(send(value))
        return self.done[-1]


class SeqAxis:
    def __init__(self):
        self.size = lax.axis_size("seq")
        self.me = lax.axis_index("seq")
        self.fast = self.size == 8
        self.lane = Lane(2)
        places = jnp.arange(self.size, dtype=jnp.int32)
        if self.fast:
            odd = self.me % 2 == 1
            self.order = self.me ^ jnp.where(odd, jnp.array(ORDER[1]), jnp.array(ORDER[0]))
        else:
            self.order = places
        self.place = jnp.sum(
            jnp.where(self.order[:, None] == places[None, :], places[:, None], 0), axis=0
        )

    def swap(self, value, even, odd, ordered=True):
        pairs = [(i, i ^ (odd if i % 2 else even)) for i in range(self.size)]

        def send(item):
            return lax.ppermute(item, "seq", pairs)

        return self.lane(send, value) if ordered else send(value)

    def begin(self, value, ordered=True):
        if not self.fast:
            return [value]
        return [value, self.swap(value, 2, 4, ordered), self.swap(value, 4, 2, ordered)]

    def finish(self, begun, axis=0, ordered=True):
        if not self.fast:
            whole = lax.all_gather(begun[0], "seq", axis=axis, tiled=True)
            half = whole.shape[axis] // 2
            return [
                lax.slice_in_dim(whole, i * half, (i + 1) * half, axis=axis) for i in range(2)
            ]
        value, one, two = begun
        mine = jnp.concatenate([value, one, two, self.swap(one, 4, 2, ordered)], axis=axis)
        return [mine, self.swap(mine, 1, 1, False)]

    def gather(self, value, axis=0, ordered=True):
        return self.finish(self.begin(value, ordered), axis, ordered)

    def reduce(self, mine, other):
        if not self.fast:
            whole = jnp.concatenate([jnp.stack(mine(None)), other], axis=0)
            return lax.psum_scatter(whole, "seq", scatter_dimension=0, tiled=False).astype(F32)
        here, one, two, corner = mine(self.swap(other, 1, 1, False))
        corner = self.swap(corner, 4, 2)
        two = self.swap(two, 4, 2)
        one = self.swap(one + corner, 2, 4)
        return here.astype(F32) + two.astype(F32) + one.astype(F32)


class HeadAxis:
    def __init__(self):
        self.size = lax.axis_size("head")
        self.me = lax.axis_index("head")
        self.fast = self.size == 4
        self.inner = (self.me == 1) | (self.me == 2)
        self.relay = jnp.array(RELAY, jnp.int32)[self.me] if self.fast else None
        self.direct = self.me ^ jnp.arange(self.size, dtype=jnp.int32)

    def send(self, value, pairs):
        return lax.ppermute(value, "head", pairs)

    def gather(self, value):
        if not self.fast:
            return lax.all_gather(value, "head", axis=0, tiled=True)
        pair = [(0, 1), (1, 0), (2, 3), (3, 2)]
        middle = [(1, 2), (2, 1)]
        outward = [(1, 0), (2, 3)]
        slot1 = self.send(value, pair)
        near = self.send(value, middle)
        far = self.send(slot1, middle)
        slot2 = jnp.where(self.inner, near, self.send(near, outward))
        slot3 = jnp.where(self.inner, far, self.send(far, outward))
        return place([value, slot1, slot2, slot3], self.relay, 0)

    def reduce(self, whole, beside):
        if not self.fast:
            return [lax.psum_scatter(whole, "head", scatter_dimension=0, tiled=True)]
        pair = [(0, 1), (1, 0), (2, 3), (3, 2)]
        middle = [(1, 2), (2, 1)]
        inward = [(0, 1), (3, 2)]
        rows = whole.shape[0] // self.size
        own, slot1, slot2, slot3 = (
            lax.dynamic_slice_in_dim(whole, self.relay[k] * rows, rows, 0) for k in range(4)
        )
        far = slot3 + after(self.send(slot3, inward), beside[0])
        near = self.send(after(slot2, far), inward)
        next_door = slot1 + after(self.send(far, middle), beside[1])
        near = slot2 + near
        return [own, after(self.send(next_door, pair), beside[2]), self.send(near, middle)]

    def gather_small(self, value, axis):
        if not self.fast:
            return lax.all_gather(value, "head", axis=axis, tiled=True)
        pieces = [value] + [
            self.send(value, [(i, i ^ k) for i in range(self.size)]) for k in range(1, 4)
        ]
        return place(pieces, self.direct, axis)

    def reduce_small(self, value, axis):
        if not self.fast:
            return lax.psum_scatter(value, "head", scatter_dimension=axis, tiled=True).astype(F32)
        width = value.shape[axis] // self.size
        total = None
        for k in range(self.size):
            part = lax.dynamic_slice_in_dim(value, (self.me ^ k) * width, width, axis)
            if k:
                part = self.send(part, [(i, i ^ k) for i in range(self.size)])
            total = part.astype(F32) if total is None else total + part.astype(F32)
        return total


def vmem():
    return pl.BlockSpec(memory_space=pltpu.VMEM)


def anywhere():
    return pl.BlockSpec(memory_space=pl.ANY)


def smem():
    return pl.BlockSpec(memory_space=pltpu.SMEM)


def place_kernel(axis, order_ref, *refs):
    out_ref = refs[-1]
    for k, piece_ref in enumerate(refs[:-1]):
        width = piece_ref.shape[axis]
        at = pl.ds(pl.multiple_of(order_ref[k] * width, width), width)
        if axis:
            out_ref[:, at] = piece_ref[...]
        else:
            out_ref[at, :] = piece_ref[...]


def place(pieces, order, axis):
    shape = list(pieces[0].shape)
    shape[axis] *= len(pieces)
    return pl.pallas_call(
        functools.partial(place_kernel, axis),
        out_shape=jax.ShapeDtypeStruct(shape, pieces[0].dtype),
        in_specs=[smem()] + [vmem()] * len(pieces),
        out_specs=vmem(),
        name="place",
    )(order, *pieces)


def shuffle_kernel(count, order_ref, *refs):
    for i in range(len(refs) // 2):
        in_ref, out_ref = refs[i], refs[len(refs) // 2 + i]
        width = in_ref.shape[1] // count
        for p in range(count):
            at = pl.ds(pl.multiple_of(order_ref[p] * width, width), width)
            out_ref[:, p * width : (p + 1) * width] = in_ref[:, at]


def shuffle(order, *values):
    return pl.pallas_call(
        functools.partial(shuffle_kernel, order.shape[0]),
        out_shape=[jax.ShapeDtypeStruct(v.shape, v.dtype) for v in values],
        in_specs=[smem()] + [vmem()] * len(values),
        out_specs=[vmem()] * len(values),
        name="shuffle",
    )(order, *values)


def turn(values, cosine, sine):
    return values * cosine + pltpu.roll(values, HD // 2, 1) * sine


def allowed_bias(tile, stream, first, shape):
    key = tile * TILE + lax.broadcasted_iota(jnp.int32, shape, 0)
    return jnp.where((key >= first) & (key <= stream), 0.0, NEGATIVE)


def fetch(half_a_ref, half_b_ref, whole_ref, sem_ref):
    half = half_a_ref.shape[0]
    copies = [
        pltpu.make_async_copy(ref, whole_ref.at[pl.ds(i * half, half)], sem_ref.at[i])
        for i, ref in enumerate((half_a_ref, half_b_ref))
    ]
    for copy in copies:
        copy.start()
    return copies


def forward_kernel(
    offset_ref, bound_ref, raw_ref, cos_ref, sin_ref, stream_ref, first_ref, half_a_ref, half_b_ref,
    query_ref, mixed_ref, lse_ref,
    top_ref, total_ref, sum_ref, bias_ref, turned_ref, kv_ref, sem_ref,
):
    copies = fetch(half_a_ref, half_b_ref, kv_ref, sem_ref)
    cosine, sine = cos_ref[...], sin_ref[...]
    for h in range(HEADS):
        query_ref[h] = turn(raw_ref[:, h * HD : (h + 1) * HD], cosine, sine).astype(BF16)
    top_ref[...] = jnp.full(top_ref.shape, NEGATIVE, F32)
    total_ref[...] = jnp.zeros(total_ref.shape, F32)
    sum_ref[...] = jnp.zeros(sum_ref.shape, F32)
    for copy in copies:
        copy.wait()

    def visit(tile, carry):
        start = pl.multiple_of(offset_ref[tile], TILE)
        bias_ref[...] = allowed_bias(tile, stream_ref[...], first_ref[...], bias_ref.shape)
        for g in range(KV):
            turned_ref[g] = kv_ref[pl.ds(start, TILE), (KV + g) * HD : (KV + g + 1) * HD].T
        for g in range(KV):
            keys = kv_ref[pl.ds(start, TILE), g * HD : (g + 1) * HD]

            def some(i, carry):
                heads = [g * GROUP + i * BATCH + b for b in range(BATCH)]
                old = [top_ref[h] for h in heads]
                total = [total_ref[h] for h in heads]
                summed = [sum_ref[h] for h in heads]
                scores = [contract(keys, query_ref[h], 1, 1) for h in heads]
                bias = bias_ref[...]
                turned = turned_ref[g]
                new, fresh, fades = [], [], []
                for b in range(BATCH):
                    score = scores[b] * (SCALE * LOG2E) + bias
                    peak = jnp.maximum(old[b], jnp.max(score, axis=0, keepdims=True))
                    weights = jnp.exp2(score - peak)
                    fade = jnp.exp2(old[b] - peak)
                    new.append(peak)
                    fades.append(fade)
                    total[b] = total[b] * fade + jnp.sum(weights, axis=0, keepdims=True)
                    fresh.append(contract(turned, weights.astype(BF16), 1, 0))
                for b, h in enumerate(heads):
                    top_ref[h] = new[b]
                    total_ref[h] = total[b]
                    sum_ref[h] = summed[b] * fades[b] + fresh[b]
                return carry

            lax.fori_loop(0, GROUP // BATCH, some, 0)
        return carry

    lax.fori_loop(bound_ref[0], bound_ref[1] + 1, visit, 0)
    for h in range(HEADS):
        lse_ref[h] = top_ref[h] + jnp.log2(total_ref[h])
        mixed_ref[:, h * HD : (h + 1) * HD] = (sum_ref[h] / total_ref[h]).T.astype(BF16)


def attention_forward(offsets, bounds, query_raw, cosine, sine, stream, first, kv_a, kv_b):
    rows = query_raw.shape[0]
    kv_shape = (2 * kv_a.shape[0], kv_a.shape[1])
    return pl.pallas_call(
        forward_kernel,
        out_shape=(
            jax.ShapeDtypeStruct((HEADS, rows, HD), BF16),
            jax.ShapeDtypeStruct((rows, HEADS * HD), BF16),
            jax.ShapeDtypeStruct((HEADS, 1, rows), F32),
        ),
        in_specs=[smem(), smem()] + [vmem()] * 5 + [anywhere()] * 2,
        out_specs=[vmem()] * 3,
        scratch_shapes=[
            pltpu.VMEM((HEADS, 1, rows), F32),
            pltpu.VMEM((HEADS, 1, rows), F32),
            pltpu.VMEM((HEADS, HD, rows), F32),
            pltpu.VMEM((TILE, rows), F32),
            pltpu.VMEM((KV, HD, TILE), BF16),
            pltpu.VMEM(kv_shape, BF16),
            pltpu.SemaphoreType.DMA((2,)),
        ],
        compiler_params=pltpu.CompilerParams(vmem_limit_bytes=48 << 20),
        cost_estimate=pl.CostEstimate(
            flops=4 * HEADS * rows * HD * 2048,
            transcendentals=HEADS * rows * 2048,
            bytes_accessed=kv_a.size * 4 + query_raw.size * 8,
        ),
        name="attention_forward",
    )(offsets, bounds, query_raw, cosine, sine, stream, first, kv_a, kv_b)


def backward_kernel(
    offset_ref, bound_ref, query_ref, cos_ref, sin_ref, stream_ref, first_ref,
    mixed_ref, grad_ref, lse_ref, half_a_ref, half_b_ref,
    d_query_ref, d_half_a_ref, d_half_b_ref,
    delta_ref, head_grad_ref, sum_ref, bias_ref, turned_ref, d_tile_ref, kv_ref, sem_ref,
):
    copies = fetch(half_a_ref, half_b_ref, kv_ref, sem_ref)
    half = half_a_ref.shape[0]
    for h in range(HEADS):
        part = grad_ref[:, h * HD : (h + 1) * HD]
        head_grad_ref[h] = part
        product = part.astype(F32) * mixed_ref[:, h * HD : (h + 1) * HD].astype(F32)
        delta_ref[h] = lax.dot_general(
            jnp.ones((8, HD), F32),
            product,
            (((1,), (1,)), ((), ())),
            precision=lax.Precision.HIGHEST,
            preferred_element_type=F32,
        )[:1]
    sum_ref[...] = jnp.zeros(sum_ref.shape, F32)
    d_half_a_ref[...] = jnp.zeros(d_half_a_ref.shape, BF16)
    d_half_b_ref[...] = jnp.zeros(d_half_b_ref.shape, BF16)
    for copy in copies:
        copy.wait()

    def visit(tile, carry):
        start = pl.multiple_of(offset_ref[tile], TILE)
        bias_ref[...] = allowed_bias(tile, stream_ref[...], first_ref[...], bias_ref.shape)
        d_tile_ref[...] = jnp.zeros(d_tile_ref.shape, F32)
        for g in range(KV):
            turned_ref[g] = kv_ref[pl.ds(start, TILE), g * HD : (g + 1) * HD].T
        for g in range(KV):
            keys = kv_ref[pl.ds(start, TILE), g * HD : (g + 1) * HD]
            values = kv_ref[pl.ds(start, TILE), (KV + g) * HD : (KV + g + 1) * HD]

            def some(i, carry):
                heads = [g * GROUP + i * BATCH + b for b in range(BATCH)]
                query = [query_ref[h] for h in heads]
                head_grad = [head_grad_ref[h] for h in heads]
                summed = [sum_ref[h] for h in heads]
                bias = bias_ref[...]
                turned = turned_ref[g]
                d_keys, d_values = d_tile_ref[g], d_tile_ref[KV + g]
                for b, h in enumerate(heads):
                    scores = contract(keys, query[b], 1, 1) * (SCALE * LOG2E) + bias
                    weights = jnp.exp2(scores - lse_ref[h])
                    d_weights = contract(values, head_grad[b], 1, 1)
                    d_scores = (weights * (d_weights - delta_ref[h])).astype(BF16)
                    d_keys += contract(d_scores, query[b], 1, 0)
                    d_values += contract(weights.astype(BF16), head_grad[b], 1, 0)
                    summed[b] += contract(turned, d_scores, 1, 0)
                for b, h in enumerate(heads):
                    sum_ref[h] = summed[b]
                d_tile_ref[g] = d_keys
                d_tile_ref[KV + g] = d_values
                return carry

            lax.fori_loop(0, GROUP // BATCH, some, 0)
        for i, d_ref in enumerate((d_half_a_ref, d_half_b_ref)):

            @pl.when(start // half == i)
            def _():
                at = pl.ds(pl.multiple_of(start - i * half, TILE), TILE)
                for g in range(KV):
                    d_ref[at, g * HD : (g + 1) * HD] = (d_tile_ref[g] * SCALE).astype(BF16)
                    d_ref[at, (KV + g) * HD : (KV + g + 1) * HD] = d_tile_ref[KV + g].astype(BF16)

        return carry

    lax.fori_loop(bound_ref[0], bound_ref[1] + 1, visit, 0)
    cosine, sine = cos_ref[...], -sin_ref[...]
    for h in range(HEADS):
        d_query_ref[:, h * HD : (h + 1) * HD] = turn(
            sum_ref[h].T * SCALE, cosine, sine
        ).astype(BF16)


def attention_backward(
    offsets, bounds, queries, cosine, sine, stream, first, mixed, d_mixed, lse, kv_a, kv_b
):
    rows = mixed.shape[0]
    kv_shape = (2 * kv_a.shape[0], kv_a.shape[1])
    return pl.pallas_call(
        backward_kernel,
        out_shape=(
            jax.ShapeDtypeStruct((rows, HEADS * HD), BF16),
            jax.ShapeDtypeStruct(kv_a.shape, BF16),
            jax.ShapeDtypeStruct(kv_b.shape, BF16),
        ),
        in_specs=[smem(), smem()] + [vmem()] * 8 + [anywhere()] * 2,
        out_specs=[vmem()] * 3,
        scratch_shapes=[
            pltpu.VMEM((HEADS, 1, rows), F32),
            pltpu.VMEM((HEADS, rows, HD), BF16),
            pltpu.VMEM((HEADS, HD, rows), F32),
            pltpu.VMEM((TILE, rows), F32),
            pltpu.VMEM((KV, HD, TILE), BF16),
            pltpu.VMEM((2 * KV, TILE, HD), F32),
            pltpu.VMEM(kv_shape, BF16),
            pltpu.SemaphoreType.DMA((2,)),
        ],
        compiler_params=pltpu.CompilerParams(vmem_limit_bytes=56 << 20),
        cost_estimate=pl.CostEstimate(
            flops=10 * HEADS * rows * HD * 2048,
            transcendentals=HEADS * rows * 2048,
            bytes_accessed=kv_a.size * 8 + mixed.size * 8,
        ),
        name="attention_backward",
    )(offsets, bounds, queries, cosine, sine, stream, first, mixed, d_mixed, lse, kv_a, kv_b)


def side_by_side(order_ref, weight_ref):
    return jnp.concatenate([weight_ref[order_ref[p]] for p in range(weight_ref.shape[0])], axis=1)


def ffn_kernel(
    order_ref, normed_ref, grad_ref, gate_ref, up_ref, down_a_ref, down_b_ref,
    act_ref, d_gate_ref, d_up_ref,
):
    step = ROWS

    def chunk(i, carry):
        at = pl.ds(pl.multiple_of(i * step, step), step)
        normed = normed_ref[at, :]
        gate = contract(normed, side_by_side(order_ref, gate_ref), 1, 1)
        up = contract(normed, side_by_side(order_ref, up_ref), 1, 1)
        down = [ref[p] for ref in (down_a_ref, down_b_ref) for p in range(ref.shape[0])]
        d_act = contract(grad_ref[at, :], jnp.concatenate(down, axis=1), 1, 1)
        sigmoid = jax.nn.sigmoid(gate)
        silu = gate * sigmoid
        act_ref[at, :] = (silu * up).astype(BF16)
        d_up_ref[at, :] = (d_act * silu).astype(BF16)
        d_gate_ref[at, :] = (d_act * up * (sigmoid + silu * (1.0 - sigmoid))).astype(BF16)
        return carry

    lax.fori_loop(0, normed_ref.shape[0] // step, chunk, 0)


def ffn_middle(order, normed, grad, gate, up, down_a, down_b):
    rows, depth = normed.shape
    pieces, units, piece = gate.shape
    width = UNITS
    whole = pl.BlockSpec((rows, depth), lambda i, order_ref: (0, 0), pipeline_mode=pl.Buffered(1))
    weight = pl.BlockSpec((pieces, width, piece), lambda i, order_ref: (0, i, 0))
    half = pl.BlockSpec((pieces // 2, width, piece), lambda i, order_ref: (0, i, 0))
    return pl.pallas_call(
        ffn_kernel,
        out_shape=(jax.ShapeDtypeStruct((rows, units), BF16),) * 3,
        grid_spec=pltpu.PrefetchScalarGridSpec(
            num_scalar_prefetch=1,
            grid=(pl.cdiv(units, width),),
            in_specs=[whole, whole, weight, weight, half, half],
            out_specs=[pl.BlockSpec((rows, width), lambda i, order_ref: (0, i))] * 3,
        ),
        compiler_params=pltpu.CompilerParams(vmem_limit_bytes=48 << 20),
        cost_estimate=pl.CostEstimate(
            flops=6 * rows * depth * units,
            transcendentals=rows * units,
            bytes_accessed=2 * (3 * depth * units + 3 * rows * units + 2 * rows * depth),
        ),
        name="ffn_middle",
    )(order, normed, grad, gate, up, down_a, down_b)


def back_kernel(order_ref, d_gate_ref, d_up_ref, gate_ref, up_ref, out_ref):
    out_ref[...] = (
        contract(d_gate_ref[...], gate_ref[0], 1, 0) + contract(d_up_ref[...], up_ref[0], 1, 0)
    ).astype(BF16)


def ffn_back(order, d_gate, d_up, gate, up):
    rows, units = d_gate.shape
    pieces, _, piece = gate.shape
    whole = pl.BlockSpec((rows, units), lambda i, order_ref: (0, 0), pipeline_mode=pl.Buffered(1))
    part = pl.BlockSpec((1, units, piece), lambda i, order_ref: (order_ref[i], 0, 0))
    return pl.pallas_call(
        back_kernel,
        out_shape=jax.ShapeDtypeStruct((rows, pieces * piece), BF16),
        grid_spec=pltpu.PrefetchScalarGridSpec(
            num_scalar_prefetch=1,
            grid=(pieces,),
            in_specs=[whole, whole, part, part],
            out_specs=pl.BlockSpec((rows, piece), lambda i, order_ref: (0, i)),
        ),
        compiler_params=pltpu.CompilerParams(vmem_limit_bytes=48 << 20),
        cost_estimate=pl.CostEstimate(
            flops=4 * rows * pieces * piece * units,
            transcendentals=0,
            bytes_accessed=2 * (2 * pieces * piece * units + 2 * rows * units),
        ),
        name="ffn_back",
    )(order, d_gate, d_up, gate, up)


def forth_kernel(act_ref, down_a_ref, down_b_ref, out_ref):
    count = pl.num_programs(0) // 2
    for i, down_ref in enumerate((down_a_ref, down_b_ref)):

        @pl.when(pl.program_id(0) // count == i)
        def _():
            out_ref[...] = contract(act_ref[...], down_ref[0], 1, 0).astype(BF16)


def ffn_forth(act, down_a, down_b):
    rows, units = act.shape
    count, _, piece = down_a.shape
    return pl.pallas_call(
        forth_kernel,
        out_shape=jax.ShapeDtypeStruct((rows, 2 * count * piece), BF16),
        grid=(2 * count,),
        in_specs=[
            pl.BlockSpec((rows, units), lambda i: (0, 0), pipeline_mode=pl.Buffered(1)),
            pl.BlockSpec((1, units, piece), lambda i: (jnp.minimum(i, count - 1), 0, 0)),
            pl.BlockSpec((1, units, piece), lambda i: (jnp.maximum(i - count, 0), 0, 0)),
        ],
        out_specs=pl.BlockSpec((rows, piece), lambda i: (0, i)),
        compiler_params=pltpu.CompilerParams(vmem_limit_bytes=48 << 20),
        cost_estimate=pl.CostEstimate(
            flops=4 * rows * count * piece * units,
            transcendentals=0,
            bytes_accessed=2 * (2 * count * piece * units + rows * units),
        ),
        name="ffn_forth",
    )(act, down_a, down_b)


def unit_grad_kernel(count, shift, added, stacked, order_ref, left_ref, right_ref, *refs):
    outs = refs[added:]
    piece = outs[0].shape[-1]
    turned = left_ref[...].T
    for p in range(count):
        at = pl.ds(pl.multiple_of(order_ref[shift + p] * piece, piece), piece)
        term = contract(turned, right_ref[:, at], 1, 0)
        if added:
            term = term + refs[0][p].astype(F32)
        if stacked:
            outs[0][p] = term.astype(BF16)
        else:
            outs[p][...] = term.astype(BF16)


def unit_grad(left, right, order, shift, count, piece, received=None, apart=False):
    rows, units = left.shape
    columns = right.shape[1]
    width = GRAD_UNITS if count <= 4 else UNITS
    stack = pl.BlockSpec((count, width, piece), lambda i, order_ref: (0, i, 0))
    single = pl.BlockSpec((width, piece), lambda i, order_ref: (i, 0))
    extra = [] if received is None else [received]
    if apart:
        out_shape = [jax.ShapeDtypeStruct((units, piece), BF16)] * count
        out_specs = [single] * count
    else:
        out_shape = jax.ShapeDtypeStruct((count, units, piece), BF16)
        out_specs = stack
    return pl.pallas_call(
        functools.partial(unit_grad_kernel, count, shift, len(extra), not apart),
        out_shape=out_shape,
        grid_spec=pltpu.PrefetchScalarGridSpec(
            num_scalar_prefetch=1,
            grid=(pl.cdiv(units, width),),
            in_specs=[
                pl.BlockSpec((rows, width), lambda i, order_ref: (0, i)),
                pl.BlockSpec(
                    (rows, columns), lambda i, order_ref: (0, 0), pipeline_mode=pl.Buffered(1)
                ),
            ]
            + [stack] * len(extra),
            out_specs=out_specs,
        ),
        compiler_params=pltpu.CompilerParams(vmem_limit_bytes=48 << 20),
        cost_estimate=pl.CostEstimate(
            flops=2 * rows * units * count * piece,
            transcendentals=0,
            bytes_accessed=2
            * (rows * units + rows * columns + (1 + len(extra)) * units * count * piece),
        ),
        name="unit_grad",
    )(order, left, right, *extra)


def rope_tables(position):
    half_width = HD // 2
    inverse = ROPE_BASE ** (-(jnp.arange(half_width, dtype=F32) * 2.0 / HD))
    angles = position.astype(F32)[:, None] * inverse[None, :]
    cosine, sine = jnp.cos(angles), jnp.sin(angles)
    return (
        jnp.concatenate([cosine, cosine], axis=1),
        jnp.concatenate([-sine, sine], axis=1),
    )


def rotate(values, cosine, sine):
    half_width = values.shape[-1] // 2
    swapped = jnp.concatenate([values[..., half_width:], values[..., :half_width]], axis=-1)
    return values * cosine + swapped * sine


def norm_forward(values, gain_vector):
    rms_scale = lax.rsqrt(jnp.mean(values * values, axis=1, keepdims=True) + EPSILON)
    return (values * rms_scale * gain_vector, rms_scale)


def norm_backward(values, rms_scale, gain_vector, gradient):
    weighted = gradient * gain_vector
    gain_grad = jnp.sum(gradient * values * rms_scale, axis=0)
    inner_mean = jnp.mean(weighted * values, axis=1, keepdims=True)
    return (rms_scale * weighted - values * rms_scale**3 * inner_mean, gain_grad)


def local(
    inputs,
    out_grad,
    q_weight,
    q_bias,
    kv_weight,
    kv_bias,
    out_weight,
    attn_gain,
    ffn_gain,
    gate_weight,
    up_weight,
    down_weight,
    block_order,
    long_docs,
    short_docs,
):
    seq, head = SeqAxis(), HeadAxis()
    local_rows, depth = inputs.shape
    span_rows = local_rows * head.size
    wide = KV * HD * 2
    half = depth // 2
    pieces = seq.size // 2

    inputs16, cotangent16 = shuffle(seq.order, inputs, out_grad)
    grad_all = lax.all_gather(cotangent16, "head", axis=0, tiled=True)
    q_a, q_b = seq.gather(head.gather_small(q_weight, 1))
    out_a, out_b = seq.gather(head.gather_small(out_weight, 0), axis=1)

    kv_rows_each = kv_weight.shape[0]
    sizes = [q_bias.shape[0], kv_bias.shape[0], attn_gain.shape[0], ffn_gain.shape[0]]
    cuts = [sum(sizes[:i]) for i in range(5)]
    padded = -(-(kv_rows_each + 1) // 16) * 16
    strip = jnp.concatenate([q_bias, kv_bias, attn_gain, ffn_gain])
    strip = jnp.pad(strip[None, :], ((0, padded - kv_rows_each - 1), (0, wide - strip.shape[0])))
    pack = jnp.concatenate([kv_weight, strip], axis=0)
    pack_all = jnp.concatenate(seq.gather(head.gather_small(pack, 0), ordered=False), axis=0)
    pack_all = pack_all.reshape(seq.size, head.size, padded, wide)
    kv_full = pack_all[:, :, :kv_rows_each].reshape(depth, wide)
    strips = pack_all[:, :, kv_rows_each].astype(F32)

    def part_of(i):
        return strips[:, :, cuts[i] : cuts[i + 1]].reshape(seq.size, -1)

    q_bias_full = part_of(0)[seq.place].reshape(1, -1)
    kv_bias_full = part_of(1)[seq.place].reshape(1, -1)
    attn_gain32 = part_of(2).reshape(1, -1)
    ffn_gain32 = part_of(3).reshape(1, -1)

    lengths = jnp.concatenate([long_docs, short_docs])
    index = jnp.arange(lengths.shape[0], dtype=jnp.int32)
    starts = jnp.sum(jnp.where(index[None, :] < index[:, None], lengths[None, :], 0), axis=1)
    long_total = starts[long_docs.shape[0]]
    row_start = (seq.me * head.size + head.me) * local_rows
    stream = (
        block_order[row_start // BLK] * BLK
        + row_start % BLK
        + jnp.arange(local_rows, dtype=jnp.int32)
    )
    position = jnp.where(stream >= long_total, stream - long_total, stream)
    first = jnp.max(jnp.where(starts[None, :] <= stream[:, None], starts[None, :], 0), axis=1)
    cosine, sine = rope_tables(position)
    blocks = jnp.arange(block_order.shape[0], dtype=jnp.int32)
    storage = jnp.sum(
        jnp.where(block_order[:, None] == blocks[None, :], blocks[:, None], 0), axis=0
    )
    span_blocks = span_rows // BLK
    base = seq.place[storage // span_blocks] * span_rows + storage % span_blocks * BLK
    per_block = BLK // TILE
    offsets = (base[:, None] + jnp.arange(per_block, dtype=jnp.int32)[None, :] * TILE).reshape(-1)
    bounds = jnp.stack([first[0] // TILE, stream[-1] // TILE]).astype(jnp.int32)
    where = (offsets.astype(jnp.int32), bounds)
    tables = (cosine, sine, stream[None, :], first[None, :])

    residual = inputs16.astype(F32)
    normed32, attn_scale = norm_forward(residual, attn_gain32)
    normed = normed32.astype(BF16)
    kv_raw = jnp.dot(normed, kv_full, preferred_element_type=F32) + kv_bias_full
    key_part = rotate(
        kv_raw[:, : KV * HD].reshape(local_rows, KV, HD), cosine[:, None, :], sine[:, None, :]
    )
    kv_rows = jnp.concatenate(
        [key_part.reshape(local_rows, KV * HD), kv_raw[:, KV * HD :]], axis=1
    ).astype(BF16)
    query_raw = (
        jnp.dot(normed[:, :half], q_a, preferred_element_type=F32)
        + jnp.dot(normed[:, half:], q_b, preferred_element_type=F32)
        + q_bias_full
    )
    kv_halves = seq.gather(head.gather_small(kv_rows, 0))
    queries, mixed, lse = attention_forward(*where, query_raw, *tables, *kv_halves)
    hidden = residual + jnp.concatenate(
        [jnp.dot(mixed, part, preferred_element_type=F32) for part in (out_a, out_b)], axis=1
    )
    normed2_32, ffn_scale = norm_forward(hidden, ffn_gain32)
    normed2 = normed2_32.astype(BF16)

    straight = jnp.arange(seq.size, dtype=jnp.int32)
    gate_own, up_own = after((gate_weight.T, up_weight.T), kv_halves[0])
    gate_all = lax.all_gather(gate_own, "seq", axis=0, tiled=False)
    up_all = lax.all_gather(up_own, "seq", axis=0, tiled=False)
    down = [
        half_of.reshape(pieces, -1, depth // seq.size)
        for half_of in seq.gather(after(down_weight, kv_halves[0]))
    ]
    normed2_all = head.gather(normed2)
    act, d_gate, d_up = ffn_middle(seq.order, normed2_all, grad_all, gate_all, up_all, *down)
    d_normed2_terms = ffn_back(seq.order, d_gate, d_up, gate_all, up_all)

    def total(parts):
        return sum(part.astype(F32) for part in parts)

    piece = depth // seq.size

    def by_lane(left, right):
        def mine(received):
            return unit_grad(left, right, straight, 0, pieces, piece, received, True)

        return seq.reduce(mine, unit_grad(left, right, straight, pieces, pieces, piece))

    def whole_grad(left, right):
        return unit_grad(after(left, d_normed2_terms), right, seq.place, 0, seq.size, piece)

    def scattered(whole):
        return lax.psum_scatter(whole, "seq", scatter_dimension=0, tiled=False).astype(F32)

    terms = [
        whole_grad(act, grad_all), whole_grad(d_gate, normed2_all), whole_grad(d_up, normed2_all)
    ]
    d_normed2 = total(head.reduce(d_normed2_terms, terms))
    down_grad, gate_grad, up_grad = (scattered(whole) for whole in terms)
    gate_grad, up_grad = gate_grad.T, up_grad.T

    d_hidden_norm, ffn_gain_grad = norm_backward(hidden, ffn_scale, ffn_gain32, d_normed2)
    d_hidden = cotangent16.astype(F32) + d_hidden_norm
    d_attn = d_hidden.astype(BF16)
    d_mixed = (
        contract(d_attn[:, :half], out_a, 1, 1) + contract(d_attn[:, half:], out_b, 1, 1)
    ).astype(BF16)
    d_queries, d_kv_a, d_kv_b = attention_backward(
        *where, queries, *tables, mixed, d_mixed, lse, *kv_halves
    )

    ffn_terms = ffn_forth(after(act, d_normed2), *down)
    beside = (d_queries, d_kv_a, d_kv_b)
    (output,) = shuffle(seq.place, hidden + total(head.reduce(ffn_terms, beside)))

    def stacked(value):
        return value.reshape(pieces, value.shape[0] // pieces, value.shape[1])

    def adding(value):
        def add(received):
            return list(value if received is None else value + received)

        return add

    d_kv_span = seq.reduce(adding(stacked(d_kv_a)), stacked(d_kv_b))
    d_kv_own = head.reduce_small(d_kv_span.astype(BF16), 0)
    key_back = rotate(
        d_kv_own[:, : KV * HD].reshape(local_rows, KV, HD), cosine[:, None, :], -sine[:, None, :]
    )
    d_kv = jnp.concatenate(
        [key_back.reshape(local_rows, KV * HD), d_kv_own[:, KV * HD :]], axis=1
    ).astype(BF16)
    d_normed = jnp.concatenate(
        [contract(d_queries, part, 1, 1) for part in (q_a, q_b)], axis=1
    ) + contract(d_kv, kv_full, 1, 1)
    d_input_norm, attn_gain_grad = norm_backward(residual, attn_scale, attn_gain32, d_normed)
    (input_grad,) = shuffle(seq.place, d_hidden + d_input_norm)

    out_span = by_lane(mixed, d_attn)
    out_weight_grad = head.reduce_small(out_span.astype(BF16), 0)
    rest = (straight, 0, 1, d_queries.shape[1])

    def q_part(i, received):
        columns = normed[:, i * half : (i + 1) * half]
        if received is not None:
            received = received.reshape(1, half, -1)
        return stacked(unit_grad(columns, d_queries, *rest, received)[0])

    q_span = seq.reduce(lambda received: list(q_part(0, received)), q_part(1, None))
    q_weight_grad = head.reduce_small(q_span.astype(BF16), 1)
    kv_part = contract(normed, d_kv, 0, 0).reshape(seq.size, head.size, kv_rows_each, wide)
    q_bias_part = jnp.sum(d_queries.astype(F32), axis=0).reshape(seq.size, -1)[seq.order]
    kv_bias_part = jnp.sum(d_kv.astype(F32), axis=0).reshape(seq.size, -1)[seq.order]
    strips = jnp.concatenate(
        [
            item.reshape(seq.size, head.size, 1, -1)
            for item in (q_bias_part, kv_bias_part, attn_gain_grad, ffn_gain_grad)
        ],
        axis=3,
    )
    strips = jnp.pad(
        strips,
        ((0, 0), (0, 0), (0, padded - kv_rows_each - 1), (0, wide - strips.shape[3])),
    )
    small = jnp.concatenate([kv_part, strips], axis=2).astype(BF16)
    small = small.reshape(seq.size, head.size * padded, wide)
    small = seq.reduce(adding(small[:pieces]), small[pieces:])
    small = head.reduce_small(small.astype(BF16), 0)
    kv_weight_grad = small[:kv_rows_each]
    tail = small[kv_rows_each]
    q_bias_grad, kv_bias_grad, attn_grad, ffn_grad = (
        tail[cuts[i] : cuts[i + 1]] for i in range(4)
    )
    return (
        output,
        input_grad,
        q_weight_grad,
        q_bias_grad,
        kv_weight_grad,
        kv_bias_grad,
        out_weight_grad,
        attn_grad,
        ffn_grad,
        gate_grad,
        up_grad,
        down_grad,
    )


def solution(mesh):
    in_specs = (
        P(("seq", "head"), None),
        P(("seq", "head"), None),
        P("seq", "head"),
        P(("seq", "head")),
        P(("seq", "head"), None),
        P(("seq", "head")),
        P("head", "seq"),
        P(("seq", "head")),
        P(("seq", "head")),
        P("seq", "head"),
        P("seq", "head"),
        P("head", "seq"),
        P(),
        P(),
        P(),
    )
    out_specs = (
        P(("seq", "head"), None),
        P(("seq", "head"), None),
        P("seq", "head"),
        P(("seq", "head")),
        P(("seq", "head"), None),
        P(("seq", "head")),
        P("head", "seq"),
        P(("seq", "head")),
        P(("seq", "head")),
        P("seq", "head"),
        P("seq", "head"),
        P("head", "seq"),
    )
    return jax.shard_map(local, mesh=mesh, in_specs=in_specs, out_specs=out_specs, check_vma=False)
```

```python
import functools

import jax
import jax.numpy as jnp
from jax import lax
from jax.experimental import pallas as pl
from jax.experimental.pallas import tpu as pltpu
from jax.sharding import PartitionSpec as P

HEADS = 16
KV = 2
HD = 128
BLK = 512
GROUP = HEADS // KV
TILE = 512
BATCH = 8
ROWS = 1024
UNITS = 256
GRAD_UNITS = 512

EPSILON = 1e-06
ROPE_BASE = 1000000.0
NEGATIVE = -1e30
SCALE = HD**-0.5
LOG2E = 1.4426950408889634

F32 = jnp.float32
BF16 = jnp.bfloat16

ORDER = ((0, 2, 4, 6, 1, 5, 3, 7), (0, 4, 2, 6, 1, 3, 5, 7))
RELAY = ((0, 1, 2, 3), (1, 0, 2, 3), (2, 3, 1, 0), (3, 2, 1, 0))


def contract(left_side, right_side, left_dim, right_dim):
    return lax.dot_general(
        left_side,
        right_side,
        (((left_dim,), (right_dim,)), ((), ())),
        preferred_element_type=F32,
    )


def after(value, *others):
    return lax.optimization_barrier((value, *others))[0]


class Lane:
    def __init__(self, depth):
        self.depth = depth
        self.done = []

    def __call__(self, send, value):
        if len(self.done) >= self.depth:
            value = after(value, self.done[-self.depth])
        self.done.append(send(value))
        return self.done[-1]


class SeqAxis:
    def __init__(self):
        self.size = lax.axis_size("seq")
        self.me = lax.axis_index("seq")
        self.fast = self.size == 8
        self.lane = Lane(2)
        places = jnp.arange(self.size, dtype=jnp.int32)
        if self.fast:
            odd = self.me % 2 == 1
            self.order = self.me ^ jnp.where(odd, jnp.array(ORDER[1]), jnp.array(ORDER[0]))
        else:
            self.order = places
        self.place = jnp.sum(
            jnp.where(self.order[:, None] == places[None, :], places[:, None], 0), axis=0
        )

    def swap(self, value, even, odd, ordered=True):
        pairs = [(i, i ^ (odd if i % 2 else even)) for i in range(self.size)]

        def send(item):
            return lax.ppermute(item, "seq", pairs)

        return self.lane(send, value) if ordered else send(value)

    def begin(self, value, ordered=True):
        if not self.fast:
            return [value]
        return [value, self.swap(value, 2, 4, ordered), self.swap(value, 4, 2, ordered)]

    def finish(self, begun, axis=0, ordered=True):
        if not self.fast:
            whole = lax.all_gather(begun[0], "seq", axis=axis, tiled=True)
            half = whole.shape[axis] // 2
            return [
                lax.slice_in_dim(whole, i * half, (i + 1) * half, axis=axis) for i in range(2)
            ]
        value, one, two = begun
        mine = jnp.concatenate([value, one, two, self.swap(one, 4, 2, ordered)], axis=axis)
        return [mine, self.swap(mine, 1, 1, False)]

    def gather(self, value, axis=0, ordered=True):
        return self.finish(self.begin(value, ordered), axis, ordered)

    def reduce(self, mine, other):
        if not self.fast:
            whole = jnp.concatenate([jnp.stack(mine(None)), other], axis=0)
            return lax.psum_scatter(whole, "seq", scatter_dimension=0, tiled=False).astype(F32)
        here, one, two, corner = mine(self.swap(other, 1, 1, False))
        corner = self.swap(corner, 4, 2)
        two = self.swap(two, 4, 2)
        one = self.swap(one + corner, 2, 4)
        return here.astype(F32) + two.astype(F32) + one.astype(F32)


class HeadAxis:
    def __init__(self):
        self.size = lax.axis_size("head")
        self.me = lax.axis_index("head")
        self.fast = self.size == 4
        self.inner = (self.me == 1) | (self.me == 2)
        self.relay = jnp.array(RELAY, jnp.int32)[self.me] if self.fast else None
        self.direct = self.me ^ jnp.arange(self.size, dtype=jnp.int32)

    def send(self, value, pairs):
        return lax.ppermute(value, "head", pairs)

    def gather(self, value):
        if not self.fast:
            return lax.all_gather(value, "head", axis=0, tiled=True), (value,)
        pair = [(0, 1), (1, 0), (2, 3), (3, 2)]
        middle = [(1, 2), (2, 1)]
        outward = [(1, 0), (2, 3)]
        slot1 = self.send(value, pair)
        near = self.send(value, middle)
        far = self.send(slot1, middle)
        slot2 = jnp.where(self.inner, near, self.send(near, outward))
        slot3 = jnp.where(self.inner, far, self.send(far, outward))
        return place([value, slot1, slot2, slot3], self.relay, 0), (slot1, near)

    def reduce(self, whole, beside):
        if not self.fast:
            return [lax.psum_scatter(whole, "head", scatter_dimension=0, tiled=True)]
        pair = [(0, 1), (1, 0), (2, 3), (3, 2)]
        middle = [(1, 2), (2, 1)]
        inward = [(0, 1), (3, 2)]
        rows = whole.shape[0] // self.size
        own, slot1, slot2, slot3 = (
            lax.dynamic_slice_in_dim(whole, self.relay[k] * rows, rows, 0) for k in range(4)
        )
        far = slot3 + after(self.send(slot3, inward), beside[0])
        near = self.send(after(slot2, far), inward)
        next_door = slot1 + after(self.send(far, middle), beside[1])
        near = slot2 + near
        return [own, after(self.send(next_door, pair), beside[2]), self.send(near, middle)]

    def gather_small(self, value, axis):
        if not self.fast:
            return lax.all_gather(value, "head", axis=axis, tiled=True)
        pieces = [value] + [
            self.send(value, [(i, i ^ k) for i in range(self.size)]) for k in range(1, 4)
        ]
        return place(pieces, self.direct, axis)

    def reduce_small(self, value, axis):
        if not self.fast:
            return lax.psum_scatter(value, "head", scatter_dimension=axis, tiled=True).astype(F32)
        width = value.shape[axis] // self.size
        total = None
        for k in range(self.size):
            part = lax.dynamic_slice_in_dim(value, (self.me ^ k) * width, width, axis)
            if k:
                part = self.send(part, [(i, i ^ k) for i in range(self.size)])
            total = part.astype(F32) if total is None else total + part.astype(F32)
        return total


def vmem():
    return pl.BlockSpec(memory_space=pltpu.VMEM)


def anywhere():
    return pl.BlockSpec(memory_space=pl.ANY)


def smem():
    return pl.BlockSpec(memory_space=pltpu.SMEM)


def place_kernel(axis, order_ref, *refs):
    out_ref = refs[-1]
    for k, piece_ref in enumerate(refs[:-1]):
        width = piece_ref.shape[axis]
        at = pl.ds(pl.multiple_of(order_ref[k] * width, width), width)
        if axis:
            out_ref[:, at] = piece_ref[...]
        else:
            out_ref[at, :] = piece_ref[...]


def place(pieces, order, axis):
    shape = list(pieces[0].shape)
    shape[axis] *= len(pieces)
    return pl.pallas_call(
        functools.partial(place_kernel, axis),
        out_shape=jax.ShapeDtypeStruct(shape, pieces[0].dtype),
        in_specs=[smem()] + [vmem()] * len(pieces),
        out_specs=vmem(),
        name="place",
    )(order, *pieces)


def shuffle_kernel(count, order_ref, *refs):
    for i in range(len(refs) // 2):
        in_ref, out_ref = refs[i], refs[len(refs) // 2 + i]
        width = in_ref.shape[1] // count
        for p in range(count):
            at = pl.ds(pl.multiple_of(order_ref[p] * width, width), width)
            out_ref[:, p * width : (p + 1) * width] = in_ref[:, at]


def shuffle(order, *values):
    return pl.pallas_call(
        functools.partial(shuffle_kernel, order.shape[0]),
        out_shape=[jax.ShapeDtypeStruct(v.shape, v.dtype) for v in values],
        in_specs=[smem()] + [vmem()] * len(values),
        out_specs=[vmem()] * len(values),
        name="shuffle",
    )(order, *values)


def turn(values, cosine, sine):
    return values * cosine + pltpu.roll(values, HD // 2, 1) * sine


def allowed_bias(tile, stream, first, shape):
    key = tile * TILE + lax.broadcasted_iota(jnp.int32, shape, 0)
    return jnp.where((key >= first) & (key <= stream), 0.0, NEGATIVE)


def fetch(half_a_ref, half_b_ref, whole_ref, sem_ref):
    half = half_a_ref.shape[0]
    copies = [
        pltpu.make_async_copy(ref, whole_ref.at[pl.ds(i * half, half)], sem_ref.at[i])
        for i, ref in enumerate((half_a_ref, half_b_ref))
    ]
    for copy in copies:
        copy.start()
    return copies


def forward_kernel(
    offset_ref, bound_ref, raw_ref, cos_ref, sin_ref, stream_ref, first_ref, half_a_ref, half_b_ref,
    query_ref, mixed_ref, lse_ref,
    top_ref, total_ref, sum_ref, bias_ref, turned_ref, kv_ref, sem_ref,
):
    copies = fetch(half_a_ref, half_b_ref, kv_ref, sem_ref)
    cosine, sine = cos_ref[...], sin_ref[...]
    for h in range(HEADS):
        query_ref[h] = turn(raw_ref[:, h * HD : (h + 1) * HD], cosine, sine).astype(BF16)
    top_ref[...] = jnp.full(top_ref.shape, NEGATIVE, F32)
    total_ref[...] = jnp.zeros(total_ref.shape, F32)
    sum_ref[...] = jnp.zeros(sum_ref.shape, F32)
    for copy in copies:
        copy.wait()

    def visit(tile, carry):
        start = pl.multiple_of(offset_ref[tile], TILE)
        bias_ref[...] = allowed_bias(tile, stream_ref[...], first_ref[...], bias_ref.shape)
        for g in range(KV):
            turned_ref[g] = kv_ref[pl.ds(start, TILE), (KV + g) * HD : (KV + g + 1) * HD].T
        for g in range(KV):
            keys = kv_ref[pl.ds(start, TILE), g * HD : (g + 1) * HD]

            def some(i, carry):
                heads = [g * GROUP + i * BATCH + b for b in range(BATCH)]
                old = [top_ref[h] for h in heads]
                total = [total_ref[h] for h in heads]
                summed = [sum_ref[h] for h in heads]
                scores = [contract(keys, query_ref[h], 1, 1) for h in heads]
                bias = bias_ref[...]
                turned = turned_ref[g]
                new, fresh, fades = [], [], []
                for b in range(BATCH):
                    score = scores[b] * (SCALE * LOG2E) + bias
                    peak = jnp.maximum(old[b], jnp.max(score, axis=0, keepdims=True))
                    weights = jnp.exp2(score - peak)
                    fade = jnp.exp2(old[b] - peak)
                    new.append(peak)
                    fades.append(fade)
                    total[b] = total[b] * fade + jnp.sum(weights, axis=0, keepdims=True)
                    fresh.append(contract(turned, weights.astype(BF16), 1, 0))
                for b, h in enumerate(heads):
                    top_ref[h] = new[b]
                    total_ref[h] = total[b]
                    sum_ref[h] = summed[b] * fades[b] + fresh[b]
                return carry

            lax.fori_loop(0, GROUP // BATCH, some, 0)
        return carry

    lax.fori_loop(bound_ref[0], bound_ref[1] + 1, visit, 0)
    for h in range(HEADS):
        lse_ref[h] = top_ref[h] + jnp.log2(total_ref[h])
        mixed_ref[:, h * HD : (h + 1) * HD] = (sum_ref[h] / total_ref[h]).T.astype(BF16)


def attention_forward(offsets, bounds, query_raw, cosine, sine, stream, first, kv_a, kv_b):
    rows = query_raw.shape[0]
    kv_shape = (2 * kv_a.shape[0], kv_a.shape[1])
    return pl.pallas_call(
        forward_kernel,
        out_shape=(
            jax.ShapeDtypeStruct((HEADS, rows, HD), BF16),
            jax.ShapeDtypeStruct((rows, HEADS * HD), BF16),
            jax.ShapeDtypeStruct((HEADS, 1, rows), F32),
        ),
        in_specs=[smem(), smem()] + [vmem()] * 5 + [anywhere()] * 2,
        out_specs=[vmem()] * 3,
        scratch_shapes=[
            pltpu.VMEM((HEADS, 1, rows), F32),
            pltpu.VMEM((HEADS, 1, rows), F32),
            pltpu.VMEM((HEADS, HD, rows), F32),
            pltpu.VMEM((TILE, rows), F32),
            pltpu.VMEM((KV, HD, TILE), BF16),
            pltpu.VMEM(kv_shape, BF16),
            pltpu.SemaphoreType.DMA((2,)),
        ],
        compiler_params=pltpu.CompilerParams(vmem_limit_bytes=48 << 20),
        cost_estimate=pl.CostEstimate(
            flops=4 * HEADS * rows * HD * 2048,
            transcendentals=HEADS * rows * 2048,
            bytes_accessed=kv_a.size * 4 + query_raw.size * 8,
        ),
        name="attention_forward",
    )(offsets, bounds, query_raw, cosine, sine, stream, first, kv_a, kv_b)


def backward_kernel(
    offset_ref, bound_ref, query_ref, cos_ref, sin_ref, stream_ref, first_ref,
    mixed_ref, grad_ref, lse_ref, half_a_ref, half_b_ref,
    d_query_ref, d_half_a_ref, d_half_b_ref,
    delta_ref, head_grad_ref, sum_ref, bias_ref, turned_ref, d_tile_ref, kv_ref, sem_ref,
):
    copies = fetch(half_a_ref, half_b_ref, kv_ref, sem_ref)
    half = half_a_ref.shape[0]
    for h in range(HEADS):
        part = grad_ref[:, h * HD : (h + 1) * HD]
        head_grad_ref[h] = part
        product = part.astype(F32) * mixed_ref[:, h * HD : (h + 1) * HD].astype(F32)
        delta_ref[h] = lax.dot_general(
            jnp.ones((8, HD), F32),
            product,
            (((1,), (1,)), ((), ())),
            precision=lax.Precision.HIGHEST,
            preferred_element_type=F32,
        )[:1]
    sum_ref[...] = jnp.zeros(sum_ref.shape, F32)
    d_half_a_ref[...] = jnp.zeros(d_half_a_ref.shape, BF16)
    d_half_b_ref[...] = jnp.zeros(d_half_b_ref.shape, BF16)
    for copy in copies:
        copy.wait()

    def visit(tile, carry):
        start = pl.multiple_of(offset_ref[tile], TILE)
        bias_ref[...] = allowed_bias(tile, stream_ref[...], first_ref[...], bias_ref.shape)
        d_tile_ref[...] = jnp.zeros(d_tile_ref.shape, F32)
        for g in range(KV):
            turned_ref[g] = kv_ref[pl.ds(start, TILE), g * HD : (g + 1) * HD].T
        for g in range(KV):
            keys = kv_ref[pl.ds(start, TILE), g * HD : (g + 1) * HD]
            values = kv_ref[pl.ds(start, TILE), (KV + g) * HD : (KV + g + 1) * HD]

            def some(i, carry):
                heads = [g * GROUP + i * BATCH + b for b in range(BATCH)]
                query = [query_ref[h] for h in heads]
                head_grad = [head_grad_ref[h] for h in heads]
                summed = [sum_ref[h] for h in heads]
                bias = bias_ref[...]
                turned = turned_ref[g]
                d_keys, d_values = d_tile_ref[g], d_tile_ref[KV + g]
                for b, h in enumerate(heads):
                    scores = contract(keys, query[b], 1, 1) * (SCALE * LOG2E) + bias
                    weights = jnp.exp2(scores - lse_ref[h])
                    d_weights = contract(values, head_grad[b], 1, 1)
                    d_scores = (weights * (d_weights - delta_ref[h])).astype(BF16)
                    d_keys += contract(d_scores, query[b], 1, 0)
                    d_values += contract(weights.astype(BF16), head_grad[b], 1, 0)
                    summed[b] += contract(turned, d_scores, 1, 0)
                for b, h in enumerate(heads):
                    sum_ref[h] = summed[b]
                d_tile_ref[g] = d_keys
                d_tile_ref[KV + g] = d_values
                return carry

            lax.fori_loop(0, GROUP // BATCH, some, 0)
        for i, d_ref in enumerate((d_half_a_ref, d_half_b_ref)):

            @pl.when(start // half == i)
            def _():
                at = pl.ds(pl.multiple_of(start - i * half, TILE), TILE)
                for g in range(KV):
                    d_ref[at, g * HD : (g + 1) * HD] = (d_tile_ref[g] * SCALE).astype(BF16)
                    d_ref[at, (KV + g) * HD : (KV + g + 1) * HD] = d_tile_ref[KV + g].astype(BF16)

        return carry

    lax.fori_loop(bound_ref[0], bound_ref[1] + 1, visit, 0)
    cosine, sine = cos_ref[...], -sin_ref[...]
    for h in range(HEADS):
        d_query_ref[:, h * HD : (h + 1) * HD] = turn(
            sum_ref[h].T * SCALE, cosine, sine
        ).astype(BF16)


def attention_backward(
    offsets, bounds, queries, cosine, sine, stream, first, mixed, d_mixed, lse, kv_a, kv_b
):
    rows = mixed.shape[0]
    kv_shape = (2 * kv_a.shape[0], kv_a.shape[1])
    return pl.pallas_call(
        backward_kernel,
        out_shape=(
            jax.ShapeDtypeStruct((rows, HEADS * HD), BF16),
            jax.ShapeDtypeStruct(kv_a.shape, BF16),
            jax.ShapeDtypeStruct(kv_b.shape, BF16),
        ),
        in_specs=[smem(), smem()] + [vmem()] * 8 + [anywhere()] * 2,
        out_specs=[vmem()] * 3,
        scratch_shapes=[
            pltpu.VMEM((HEADS, 1, rows), F32),
            pltpu.VMEM((HEADS, rows, HD), BF16),
            pltpu.VMEM((HEADS, HD, rows), F32),
            pltpu.VMEM((TILE, rows), F32),
            pltpu.VMEM((KV, HD, TILE), BF16),
            pltpu.VMEM((2 * KV, TILE, HD), F32),
            pltpu.VMEM(kv_shape, BF16),
            pltpu.SemaphoreType.DMA((2,)),
        ],
        compiler_params=pltpu.CompilerParams(vmem_limit_bytes=56 << 20),
        cost_estimate=pl.CostEstimate(
            flops=10 * HEADS * rows * HD * 2048,
            transcendentals=HEADS * rows * 2048,
            bytes_accessed=kv_a.size * 8 + mixed.size * 8,
        ),
        name="attention_backward",
    )(offsets, bounds, queries, cosine, sine, stream, first, mixed, d_mixed, lse, kv_a, kv_b)


def side_by_side(order_ref, weight_ref):
    return jnp.concatenate([weight_ref[order_ref[p]] for p in range(weight_ref.shape[0])], axis=1)


def ffn_kernel(
    order_ref, normed_ref, grad_ref, gate_ref, up_ref, down_a_ref, down_b_ref,
    act_ref, d_gate_ref, d_up_ref,
):
    step = ROWS

    def chunk(i, carry):
        at = pl.ds(pl.multiple_of(i * step, step), step)
        normed = normed_ref[at, :]
        gate = contract(normed, side_by_side(order_ref, gate_ref), 1, 1)
        up = contract(normed, side_by_side(order_ref, up_ref), 1, 1)
        down = [ref[p] for ref in (down_a_ref, down_b_ref) for p in range(ref.shape[0])]
        d_act = contract(grad_ref[at, :], jnp.concatenate(down, axis=1), 1, 1)
        sigmoid = jax.nn.sigmoid(gate)
        silu = gate * sigmoid
        act_ref[at, :] = (silu * up).astype(BF16)
        d_up_ref[at, :] = (d_act * silu).astype(BF16)
        d_gate_ref[at, :] = (d_act * up * (sigmoid + silu * (1.0 - sigmoid))).astype(BF16)
        return carry

    lax.fori_loop(0, normed_ref.shape[0] // step, chunk, 0)


def ffn_middle(order, normed, grad, gate, up, down_a, down_b):
    rows, depth = normed.shape
    pieces, units, piece = gate.shape
    width = UNITS
    whole = pl.BlockSpec((rows, depth), lambda i, order_ref: (0, 0), pipeline_mode=pl.Buffered(1))
    weight = pl.BlockSpec((pieces, width, piece), lambda i, order_ref: (0, i, 0))
    half = pl.BlockSpec((pieces // 2, width, piece), lambda i, order_ref: (0, i, 0))
    return pl.pallas_call(
        ffn_kernel,
        out_shape=(jax.ShapeDtypeStruct((rows, units), BF16),) * 3,
        grid_spec=pltpu.PrefetchScalarGridSpec(
            num_scalar_prefetch=1,
            grid=(pl.cdiv(units, width),),
            in_specs=[whole, whole, weight, weight, half, half],
            out_specs=[pl.BlockSpec((rows, width), lambda i, order_ref: (0, i))] * 3,
        ),
        compiler_params=pltpu.CompilerParams(vmem_limit_bytes=48 << 20),
        cost_estimate=pl.CostEstimate(
            flops=6 * rows * depth * units,
            transcendentals=rows * units,
            bytes_accessed=2 * (3 * depth * units + 3 * rows * units + 2 * rows * depth),
        ),
        name="ffn_middle",
    )(order, normed, grad, gate, up, down_a, down_b)


def back_kernel(order_ref, d_gate_ref, d_up_ref, gate_ref, up_ref, out_ref):
    out_ref[...] = (
        contract(d_gate_ref[...], gate_ref[0], 1, 0) + contract(d_up_ref[...], up_ref[0], 1, 0)
    ).astype(BF16)


def ffn_back(order, d_gate, d_up, gate, up):
    rows, units = d_gate.shape
    pieces, _, piece = gate.shape
    whole = pl.BlockSpec((rows, units), lambda i, order_ref: (0, 0), pipeline_mode=pl.Buffered(1))
    part = pl.BlockSpec((1, units, piece), lambda i, order_ref: (order_ref[i], 0, 0))
    return pl.pallas_call(
        back_kernel,
        out_shape=jax.ShapeDtypeStruct((rows, pieces * piece), BF16),
        grid_spec=pltpu.PrefetchScalarGridSpec(
            num_scalar_prefetch=1,
            grid=(pieces,),
            in_specs=[whole, whole, part, part],
            out_specs=pl.BlockSpec((rows, piece), lambda i, order_ref: (0, i)),
        ),
        compiler_params=pltpu.CompilerParams(vmem_limit_bytes=48 << 20),
        cost_estimate=pl.CostEstimate(
            flops=4 * rows * pieces * piece * units,
            transcendentals=0,
            bytes_accessed=2 * (2 * pieces * piece * units + 2 * rows * units),
        ),
        name="ffn_back",
    )(order, d_gate, d_up, gate, up)


def forth_kernel(act_ref, down_a_ref, down_b_ref, out_ref):
    count = pl.num_programs(0) // 2
    for i, down_ref in enumerate((down_a_ref, down_b_ref)):

        @pl.when(pl.program_id(0) // count == i)
        def _():
            out_ref[...] = contract(act_ref[...], down_ref[0], 1, 0).astype(BF16)


def ffn_forth(act, down_a, down_b):
    rows, units = act.shape
    count, _, piece = down_a.shape
    return pl.pallas_call(
        forth_kernel,
        out_shape=jax.ShapeDtypeStruct((rows, 2 * count * piece), BF16),
        grid=(2 * count,),
        in_specs=[
            pl.BlockSpec((rows, units), lambda i: (0, 0), pipeline_mode=pl.Buffered(1)),
            pl.BlockSpec((1, units, piece), lambda i: (jnp.minimum(i, count - 1), 0, 0)),
            pl.BlockSpec((1, units, piece), lambda i: (jnp.maximum(i - count, 0), 0, 0)),
        ],
        out_specs=pl.BlockSpec((rows, piece), lambda i: (0, i)),
        compiler_params=pltpu.CompilerParams(vmem_limit_bytes=48 << 20),
        cost_estimate=pl.CostEstimate(
            flops=4 * rows * count * piece * units,
            transcendentals=0,
            bytes_accessed=2 * (2 * count * piece * units + rows * units),
        ),
        name="ffn_forth",
    )(act, down_a, down_b)


def unit_grad_kernel(count, shift, added, stacked, order_ref, left_ref, right_ref, *refs):
    outs = refs[added:]
    piece = outs[0].shape[-1]
    turned = left_ref[...].T
    for p in range(count):
        at = pl.ds(pl.multiple_of(order_ref[shift + p] * piece, piece), piece)
        term = contract(turned, right_ref[:, at], 1, 0)
        if added:
            term = term + refs[0][p].astype(F32)
        if stacked:
            outs[0][p] = term.astype(BF16)
        else:
            outs[p][...] = term.astype(BF16)


def unit_grad(left, right, order, shift, count, piece, received=None, apart=False):
    rows, units = left.shape
    columns = right.shape[1]
    width = GRAD_UNITS if count <= 4 else UNITS
    stack = pl.BlockSpec((count, width, piece), lambda i, order_ref: (0, i, 0))
    single = pl.BlockSpec((width, piece), lambda i, order_ref: (i, 0))
    extra = [] if received is None else [received]
    if apart:
        out_shape = [jax.ShapeDtypeStruct((units, piece), BF16)] * count
        out_specs = [single] * count
    else:
        out_shape = jax.ShapeDtypeStruct((count, units, piece), BF16)
        out_specs = stack
    return pl.pallas_call(
        functools.partial(unit_grad_kernel, count, shift, len(extra), not apart),
        out_shape=out_shape,
        grid_spec=pltpu.PrefetchScalarGridSpec(
            num_scalar_prefetch=1,
            grid=(pl.cdiv(units, width),),
            in_specs=[
                pl.BlockSpec((rows, width), lambda i, order_ref: (0, i)),
                pl.BlockSpec(
                    (rows, columns), lambda i, order_ref: (0, 0), pipeline_mode=pl.Buffered(1)
                ),
            ]
            + [stack] * len(extra),
            out_specs=out_specs,
        ),
        compiler_params=pltpu.CompilerParams(vmem_limit_bytes=48 << 20),
        cost_estimate=pl.CostEstimate(
            flops=2 * rows * units * count * piece,
            transcendentals=0,
            bytes_accessed=2
            * (rows * units + rows * columns + (1 + len(extra)) * units * count * piece),
        ),
        name="unit_grad",
    )(order, left, right, *extra)


def rope_tables(position):
    half_width = HD // 2
    inverse = ROPE_BASE ** (-(jnp.arange(half_width, dtype=F32) * 2.0 / HD))
    angles = position.astype(F32)[:, None] * inverse[None, :]
    cosine, sine = jnp.cos(angles), jnp.sin(angles)
    return (
        jnp.concatenate([cosine, cosine], axis=1),
        jnp.concatenate([-sine, sine], axis=1),
    )


def rotate(values, cosine, sine):
    half_width = values.shape[-1] // 2
    swapped = jnp.concatenate([values[..., half_width:], values[..., :half_width]], axis=-1)
    return values * cosine + swapped * sine


def norm_forward(values, gain_vector):
    rms_scale = lax.rsqrt(jnp.mean(values * values, axis=1, keepdims=True) + EPSILON)
    return (values * rms_scale * gain_vector, rms_scale)


def norm_backward(values, rms_scale, gain_vector, gradient):
    weighted = gradient * gain_vector
    gain_grad = jnp.sum(gradient * values * rms_scale, axis=0)
    inner_mean = jnp.mean(weighted * values, axis=1, keepdims=True)
    return (rms_scale * weighted - values * rms_scale**3 * inner_mean, gain_grad)


def local(
    inputs,
    out_grad,
    q_weight,
    q_bias,
    kv_weight,
    kv_bias,
    out_weight,
    attn_gain,
    ffn_gain,
    gate_weight,
    up_weight,
    down_weight,
    block_order,
    long_docs,
    short_docs,
):
    seq, head = SeqAxis(), HeadAxis()
    local_rows, depth = inputs.shape
    span_rows = local_rows * head.size
    wide = KV * HD * 2
    half = depth // 2
    pieces = seq.size // 2

    inputs16, cotangent16 = shuffle(seq.order, inputs, out_grad)
    gate_all = lax.all_gather(gate_weight.T, "seq", axis=0, tiled=False)
    q_span = head.gather_small(q_weight, 1)
    out_span = head.gather_small(out_weight, 0)
    q_a, q_b = seq.gather(q_span)

    kv_rows_each = kv_weight.shape[0]
    sizes = [q_bias.shape[0], kv_bias.shape[0], attn_gain.shape[0], ffn_gain.shape[0]]
    cuts = [sum(sizes[:i]) for i in range(5)]
    padded = -(-(kv_rows_each + 1) // 16) * 16
    strip = jnp.concatenate([q_bias, kv_bias, attn_gain, ffn_gain])
    strip = jnp.pad(strip[None, :], ((0, padded - kv_rows_each - 1), (0, wide - strip.shape[0])))
    pack = jnp.concatenate([kv_weight, strip], axis=0)
    pack_all = jnp.concatenate(seq.gather(head.gather_small(pack, 0), ordered=False), axis=0)
    pack_all = pack_all.reshape(seq.size, head.size, padded, wide)
    kv_full = pack_all[:, :, :kv_rows_each].reshape(depth, wide)
    strips = pack_all[:, :, kv_rows_each].astype(F32)

    def part_of(i):
        return strips[:, :, cuts[i] : cuts[i + 1]].reshape(seq.size, -1)

    q_bias_full = part_of(0)[seq.place].reshape(1, -1)
    kv_bias_full = part_of(1)[seq.place].reshape(1, -1)
    attn_gain32 = part_of(2).reshape(1, -1)
    ffn_gain32 = part_of(3).reshape(1, -1)

    lengths = jnp.concatenate([long_docs, short_docs])
    index = jnp.arange(lengths.shape[0], dtype=jnp.int32)
    starts = jnp.sum(jnp.where(index[None, :] < index[:, None], lengths[None, :], 0), axis=1)
    long_total = starts[long_docs.shape[0]]
    row_start = (seq.me * head.size + head.me) * local_rows
    stream = (
        block_order[row_start // BLK] * BLK
        + row_start % BLK
        + jnp.arange(local_rows, dtype=jnp.int32)
    )
    position = jnp.where(stream >= long_total, stream - long_total, stream)
    first = jnp.max(jnp.where(starts[None, :] <= stream[:, None], starts[None, :], 0), axis=1)
    cosine, sine = rope_tables(position)
    blocks = jnp.arange(block_order.shape[0], dtype=jnp.int32)
    storage = jnp.sum(
        jnp.where(block_order[:, None] == blocks[None, :], blocks[:, None], 0), axis=0
    )
    span_blocks = span_rows // BLK
    base = seq.place[storage // span_blocks] * span_rows + storage % span_blocks * BLK
    per_block = BLK // TILE
    offsets = (base[:, None] + jnp.arange(per_block, dtype=jnp.int32)[None, :] * TILE).reshape(-1)
    bounds = jnp.stack([first[0] // TILE, stream[-1] // TILE]).astype(jnp.int32)
    where = (offsets.astype(jnp.int32), bounds)
    tables = (cosine, sine, stream[None, :], first[None, :])

    residual = inputs16.astype(F32)
    normed32, attn_scale = norm_forward(residual, attn_gain32)
    normed = normed32.astype(BF16)
    kv_raw = jnp.dot(normed, kv_full, preferred_element_type=F32) + kv_bias_full
    key_part = rotate(
        kv_raw[:, : KV * HD].reshape(local_rows, KV, HD), cosine[:, None, :], sine[:, None, :]
    )
    kv_rows = jnp.concatenate(
        [key_part.reshape(local_rows, KV * HD), kv_raw[:, KV * HD :]], axis=1
    ).astype(BF16)
    query_raw = (
        jnp.dot(normed[:, :half], q_a, preferred_element_type=F32)
        + jnp.dot(normed[:, half:], q_b, preferred_element_type=F32)
        + q_bias_full
    )
    kv_span = head.gather_small(after(kv_rows, q_span, out_span), 0)
    cotangent_late = after(cotangent16, kv_span, gate_all)
    kv_halves = seq.gather(after(kv_span, cotangent_late))
    out_a, out_b = seq.gather(out_span, axis=1)
    grad_all = lax.all_gather(cotangent_late, "head", axis=0, tiled=True)
    up_all = lax.all_gather(after(up_weight.T, kv_halves[0]), "seq", axis=0, tiled=False)
    queries, mixed, lse = attention_forward(*where, query_raw, *tables, *kv_halves)
    hidden = residual + jnp.concatenate(
        [jnp.dot(mixed, part, preferred_element_type=F32) for part in (out_a, out_b)], axis=1
    )
    normed2_32, ffn_scale = norm_forward(hidden, ffn_gain32)
    normed2 = normed2_32.astype(BF16)

    straight = jnp.arange(seq.size, dtype=jnp.int32)
    normed2_all, first_step = head.gather(normed2)
    down_begun = seq.begin(after(down_weight, *first_step))
    down_begun = [after(item, normed2_all) for item in down_begun]
    down = [
        half_of.reshape(pieces, -1, depth // seq.size) for half_of in seq.finish(down_begun)
    ]
    act, d_gate, d_up = ffn_middle(seq.order, normed2_all, grad_all, gate_all, up_all, *down)
    d_normed2_terms = ffn_back(seq.order, d_gate, d_up, gate_all, up_all)

    def total(parts):
        return sum(part.astype(F32) for part in parts)

    piece = depth // seq.size

    def by_lane(left, right):
        def mine(received):
            return unit_grad(left, right, straight, 0, pieces, piece, received, True)

        return seq.reduce(mine, unit_grad(left, right, straight, pieces, pieces, piece))

    def whole_grad(left, right):
        return unit_grad(after(left, d_normed2_terms), right, seq.place, 0, seq.size, piece)

    def scattered(whole):
        return lax.psum_scatter(whole, "seq", scatter_dimension=0, tiled=False).astype(F32)

    terms = [
        whole_grad(act, grad_all), whole_grad(d_gate, normed2_all), whole_grad(d_up, normed2_all)
    ]
    d_normed2 = total(head.reduce(d_normed2_terms, terms))
    down_grad, gate_grad, up_grad = (scattered(whole) for whole in terms)
    gate_grad, up_grad = gate_grad.T, up_grad.T

    d_hidden_norm, ffn_gain_grad = norm_backward(hidden, ffn_scale, ffn_gain32, d_normed2)
    d_hidden = cotangent16.astype(F32) + d_hidden_norm
    d_attn = d_hidden.astype(BF16)
    d_mixed = (
        contract(d_attn[:, :half], out_a, 1, 1) + contract(d_attn[:, half:], out_b, 1, 1)
    ).astype(BF16)
    d_queries, d_kv_a, d_kv_b = attention_backward(
        *where, queries, *tables, mixed, d_mixed, lse, *kv_halves
    )

    ffn_terms = ffn_forth(after(act, d_normed2), *down)
    beside = (d_queries, d_kv_a, d_kv_b)
    (output,) = shuffle(seq.place, hidden + total(head.reduce(ffn_terms, beside)))

    def stacked(value):
        return value.reshape(pieces, value.shape[0] // pieces, value.shape[1])

    def adding(value):
        def add(received):
            return list(value if received is None else value + received)

        return add

    d_kv_span = seq.reduce(adding(stacked(d_kv_a)), stacked(d_kv_b))
    d_kv_own = head.reduce_small(d_kv_span.astype(BF16), 0)
    key_back = rotate(
        d_kv_own[:, : KV * HD].reshape(local_rows, KV, HD), cosine[:, None, :], -sine[:, None, :]
    )
    d_kv = jnp.concatenate(
        [key_back.reshape(local_rows, KV * HD), d_kv_own[:, KV * HD :]], axis=1
    ).astype(BF16)
    d_normed = jnp.concatenate(
        [contract(d_queries, part, 1, 1) for part in (q_a, q_b)], axis=1
    ) + contract(d_kv, kv_full, 1, 1)
    d_input_norm, attn_gain_grad = norm_backward(residual, attn_scale, attn_gain32, d_normed)
    (input_grad,) = shuffle(seq.place, d_hidden + d_input_norm)

    out_span = by_lane(mixed, d_attn)
    out_weight_grad = head.reduce_small(out_span.astype(BF16), 0)
    rest = (straight, 0, 1, d_queries.shape[1])

    def q_part(i, received):
        columns = normed[:, i * half : (i + 1) * half]
        if received is not None:
            received = received.reshape(1, half, -1)
        return stacked(unit_grad(columns, d_queries, *rest, received)[0])

    q_span = seq.reduce(lambda received: list(q_part(0, received)), q_part(1, None))
    q_weight_grad = head.reduce_small(q_span.astype(BF16), 1)
    kv_part = contract(normed, d_kv, 0, 0).reshape(seq.size, head.size, kv_rows_each, wide)
    q_bias_part = jnp.sum(d_queries.astype(F32), axis=0).reshape(seq.size, -1)[seq.order]
    kv_bias_part = jnp.sum(d_kv.astype(F32), axis=0).reshape(seq.size, -1)[seq.order]
    strips = jnp.concatenate(
        [
            item.reshape(seq.size, head.size, 1, -1)
            for item in (q_bias_part, kv_bias_part, attn_gain_grad, ffn_gain_grad)
        ],
        axis=3,
    )
    strips = jnp.pad(
        strips,
        ((0, 0), (0, 0), (0, padded - kv_rows_each - 1), (0, wide - strips.shape[3])),
    )
    small = jnp.concatenate([kv_part, strips], axis=2).astype(BF16)
    small = small.reshape(seq.size, head.size * padded, wide)
    small = seq.reduce(adding(small[:pieces]), small[pieces:])
    small = head.reduce_small(small.astype(BF16), 0)
    kv_weight_grad = small[:kv_rows_each]
    tail = small[kv_rows_each]
    q_bias_grad, kv_bias_grad, attn_grad, ffn_grad = (
        tail[cuts[i] : cuts[i + 1]] for i in range(4)
    )
    return (
        output,
        input_grad,
        q_weight_grad,
        q_bias_grad,
        kv_weight_grad,
        kv_bias_grad,
        out_weight_grad,
        attn_grad,
        ffn_grad,
        gate_grad,
        up_grad,
        down_grad,
    )


def solution(mesh):
    in_specs = (
        P(("seq", "head"), None),
        P(("seq", "head"), None),
        P("seq", "head"),
        P(("seq", "head")),
        P(("seq", "head"), None),
        P(("seq", "head")),
        P("head", "seq"),
        P(("seq", "head")),
        P(("seq", "head")),
        P("seq", "head"),
        P("seq", "head"),
        P("head", "seq"),
        P(),
        P(),
        P(),
    )
    out_specs = (
        P(("seq", "head"), None),
        P(("seq", "head"), None),
        P("seq", "head"),
        P(("seq", "head")),
        P(("seq", "head"), None),
        P(("seq", "head")),
        P("head", "seq"),
        P(("seq", "head")),
        P(("seq", "head")),
        P("seq", "head"),
        P("seq", "head"),
        P("head", "seq"),
    )
    return jax.shard_map(local, mesh=mesh, in_specs=in_specs, out_specs=out_specs, check_vma=False)
```

```python
import functools

import jax
import jax.numpy as jnp
from jax import lax
from jax.experimental import pallas as pl
from jax.experimental.pallas import tpu as pltpu
from jax.sharding import PartitionSpec as P

HEADS = 16
KV = 2
HD = 128
BLK = 512
GROUP = HEADS // KV
TILE = 512
BATCH = 8
ROWS = 1024
UNITS = 256
GRAD_UNITS = 512

EPSILON = 1e-06
ROPE_BASE = 1000000.0
NEGATIVE = -1e30
SCALE = HD**-0.5
LOG2E = 1.4426950408889634

F32 = jnp.float32
BF16 = jnp.bfloat16

ORDER = ((0, 2, 4, 6, 1, 5, 3, 7), (0, 4, 2, 6, 1, 3, 5, 7))
RELAY = ((0, 1, 2, 3), (1, 0, 2, 3), (2, 3, 1, 0), (3, 2, 1, 0))


def contract(left_side, right_side, left_dim, right_dim):
    return lax.dot_general(
        left_side,
        right_side,
        (((left_dim,), (right_dim,)), ((), ())),
        preferred_element_type=F32,
    )


def after(value, *others):
    return lax.optimization_barrier((value, *others))[0]


class Lane:
    def __init__(self, depth):
        self.depth = depth
        self.done = []

    def __call__(self, send, value):
        if len(self.done) >= self.depth:
            value = after(value, self.done[-self.depth])
        self.done.append(send(value))
        return self.done[-1]


class SeqAxis:
    def __init__(self):
        self.size = lax.axis_size("seq")
        self.me = lax.axis_index("seq")
        self.fast = self.size == 8
        self.lane = Lane(2)
        places = jnp.arange(self.size, dtype=jnp.int32)
        if self.fast:
            odd = self.me % 2 == 1
            self.order = self.me ^ jnp.where(odd, jnp.array(ORDER[1]), jnp.array(ORDER[0]))
        else:
            self.order = places
        self.place = jnp.sum(
            jnp.where(self.order[:, None] == places[None, :], places[:, None], 0), axis=0
        )

    def swap(self, value, even, odd, ordered=True):
        pairs = [(i, i ^ (odd if i % 2 else even)) for i in range(self.size)]

        def send(item):
            return lax.ppermute(item, "seq", pairs)

        return self.lane(send, value) if ordered else send(value)

    def begin(self, value, ordered=True):
        if not self.fast:
            return [value]
        return [value, self.swap(value, 2, 4, ordered), self.swap(value, 4, 2, ordered)]

    def finish(self, begun, axis=0, ordered=True):
        if not self.fast:
            whole = lax.all_gather(begun[0], "seq", axis=axis, tiled=True)
            half = whole.shape[axis] // 2
            return [
                lax.slice_in_dim(whole, i * half, (i + 1) * half, axis=axis) for i in range(2)
            ]
        value, one, two = begun
        mine = jnp.concatenate([value, one, two, self.swap(one, 4, 2, ordered)], axis=axis)
        return [mine, self.swap(mine, 1, 1, False)]

    def gather(self, value, axis=0, ordered=True):
        return self.finish(self.begin(value, ordered), axis, ordered)

    def reduce(self, mine, other):
        if not self.fast:
            whole = jnp.concatenate([jnp.stack(mine(None)), other], axis=0)
            return lax.psum_scatter(whole, "seq", scatter_dimension=0, tiled=False).astype(F32)
        here, one, two, corner = mine(self.swap(other, 1, 1, False))
        corner = self.swap(corner, 4, 2)
        two = self.swap(two, 4, 2)
        one = self.swap(one + corner, 2, 4)
        return here.astype(F32) + two.astype(F32) + one.astype(F32)


class HeadAxis:
    def __init__(self):
        self.size = lax.axis_size("head")
        self.me = lax.axis_index("head")
        self.fast = self.size == 4
        self.inner = (self.me == 1) | (self.me == 2)
        self.relay = jnp.array(RELAY, jnp.int32)[self.me] if self.fast else None
        self.direct = self.me ^ jnp.arange(self.size, dtype=jnp.int32)

    def send(self, value, pairs):
        return lax.ppermute(value, "head", pairs)

    def gather(self, value):
        if not self.fast:
            return lax.all_gather(value, "head", axis=0, tiled=True), (value,)
        pair = [(0, 1), (1, 0), (2, 3), (3, 2)]
        middle = [(1, 2), (2, 1)]
        outward = [(1, 0), (2, 3)]
        slot1 = self.send(value, pair)
        near = self.send(value, middle)
        far = self.send(slot1, middle)
        slot2 = jnp.where(self.inner, near, self.send(near, outward))
        slot3 = jnp.where(self.inner, far, self.send(far, outward))
        return place([value, slot1, slot2, slot3], self.relay, 0), (slot1, near)

    def reduce(self, whole, beside):
        if not self.fast:
            return [lax.psum_scatter(whole, "head", scatter_dimension=0, tiled=True)]
        pair = [(0, 1), (1, 0), (2, 3), (3, 2)]
        middle = [(1, 2), (2, 1)]
        inward = [(0, 1), (3, 2)]
        rows = whole.shape[0] // self.size
        own, slot1, slot2, slot3 = (
            lax.dynamic_slice_in_dim(whole, self.relay[k] * rows, rows, 0) for k in range(4)
        )
        far = slot3 + after(self.send(slot3, inward), beside[0])
        near = self.send(after(slot2, far), inward)
        next_door = slot1 + after(self.send(far, middle), near, beside[1])
        near = slot2 + near
        return [own, after(self.send(next_door, pair), beside[2]), self.send(near, middle)]

    def gather_small(self, value, axis):
        if not self.fast:
            return lax.all_gather(value, "head", axis=axis, tiled=True)
        pieces = [value] + [
            self.send(value, [(i, i ^ k) for i in range(self.size)]) for k in range(1, 4)
        ]
        return place(pieces, self.direct, axis)

    def reduce_small(self, value, axis):
        if not self.fast:
            return lax.psum_scatter(value, "head", scatter_dimension=axis, tiled=True).astype(F32)
        width = value.shape[axis] // self.size
        total = None
        for k in range(self.size):
            part = lax.dynamic_slice_in_dim(value, (self.me ^ k) * width, width, axis)
            if k:
                part = self.send(part, [(i, i ^ k) for i in range(self.size)])
            total = part.astype(F32) if total is None else total + part.astype(F32)
        return total


def vmem():
    return pl.BlockSpec(memory_space=pltpu.VMEM)


def anywhere():
    return pl.BlockSpec(memory_space=pl.ANY)


def smem():
    return pl.BlockSpec(memory_space=pltpu.SMEM)


def place_kernel(axis, order_ref, *refs):
    out_ref = refs[-1]
    for k, piece_ref in enumerate(refs[:-1]):
        width = piece_ref.shape[axis]
        at = pl.ds(pl.multiple_of(order_ref[k] * width, width), width)
        if axis:
            out_ref[:, at] = piece_ref[...]
        else:
            out_ref[at, :] = piece_ref[...]


def place(pieces, order, axis):
    shape = list(pieces[0].shape)
    shape[axis] *= len(pieces)
    return pl.pallas_call(
        functools.partial(place_kernel, axis),
        out_shape=jax.ShapeDtypeStruct(shape, pieces[0].dtype),
        in_specs=[smem()] + [vmem()] * len(pieces),
        out_specs=vmem(),
        name="place",
    )(order, *pieces)


def shuffle_kernel(count, order_ref, *refs):
    for i in range(len(refs) // 2):
        in_ref, out_ref = refs[i], refs[len(refs) // 2 + i]
        width = in_ref.shape[1] // count
        for p in range(count):
            at = pl.ds(pl.multiple_of(order_ref[p] * width, width), width)
            out_ref[:, p * width : (p + 1) * width] = in_ref[:, at]


def shuffle(order, *values):
    return pl.pallas_call(
        functools.partial(shuffle_kernel, order.shape[0]),
        out_shape=[jax.ShapeDtypeStruct(v.shape, v.dtype) for v in values],
        in_specs=[smem()] + [vmem()] * len(values),
        out_specs=[vmem()] * len(values),
        name="shuffle",
    )(order, *values)


def turn(values, cosine, sine):
    return values * cosine + pltpu.roll(values, HD // 2, 1) * sine


def allowed_bias(tile, stream, first, shape):
    key = tile * TILE + lax.broadcasted_iota(jnp.int32, shape, 0)
    return jnp.where((key >= first) & (key <= stream), 0.0, NEGATIVE)


def fetch(half_a_ref, half_b_ref, whole_ref, sem_ref):
    half = half_a_ref.shape[0]
    copies = [
        pltpu.make_async_copy(ref, whole_ref.at[pl.ds(i * half, half)], sem_ref.at[i])
        for i, ref in enumerate((half_a_ref, half_b_ref))
    ]
    for copy in copies:
        copy.start()
    return copies


def forward_kernel(
    offset_ref, bound_ref, raw_ref, cos_ref, sin_ref, stream_ref, first_ref, half_a_ref, half_b_ref,
    query_ref, mixed_ref, lse_ref,
    top_ref, total_ref, sum_ref, bias_ref, turned_ref, kv_ref, sem_ref,
):
    copies = fetch(half_a_ref, half_b_ref, kv_ref, sem_ref)
    cosine, sine = cos_ref[...], sin_ref[...]
    for h in range(HEADS):
        query_ref[h] = turn(raw_ref[:, h * HD : (h + 1) * HD], cosine, sine).astype(BF16)
    top_ref[...] = jnp.full(top_ref.shape, NEGATIVE, F32)
    total_ref[...] = jnp.zeros(total_ref.shape, F32)
    sum_ref[...] = jnp.zeros(sum_ref.shape, F32)
    for copy in copies:
        copy.wait()

    def visit(tile, carry):
        start = pl.multiple_of(offset_ref[tile], TILE)
        bias_ref[...] = allowed_bias(tile, stream_ref[...], first_ref[...], bias_ref.shape)
        for g in range(KV):
            turned_ref[g] = kv_ref[pl.ds(start, TILE), (KV + g) * HD : (KV + g + 1) * HD].T
        for g in range(KV):
            keys = kv_ref[pl.ds(start, TILE), g * HD : (g + 1) * HD]

            def some(i, carry):
                heads = [g * GROUP + i * BATCH + b for b in range(BATCH)]
                old = [top_ref[h] for h in heads]
                total = [total_ref[h] for h in heads]
                summed = [sum_ref[h] for h in heads]
                scores = [contract(keys, query_ref[h], 1, 1) for h in heads]
                bias = bias_ref[...]
                turned = turned_ref[g]
                new, fresh, fades = [], [], []
                for b in range(BATCH):
                    score = scores[b] * (SCALE * LOG2E) + bias
                    peak = jnp.maximum(old[b], jnp.max(score, axis=0, keepdims=True))
                    weights = jnp.exp2(score - peak)
                    fade = jnp.exp2(old[b] - peak)
                    new.append(peak)
                    fades.append(fade)
                    total[b] = total[b] * fade + jnp.sum(weights, axis=0, keepdims=True)
                    fresh.append(contract(turned, weights.astype(BF16), 1, 0))
                for b, h in enumerate(heads):
                    top_ref[h] = new[b]
                    total_ref[h] = total[b]
                    sum_ref[h] = summed[b] * fades[b] + fresh[b]
                return carry

            lax.fori_loop(0, GROUP // BATCH, some, 0)
        return carry

    lax.fori_loop(bound_ref[0], bound_ref[1] + 1, visit, 0)
    for h in range(HEADS):
        lse_ref[h] = top_ref[h] + jnp.log2(total_ref[h])
        mixed_ref[:, h * HD : (h + 1) * HD] = (sum_ref[h] / total_ref[h]).T.astype(BF16)


def attention_forward(offsets, bounds, query_raw, cosine, sine, stream, first, kv_a, kv_b):
    rows = query_raw.shape[0]
    kv_shape = (2 * kv_a.shape[0], kv_a.shape[1])
    return pl.pallas_call(
        forward_kernel,
        out_shape=(
            jax.ShapeDtypeStruct((HEADS, rows, HD), BF16),
            jax.ShapeDtypeStruct((rows, HEADS * HD), BF16),
            jax.ShapeDtypeStruct((HEADS, 1, rows), F32),
        ),
        in_specs=[smem(), smem()] + [vmem()] * 5 + [anywhere()] * 2,
        out_specs=[vmem()] * 3,
        scratch_shapes=[
            pltpu.VMEM((HEADS, 1, rows), F32),
            pltpu.VMEM((HEADS, 1, rows), F32),
            pltpu.VMEM((HEADS, HD, rows), F32),
            pltpu.VMEM((TILE, rows), F32),
            pltpu.VMEM((KV, HD, TILE), BF16),
            pltpu.VMEM(kv_shape, BF16),
            pltpu.SemaphoreType.DMA((2,)),
        ],
        compiler_params=pltpu.CompilerParams(vmem_limit_bytes=48 << 20),
        cost_estimate=pl.CostEstimate(
            flops=4 * HEADS * rows * HD * 2048,
            transcendentals=HEADS * rows * 2048,
            bytes_accessed=kv_a.size * 4 + query_raw.size * 8,
        ),
        name="attention_forward",
    )(offsets, bounds, query_raw, cosine, sine, stream, first, kv_a, kv_b)


def backward_kernel(
    offset_ref, bound_ref, query_ref, cos_ref, sin_ref, stream_ref, first_ref,
    mixed_ref, grad_ref, lse_ref, half_a_ref, half_b_ref,
    d_query_ref, d_half_a_ref, d_half_b_ref,
    delta_ref, head_grad_ref, sum_ref, bias_ref, turned_ref, d_tile_ref, kv_ref, sem_ref,
):
    copies = fetch(half_a_ref, half_b_ref, kv_ref, sem_ref)
    half = half_a_ref.shape[0]
    for h in range(HEADS):
        part = grad_ref[:, h * HD : (h + 1) * HD]
        head_grad_ref[h] = part
        product = part.astype(F32) * mixed_ref[:, h * HD : (h + 1) * HD].astype(F32)
        delta_ref[h] = lax.dot_general(
            jnp.ones((8, HD), F32),
            product,
            (((1,), (1,)), ((), ())),
            precision=lax.Precision.HIGHEST,
            preferred_element_type=F32,
        )[:1]
    sum_ref[...] = jnp.zeros(sum_ref.shape, F32)
    d_half_a_ref[...] = jnp.zeros(d_half_a_ref.shape, BF16)
    d_half_b_ref[...] = jnp.zeros(d_half_b_ref.shape, BF16)
    for copy in copies:
        copy.wait()

    def visit(tile, carry):
        start = pl.multiple_of(offset_ref[tile], TILE)
        bias_ref[...] = allowed_bias(tile, stream_ref[...], first_ref[...], bias_ref.shape)
        d_tile_ref[...] = jnp.zeros(d_tile_ref.shape, F32)
        for g in range(KV):
            turned_ref[g] = kv_ref[pl.ds(start, TILE), g * HD : (g + 1) * HD].T
        for g in range(KV):
            keys = kv_ref[pl.ds(start, TILE), g * HD : (g + 1) * HD]
            values = kv_ref[pl.ds(start, TILE), (KV + g) * HD : (KV + g + 1) * HD]

            def some(i, carry):
                heads = [g * GROUP + i * BATCH + b for b in range(BATCH)]
                query = [query_ref[h] for h in heads]
                head_grad = [head_grad_ref[h] for h in heads]
                summed = [sum_ref[h] for h in heads]
                bias = bias_ref[...]
                turned = turned_ref[g]
                d_keys, d_values = d_tile_ref[g], d_tile_ref[KV + g]
                for b, h in enumerate(heads):
                    scores = contract(keys, query[b], 1, 1) * (SCALE * LOG2E) + bias
                    weights = jnp.exp2(scores - lse_ref[h])
                    d_weights = contract(values, head_grad[b], 1, 1)
                    d_scores = (weights * (d_weights - delta_ref[h])).astype(BF16)
                    d_keys += contract(d_scores, query[b], 1, 0)
                    d_values += contract(weights.astype(BF16), head_grad[b], 1, 0)
                    summed[b] += contract(turned, d_scores, 1, 0)
                for b, h in enumerate(heads):
                    sum_ref[h] = summed[b]
                d_tile_ref[g] = d_keys
                d_tile_ref[KV + g] = d_values
                return carry

            lax.fori_loop(0, GROUP // BATCH, some, 0)
        for i, d_ref in enumerate((d_half_a_ref, d_half_b_ref)):

            @pl.when(start // half == i)
            def _():
                at = pl.ds(pl.multiple_of(start - i * half, TILE), TILE)
                for g in range(KV):
                    d_ref[at, g * HD : (g + 1) * HD] = (d_tile_ref[g] * SCALE).astype(BF16)
                    d_ref[at, (KV + g) * HD : (KV + g + 1) * HD] = d_tile_ref[KV + g].astype(BF16)

        return carry

    lax.fori_loop(bound_ref[0], bound_ref[1] + 1, visit, 0)
    cosine, sine = cos_ref[...], -sin_ref[...]
    for h in range(HEADS):
        d_query_ref[:, h * HD : (h + 1) * HD] = turn(
            sum_ref[h].T * SCALE, cosine, sine
        ).astype(BF16)


def attention_backward(
    offsets, bounds, queries, cosine, sine, stream, first, mixed, d_mixed, lse, kv_a, kv_b
):
    rows = mixed.shape[0]
    kv_shape = (2 * kv_a.shape[0], kv_a.shape[1])
    return pl.pallas_call(
        backward_kernel,
        out_shape=(
            jax.ShapeDtypeStruct((rows, HEADS * HD), BF16),
            jax.ShapeDtypeStruct(kv_a.shape, BF16),
            jax.ShapeDtypeStruct(kv_b.shape, BF16),
        ),
        in_specs=[smem(), smem()] + [vmem()] * 8 + [anywhere()] * 2,
        out_specs=[vmem()] * 3,
        scratch_shapes=[
            pltpu.VMEM((HEADS, 1, rows), F32),
            pltpu.VMEM((HEADS, rows, HD), BF16),
            pltpu.VMEM((HEADS, HD, rows), F32),
            pltpu.VMEM((TILE, rows), F32),
            pltpu.VMEM((KV, HD, TILE), BF16),
            pltpu.VMEM((2 * KV, TILE, HD), F32),
            pltpu.VMEM(kv_shape, BF16),
            pltpu.SemaphoreType.DMA((2,)),
        ],
        compiler_params=pltpu.CompilerParams(vmem_limit_bytes=56 << 20),
        cost_estimate=pl.CostEstimate(
            flops=10 * HEADS * rows * HD * 2048,
            transcendentals=HEADS * rows * 2048,
            bytes_accessed=kv_a.size * 8 + mixed.size * 8,
        ),
        name="attention_backward",
    )(offsets, bounds, queries, cosine, sine, stream, first, mixed, d_mixed, lse, kv_a, kv_b)


def side_by_side(order_ref, weight_ref):
    return jnp.concatenate([weight_ref[order_ref[p]] for p in range(weight_ref.shape[0])], axis=1)


def ffn_kernel(
    order_ref, normed_ref, grad_ref, gate_ref, up_ref, down_a_ref, down_b_ref,
    act_ref, d_gate_ref, d_up_ref,
):
    step = ROWS

    def chunk(i, carry):
        at = pl.ds(pl.multiple_of(i * step, step), step)
        normed = normed_ref[at, :]
        gate = contract(normed, side_by_side(order_ref, gate_ref), 1, 1)
        up = contract(normed, side_by_side(order_ref, up_ref), 1, 1)
        down = [ref[p] for ref in (down_a_ref, down_b_ref) for p in range(ref.shape[0])]
        d_act = contract(grad_ref[at, :], jnp.concatenate(down, axis=1), 1, 1)
        sigmoid = jax.nn.sigmoid(gate)
        silu = gate * sigmoid
        act_ref[at, :] = (silu * up).astype(BF16)
        d_up_ref[at, :] = (d_act * silu).astype(BF16)
        d_gate_ref[at, :] = (d_act * up * (sigmoid + silu * (1.0 - sigmoid))).astype(BF16)
        return carry

    lax.fori_loop(0, normed_ref.shape[0] // step, chunk, 0)


def ffn_middle(order, normed, grad, gate, up, down_a, down_b):
    rows, depth = normed.shape
    pieces, units, piece = gate.shape
    width = UNITS
    whole = pl.BlockSpec((rows, depth), lambda i, order_ref: (0, 0), pipeline_mode=pl.Buffered(1))
    weight = pl.BlockSpec((pieces, width, piece), lambda i, order_ref: (0, i, 0))
    half = pl.BlockSpec((pieces // 2, width, piece), lambda i, order_ref: (0, i, 0))
    return pl.pallas_call(
        ffn_kernel,
        out_shape=(jax.ShapeDtypeStruct((rows, units), BF16),) * 3,
        grid_spec=pltpu.PrefetchScalarGridSpec(
            num_scalar_prefetch=1,
            grid=(pl.cdiv(units, width),),
            in_specs=[whole, whole, weight, weight, half, half],
            out_specs=[pl.BlockSpec((rows, width), lambda i, order_ref: (0, i))] * 3,
        ),
        compiler_params=pltpu.CompilerParams(vmem_limit_bytes=48 << 20),
        cost_estimate=pl.CostEstimate(
            flops=6 * rows * depth * units,
            transcendentals=rows * units,
            bytes_accessed=2 * (3 * depth * units + 3 * rows * units + 2 * rows * depth),
        ),
        name="ffn_middle",
    )(order, normed, grad, gate, up, down_a, down_b)


def back_kernel(order_ref, d_gate_ref, d_up_ref, gate_ref, up_ref, out_ref):
    out_ref[...] = (
        contract(d_gate_ref[...], gate_ref[0], 1, 0) + contract(d_up_ref[...], up_ref[0], 1, 0)
    ).astype(BF16)


def ffn_back(order, d_gate, d_up, gate, up):
    rows, units = d_gate.shape
    pieces, _, piece = gate.shape
    whole = pl.BlockSpec((rows, units), lambda i, order_ref: (0, 0), pipeline_mode=pl.Buffered(1))
    part = pl.BlockSpec((1, units, piece), lambda i, order_ref: (order_ref[i], 0, 0))
    return pl.pallas_call(
        back_kernel,
        out_shape=jax.ShapeDtypeStruct((rows, pieces * piece), BF16),
        grid_spec=pltpu.PrefetchScalarGridSpec(
            num_scalar_prefetch=1,
            grid=(pieces,),
            in_specs=[whole, whole, part, part],
            out_specs=pl.BlockSpec((rows, piece), lambda i, order_ref: (0, i)),
        ),
        compiler_params=pltpu.CompilerParams(vmem_limit_bytes=48 << 20),
        cost_estimate=pl.CostEstimate(
            flops=4 * rows * pieces * piece * units,
            transcendentals=0,
            bytes_accessed=2 * (2 * pieces * piece * units + 2 * rows * units),
        ),
        name="ffn_back",
    )(order, d_gate, d_up, gate, up)


def forth_kernel(act_ref, down_a_ref, down_b_ref, out_ref):
    count = pl.num_programs(0) // 2
    for i, down_ref in enumerate((down_a_ref, down_b_ref)):

        @pl.when(pl.program_id(0) // count == i)
        def _():
            out_ref[...] = contract(act_ref[...], down_ref[0], 1, 0).astype(BF16)


def ffn_forth(act, down_a, down_b):
    rows, units = act.shape
    count, _, piece = down_a.shape
    return pl.pallas_call(
        forth_kernel,
        out_shape=jax.ShapeDtypeStruct((rows, 2 * count * piece), BF16),
        grid=(2 * count,),
        in_specs=[
            pl.BlockSpec((rows, units), lambda i: (0, 0), pipeline_mode=pl.Buffered(1)),
            pl.BlockSpec((1, units, piece), lambda i: (jnp.minimum(i, count - 1), 0, 0)),
            pl.BlockSpec((1, units, piece), lambda i: (jnp.maximum(i - count, 0), 0, 0)),
        ],
        out_specs=pl.BlockSpec((rows, piece), lambda i: (0, i)),
        compiler_params=pltpu.CompilerParams(vmem_limit_bytes=48 << 20),
        cost_estimate=pl.CostEstimate(
            flops=4 * rows * count * piece * units,
            transcendentals=0,
            bytes_accessed=2 * (2 * count * piece * units + rows * units),
        ),
        name="ffn_forth",
    )(act, down_a, down_b)


def unit_grad_kernel(count, shift, added, stacked, order_ref, left_ref, right_ref, *refs):
    outs = refs[added:]
    piece = outs[0].shape[-1]
    turned = left_ref[...].T
    for p in range(count):
        at = pl.ds(pl.multiple_of(order_ref[shift + p] * piece, piece), piece)
        term = contract(turned, right_ref[:, at], 1, 0)
        if added:
            term = term + refs[0][p].astype(F32)
        if stacked:
            outs[0][p] = term.astype(BF16)
        else:
            outs[p][...] = term.astype(BF16)


def unit_grad(left, right, order, shift, count, piece, received=None, apart=False):
    rows, units = left.shape
    columns = right.shape[1]
    width = GRAD_UNITS if count <= 4 else UNITS
    stack = pl.BlockSpec((count, width, piece), lambda i, order_ref: (0, i, 0))
    single = pl.BlockSpec((width, piece), lambda i, order_ref: (i, 0))
    extra = [] if received is None else [received]
    if apart:
        out_shape = [jax.ShapeDtypeStruct((units, piece), BF16)] * count
        out_specs = [single] * count
    else:
        out_shape = jax.ShapeDtypeStruct((count, units, piece), BF16)
        out_specs = stack
    return pl.pallas_call(
        functools.partial(unit_grad_kernel, count, shift, len(extra), not apart),
        out_shape=out_shape,
        grid_spec=pltpu.PrefetchScalarGridSpec(
            num_scalar_prefetch=1,
            grid=(pl.cdiv(units, width),),
            in_specs=[
                pl.BlockSpec((rows, width), lambda i, order_ref: (0, i)),
                pl.BlockSpec(
                    (rows, columns), lambda i, order_ref: (0, 0), pipeline_mode=pl.Buffered(1)
                ),
            ]
            + [stack] * len(extra),
            out_specs=out_specs,
        ),
        compiler_params=pltpu.CompilerParams(vmem_limit_bytes=48 << 20),
        cost_estimate=pl.CostEstimate(
            flops=2 * rows * units * count * piece,
            transcendentals=0,
            bytes_accessed=2
            * (rows * units + rows * columns + (1 + len(extra)) * units * count * piece),
        ),
        name="unit_grad",
    )(order, left, right, *extra)


def rope_tables(position):
    half_width = HD // 2
    inverse = ROPE_BASE ** (-(jnp.arange(half_width, dtype=F32) * 2.0 / HD))
    angles = position.astype(F32)[:, None] * inverse[None, :]
    cosine, sine = jnp.cos(angles), jnp.sin(angles)
    return (
        jnp.concatenate([cosine, cosine], axis=1),
        jnp.concatenate([-sine, sine], axis=1),
    )


def rotate(values, cosine, sine):
    half_width = values.shape[-1] // 2
    swapped = jnp.concatenate([values[..., half_width:], values[..., :half_width]], axis=-1)
    return values * cosine + swapped * sine


def norm_forward(values, gain_vector):
    rms_scale = lax.rsqrt(jnp.mean(values * values, axis=1, keepdims=True) + EPSILON)
    return (values * rms_scale * gain_vector, rms_scale)


def norm_backward(values, rms_scale, gain_vector, gradient):
    weighted = gradient * gain_vector
    gain_grad = jnp.sum(gradient * values * rms_scale, axis=0)
    inner_mean = jnp.mean(weighted * values, axis=1, keepdims=True)
    return (rms_scale * weighted - values * rms_scale**3 * inner_mean, gain_grad)


def local(
    inputs,
    out_grad,
    q_weight,
    q_bias,
    kv_weight,
    kv_bias,
    out_weight,
    attn_gain,
    ffn_gain,
    gate_weight,
    up_weight,
    down_weight,
    block_order,
    long_docs,
    short_docs,
):
    seq, head = SeqAxis(), HeadAxis()
    local_rows, depth = inputs.shape
    span_rows = local_rows * head.size
    wide = KV * HD * 2
    half = depth // 2
    pieces = seq.size // 2

    inputs16, cotangent16 = shuffle(seq.order, inputs, out_grad)
    gate_all = lax.all_gather(gate_weight.T, "seq", axis=0, tiled=False)
    q_span = head.gather_small(q_weight, 1)
    out_span = head.gather_small(out_weight, 0)
    q_a, q_b = seq.gather(q_span)
    out_a, out_b = seq.gather(out_span, axis=1)

    kv_rows_each = kv_weight.shape[0]
    sizes = [q_bias.shape[0], kv_bias.shape[0], attn_gain.shape[0], ffn_gain.shape[0]]
    cuts = [sum(sizes[:i]) for i in range(5)]
    padded = -(-(kv_rows_each + 1) // 16) * 16
    strip = jnp.concatenate([q_bias, kv_bias, attn_gain, ffn_gain])
    strip = jnp.pad(strip[None, :], ((0, padded - kv_rows_each - 1), (0, wide - strip.shape[0])))
    pack = jnp.concatenate([kv_weight, strip], axis=0)
    pack_all = jnp.concatenate(seq.gather(head.gather_small(pack, 0), ordered=False), axis=0)
    pack_all = pack_all.reshape(seq.size, head.size, padded, wide)
    kv_full = pack_all[:, :, :kv_rows_each].reshape(depth, wide)
    strips = pack_all[:, :, kv_rows_each].astype(F32)

    def part_of(i):
        return strips[:, :, cuts[i] : cuts[i + 1]].reshape(seq.size, -1)

    q_bias_full = part_of(0)[seq.place].reshape(1, -1)
    kv_bias_full = part_of(1)[seq.place].reshape(1, -1)
    attn_gain32 = part_of(2).reshape(1, -1)
    ffn_gain32 = part_of(3).reshape(1, -1)

    lengths = jnp.concatenate([long_docs, short_docs])
    index = jnp.arange(lengths.shape[0], dtype=jnp.int32)
    starts = jnp.sum(jnp.where(index[None, :] < index[:, None], lengths[None, :], 0), axis=1)
    long_total = starts[long_docs.shape[0]]
    row_start = (seq.me * head.size + head.me) * local_rows
    stream = (
        block_order[row_start // BLK] * BLK
        + row_start % BLK
        + jnp.arange(local_rows, dtype=jnp.int32)
    )
    position = jnp.where(stream >= long_total, stream - long_total, stream)
    first = jnp.max(jnp.where(starts[None, :] <= stream[:, None], starts[None, :], 0), axis=1)
    cosine, sine = rope_tables(position)
    blocks = jnp.arange(block_order.shape[0], dtype=jnp.int32)
    storage = jnp.sum(
        jnp.where(block_order[:, None] == blocks[None, :], blocks[:, None], 0), axis=0
    )
    span_blocks = span_rows // BLK
    base = seq.place[storage // span_blocks] * span_rows + storage % span_blocks * BLK
    per_block = BLK // TILE
    offsets = (base[:, None] + jnp.arange(per_block, dtype=jnp.int32)[None, :] * TILE).reshape(-1)
    bounds = jnp.stack([first[0] // TILE, stream[-1] // TILE]).astype(jnp.int32)
    where = (offsets.astype(jnp.int32), bounds)
    tables = (cosine, sine, stream[None, :], first[None, :])

    residual = inputs16.astype(F32)
    normed32, attn_scale = norm_forward(residual, attn_gain32)
    normed = normed32.astype(BF16)
    kv_raw = jnp.dot(normed, kv_full, preferred_element_type=F32) + kv_bias_full
    key_part = rotate(
        kv_raw[:, : KV * HD].reshape(local_rows, KV, HD), cosine[:, None, :], sine[:, None, :]
    )
    kv_rows = jnp.concatenate(
        [key_part.reshape(local_rows, KV * HD), kv_raw[:, KV * HD :]], axis=1
    ).astype(BF16)
    query_raw = (
        jnp.dot(normed[:, :half], q_a, preferred_element_type=F32)
        + jnp.dot(normed[:, half:], q_b, preferred_element_type=F32)
        + q_bias_full
    )
    kv_span = head.gather_small(after(kv_rows, q_a, out_span), 0)
    cotangent_late = after(cotangent16, kv_span, gate_all)
    kv_halves = seq.gather(after(kv_span, cotangent_late))
    grad_all = lax.all_gather(cotangent_late, "head", axis=0, tiled=True)
    up_all = lax.all_gather(after(up_weight.T, kv_halves[0]), "seq", axis=0, tiled=False)
    queries, mixed, lse = attention_forward(*where, query_raw, *tables, *kv_halves)
    hidden = residual + jnp.concatenate(
        [jnp.dot(mixed, part, preferred_element_type=F32) for part in (out_a, out_b)], axis=1
    )
    normed2_32, ffn_scale = norm_forward(hidden, ffn_gain32)
    normed2 = normed2_32.astype(BF16)

    straight = jnp.arange(seq.size, dtype=jnp.int32)
    normed2_all, first_step = head.gather(normed2)
    down_begun = seq.begin(after(down_weight, *first_step))
    down_begun = [after(item, normed2_all) for item in down_begun]
    down = [
        half_of.reshape(pieces, -1, depth // seq.size) for half_of in seq.finish(down_begun)
    ]
    act, d_gate, d_up = ffn_middle(seq.order, normed2_all, grad_all, gate_all, up_all, *down)
    d_normed2_terms = ffn_back(seq.order, d_gate, d_up, gate_all, up_all)

    def total(parts):
        return sum(part.astype(F32) for part in parts)

    piece = depth // seq.size

    def by_lane(left, right):
        def mine(received):
            return unit_grad(left, right, straight, 0, pieces, piece, received, True)

        return seq.reduce(mine, unit_grad(left, right, straight, pieces, pieces, piece))

    def whole_grad(left, right):
        return unit_grad(after(left, d_normed2_terms), right, seq.place, 0, seq.size, piece)

    def scattered(whole):
        return lax.psum_scatter(whole, "seq", scatter_dimension=0, tiled=False).astype(F32)

    terms = [
        whole_grad(act, grad_all), whole_grad(d_gate, normed2_all), whole_grad(d_up, normed2_all)
    ]
    d_normed2 = total(head.reduce(d_normed2_terms, terms))
    down_grad, gate_grad, up_grad = (scattered(after(whole, d_normed2)) for whole in terms)
    gate_grad, up_grad = gate_grad.T, up_grad.T

    d_hidden_norm, ffn_gain_grad = norm_backward(hidden, ffn_scale, ffn_gain32, d_normed2)
    d_hidden = cotangent16.astype(F32) + d_hidden_norm
    d_attn = d_hidden.astype(BF16)
    d_mixed = (
        contract(d_attn[:, :half], out_a, 1, 1) + contract(d_attn[:, half:], out_b, 1, 1)
    ).astype(BF16)
    d_queries, d_kv_a, d_kv_b = attention_backward(
        *where, queries, *tables, mixed, d_mixed, lse, *kv_halves
    )

    ffn_terms = ffn_forth(after(act, d_normed2), *down)
    beside = (d_queries, d_kv_a, d_kv_b)
    (output,) = shuffle(seq.place, hidden + total(head.reduce(ffn_terms, beside)))

    def stacked(value):
        return value.reshape(pieces, value.shape[0] // pieces, value.shape[1])

    def adding(value):
        def add(received):
            return list(value if received is None else value + received)

        return add

    d_kv_span = seq.reduce(adding(stacked(d_kv_a)), stacked(d_kv_b))
    d_kv_own = head.reduce_small(d_kv_span.astype(BF16), 0)
    key_back = rotate(
        d_kv_own[:, : KV * HD].reshape(local_rows, KV, HD), cosine[:, None, :], -sine[:, None, :]
    )
    d_kv = jnp.concatenate(
        [key_back.reshape(local_rows, KV * HD), d_kv_own[:, KV * HD :]], axis=1
    ).astype(BF16)
    d_normed = jnp.concatenate(
        [contract(d_queries, part, 1, 1) for part in (q_a, q_b)], axis=1
    ) + contract(d_kv, kv_full, 1, 1)
    d_input_norm, attn_gain_grad = norm_backward(residual, attn_scale, attn_gain32, d_normed)
    (input_grad,) = shuffle(seq.place, d_hidden + d_input_norm)

    out_span = by_lane(mixed, d_attn)
    out_weight_grad = head.reduce_small(out_span.astype(BF16), 0)
    rest = (straight, 0, 1, d_queries.shape[1])

    def q_part(i, received):
        columns = normed[:, i * half : (i + 1) * half]
        if received is not None:
            received = received.reshape(1, half, -1)
        return stacked(unit_grad(columns, d_queries, *rest, received)[0])

    q_span = seq.reduce(lambda received: list(q_part(0, received)), q_part(1, None))
    q_weight_grad = head.reduce_small(q_span.astype(BF16), 1)
    kv_part = contract(normed, d_kv, 0, 0).reshape(seq.size, head.size, kv_rows_each, wide)
    q_bias_part = jnp.sum(d_queries.astype(F32), axis=0).reshape(seq.size, -1)[seq.order]
    kv_bias_part = jnp.sum(d_kv.astype(F32), axis=0).reshape(seq.size, -1)[seq.order]
    strips = jnp.concatenate(
        [
            item.reshape(seq.size, head.size, 1, -1)
            for item in (q_bias_part, kv_bias_part, attn_gain_grad, ffn_gain_grad)
        ],
        axis=3,
    )
    strips = jnp.pad(
        strips,
        ((0, 0), (0, 0), (0, padded - kv_rows_each - 1), (0, wide - strips.shape[3])),
    )
    small = jnp.concatenate([kv_part, strips], axis=2).astype(BF16)
    small = small.reshape(seq.size, head.size * padded, wide)
    small = seq.reduce(adding(small[:pieces]), small[pieces:])
    small = head.reduce_small(small.astype(BF16), 0)
    kv_weight_grad = small[:kv_rows_each]
    tail = small[kv_rows_each]
    q_bias_grad, kv_bias_grad, attn_grad, ffn_grad = (
        tail[cuts[i] : cuts[i + 1]] for i in range(4)
    )
    return (
        output,
        input_grad,
        q_weight_grad,
        q_bias_grad,
        kv_weight_grad,
        kv_bias_grad,
        out_weight_grad,
        attn_grad,
        ffn_grad,
        gate_grad,
        up_grad,
        down_grad,
    )


def solution(mesh):
    in_specs = (
        P(("seq", "head"), None),
        P(("seq", "head"), None),
        P("seq", "head"),
        P(("seq", "head")),
        P(("seq", "head"), None),
        P(("seq", "head")),
        P("head", "seq"),
        P(("seq", "head")),
        P(("seq", "head")),
        P("seq", "head"),
        P("seq", "head"),
        P("head", "seq"),
        P(),
        P(),
        P(),
    )
    out_specs = (
        P(("seq", "head"), None),
        P(("seq", "head"), None),
        P("seq", "head"),
        P(("seq", "head")),
        P(("seq", "head"), None),
        P(("seq", "head")),
        P("head", "seq"),
        P(("seq", "head")),
        P(("seq", "head")),
        P("seq", "head"),
        P("seq", "head"),
        P("head", "seq"),
    )
    return jax.shard_map(local, mesh=mesh, in_specs=in_specs, out_specs=out_specs, check_vma=False)
```

```python
import functools

import jax
import jax.numpy as jnp
from jax import lax
from jax.experimental import pallas as pl
from jax.experimental.pallas import tpu as pltpu
from jax.sharding import PartitionSpec as P

HEADS = 16
KV = 2
HD = 128
BLK = 512
GROUP = HEADS // KV
TILE = 512
BATCH = 8
ROWS = 1024
UNITS = 256
GRAD_UNITS = 512

EPSILON = 1e-06
ROPE_BASE = 1000000.0
NEGATIVE = -1e30
SCALE = HD**-0.5
LOG2E = 1.4426950408889634

F32 = jnp.float32
BF16 = jnp.bfloat16

ORDER = ((0, 2, 4, 6, 1, 5, 3, 7), (0, 4, 2, 6, 1, 3, 5, 7))
RELAY = ((0, 1, 2, 3), (1, 0, 2, 3), (2, 3, 1, 0), (3, 2, 1, 0))


def contract(left_side, right_side, left_dim, right_dim):
    return lax.dot_general(
        left_side,
        right_side,
        (((left_dim,), (right_dim,)), ((), ())),
        preferred_element_type=F32,
    )


def after(value, *others):
    return lax.optimization_barrier((value, *others))[0]


class Lane:
    def __init__(self, depth):
        self.depth = depth
        self.done = []

    def __call__(self, send, value):
        if len(self.done) >= self.depth:
            value = after(value, self.done[-self.depth])
        self.done.append(send(value))
        return self.done[-1]


class SeqAxis:
    def __init__(self):
        self.size = lax.axis_size("seq")
        self.me = lax.axis_index("seq")
        self.fast = self.size == 8
        self.lane = Lane(2)
        places = jnp.arange(self.size, dtype=jnp.int32)
        if self.fast:
            odd = self.me % 2 == 1
            self.order = self.me ^ jnp.where(odd, jnp.array(ORDER[1]), jnp.array(ORDER[0]))
        else:
            self.order = places
        self.place = jnp.sum(
            jnp.where(self.order[:, None] == places[None, :], places[:, None], 0), axis=0
        )

    def swap(self, value, even, odd, ordered=True):
        pairs = [(i, i ^ (odd if i % 2 else even)) for i in range(self.size)]

        def send(item):
            return lax.ppermute(item, "seq", pairs)

        return self.lane(send, value) if ordered else send(value)

    def begin(self, value, ordered=True):
        if not self.fast:
            return [value]
        return [value, self.swap(value, 2, 4, ordered), self.swap(value, 4, 2, ordered)]

    def finish(self, begun, axis=0, ordered=True):
        if not self.fast:
            whole = lax.all_gather(begun[0], "seq", axis=axis, tiled=True)
            half = whole.shape[axis] // 2
            return [
                lax.slice_in_dim(whole, i * half, (i + 1) * half, axis=axis) for i in range(2)
            ]
        value, one, two = begun
        mine = jnp.concatenate([value, one, two, self.swap(one, 4, 2, ordered)], axis=axis)
        return [mine, self.swap(mine, 1, 1, False)]

    def gather(self, value, axis=0, ordered=True):
        return self.finish(self.begin(value, ordered), axis, ordered)

    def reduce(self, mine, other):
        if not self.fast:
            whole = jnp.concatenate([jnp.stack(mine(None)), other], axis=0)
            return lax.psum_scatter(whole, "seq", scatter_dimension=0, tiled=False).astype(F32)
        here, one, two, corner = mine(self.swap(other, 1, 1, False))
        corner = self.swap(corner, 4, 2)
        two = self.swap(two, 4, 2)
        one = self.swap(one + corner, 2, 4)
        return here.astype(F32) + two.astype(F32) + one.astype(F32)


class HeadAxis:
    def __init__(self):
        self.size = lax.axis_size("head")
        self.me = lax.axis_index("head")
        self.fast = self.size == 4
        self.inner = (self.me == 1) | (self.me == 2)
        self.steps = None
        self.relay = jnp.array(RELAY, jnp.int32)[self.me] if self.fast else None
        self.direct = self.me ^ jnp.arange(self.size, dtype=jnp.int32)

    def send(self, value, pairs):
        return lax.ppermute(value, "head", pairs)

    def gather(self, value):
        if not self.fast:
            return lax.all_gather(value, "head", axis=0, tiled=True), (value,)
        pair = [(0, 1), (1, 0), (2, 3), (3, 2)]
        middle = [(1, 2), (2, 1)]
        outward = [(1, 0), (2, 3)]
        slot1 = self.send(value, pair)
        near = self.send(value, middle)
        far = self.send(slot1, middle)
        slot2 = jnp.where(self.inner, near, self.send(near, outward))
        slot3 = jnp.where(self.inner, far, self.send(far, outward))
        return place([value, slot1, slot2, slot3], self.relay, 0), (slot1, near)

    def reduce(self, whole, beside):
        if not self.fast:
            return [lax.psum_scatter(whole, "head", scatter_dimension=0, tiled=True)]
        pair = [(0, 1), (1, 0), (2, 3), (3, 2)]
        middle = [(1, 2), (2, 1)]
        inward = [(0, 1), (3, 2)]
        rows = whole.shape[0] // self.size
        own, slot1, slot2, slot3 = (
            lax.dynamic_slice_in_dim(whole, self.relay[k] * rows, rows, 0) for k in range(4)
        )
        far = slot3 + after(self.send(slot3, inward), beside[0])
        near = self.send(after(slot2, far), inward)
        next_door = slot1 + after(self.send(far, middle), near, beside[1])
        near = slot2 + near
        self.steps = [far, next_door]
        return [own, after(self.send(next_door, pair), beside[2]), self.send(near, middle)]

    def gather_small(self, value, axis):
        if not self.fast:
            return lax.all_gather(value, "head", axis=axis, tiled=True)
        pieces = [value] + [
            self.send(value, [(i, i ^ k) for i in range(self.size)]) for k in range(1, 4)
        ]
        return place(pieces, self.direct, axis)

    def reduce_small(self, value, axis):
        if not self.fast:
            return lax.psum_scatter(value, "head", scatter_dimension=axis, tiled=True).astype(F32)
        width = value.shape[axis] // self.size
        total = None
        for k in range(self.size):
            part = lax.dynamic_slice_in_dim(value, (self.me ^ k) * width, width, axis)
            if k:
                part = self.send(part, [(i, i ^ k) for i in range(self.size)])
            total = part.astype(F32) if total is None else total + part.astype(F32)
        return total


def vmem():
    return pl.BlockSpec(memory_space=pltpu.VMEM)


def anywhere():
    return pl.BlockSpec(memory_space=pl.ANY)


def smem():
    return pl.BlockSpec(memory_space=pltpu.SMEM)


def place_kernel(axis, order_ref, *refs):
    out_ref = refs[-1]
    for k, piece_ref in enumerate(refs[:-1]):
        width = piece_ref.shape[axis]
        at = pl.ds(pl.multiple_of(order_ref[k] * width, width), width)
        if axis:
            out_ref[:, at] = piece_ref[...]
        else:
            out_ref[at, :] = piece_ref[...]


def place(pieces, order, axis):
    shape = list(pieces[0].shape)
    shape[axis] *= len(pieces)
    return pl.pallas_call(
        functools.partial(place_kernel, axis),
        out_shape=jax.ShapeDtypeStruct(shape, pieces[0].dtype),
        in_specs=[smem()] + [vmem()] * len(pieces),
        out_specs=vmem(),
        name="place",
    )(order, *pieces)


def shuffle_kernel(count, order_ref, *refs):
    for i in range(len(refs) // 2):
        in_ref, out_ref = refs[i], refs[len(refs) // 2 + i]
        width = in_ref.shape[1] // count
        for p in range(count):
            at = pl.ds(pl.multiple_of(order_ref[p] * width, width), width)
            out_ref[:, p * width : (p + 1) * width] = in_ref[:, at]


def shuffle(order, *values):
    return pl.pallas_call(
        functools.partial(shuffle_kernel, order.shape[0]),
        out_shape=[jax.ShapeDtypeStruct(v.shape, v.dtype) for v in values],
        in_specs=[smem()] + [vmem()] * len(values),
        out_specs=[vmem()] * len(values),
        name="shuffle",
    )(order, *values)


def turn(values, cosine, sine):
    return values * cosine + pltpu.roll(values, HD // 2, 1) * sine


def allowed_bias(tile, stream, first, shape):
    key = tile * TILE + lax.broadcasted_iota(jnp.int32, shape, 0)
    return jnp.where((key >= first) & (key <= stream), 0.0, NEGATIVE)


def fetch(half_a_ref, half_b_ref, whole_ref, sem_ref):
    half = half_a_ref.shape[0]
    copies = [
        pltpu.make_async_copy(ref, whole_ref.at[pl.ds(i * half, half)], sem_ref.at[i])
        for i, ref in enumerate((half_a_ref, half_b_ref))
    ]
    for copy in copies:
        copy.start()
    return copies


def forward_kernel(
    offset_ref, bound_ref, raw_ref, cos_ref, sin_ref, stream_ref, first_ref, half_a_ref, half_b_ref,
    query_ref, mixed_ref, lse_ref,
    top_ref, total_ref, sum_ref, bias_ref, turned_ref, kv_ref, sem_ref,
):
    copies = fetch(half_a_ref, half_b_ref, kv_ref, sem_ref)
    cosine, sine = cos_ref[...], sin_ref[...]
    for h in range(HEADS):
        query_ref[h] = turn(raw_ref[:, h * HD : (h + 1) * HD], cosine, sine).astype(BF16)
    top_ref[...] = jnp.full(top_ref.shape, NEGATIVE, F32)
    total_ref[...] = jnp.zeros(total_ref.shape, F32)
    sum_ref[...] = jnp.zeros(sum_ref.shape, F32)
    for copy in copies:
        copy.wait()

    def visit(tile, carry):
        start = pl.multiple_of(offset_ref[tile], TILE)
        bias_ref[...] = allowed_bias(tile, stream_ref[...], first_ref[...], bias_ref.shape)
        for g in range(KV):
            turned_ref[g] = kv_ref[pl.ds(start, TILE), (KV + g) * HD : (KV + g + 1) * HD].T
        for g in range(KV):
            keys = kv_ref[pl.ds(start, TILE), g * HD : (g + 1) * HD]

            def some(i, carry):
                heads = [g * GROUP + i * BATCH + b for b in range(BATCH)]
                old = [top_ref[h] for h in heads]
                total = [total_ref[h] for h in heads]
                summed = [sum_ref[h] for h in heads]
                scores = [contract(keys, query_ref[h], 1, 1) for h in heads]
                bias = bias_ref[...]
                turned = turned_ref[g]
                new, fresh, fades = [], [], []
                for b in range(BATCH):
                    score = scores[b] * (SCALE * LOG2E) + bias
                    peak = jnp.maximum(old[b], jnp.max(score, axis=0, keepdims=True))
                    weights = jnp.exp2(score - peak)
                    fade = jnp.exp2(old[b] - peak)
                    new.append(peak)
                    fades.append(fade)
                    total[b] = total[b] * fade + jnp.sum(weights, axis=0, keepdims=True)
                    fresh.append(contract(turned, weights.astype(BF16), 1, 0))
                for b, h in enumerate(heads):
                    top_ref[h] = new[b]
                    total_ref[h] = total[b]
                    sum_ref[h] = summed[b] * fades[b] + fresh[b]
                return carry

            lax.fori_loop(0, GROUP // BATCH, some, 0)
        return carry

    lax.fori_loop(bound_ref[0], bound_ref[1] + 1, visit, 0)
    for h in range(HEADS):
        lse_ref[h] = top_ref[h] + jnp.log2(total_ref[h])
        mixed_ref[:, h * HD : (h + 1) * HD] = (sum_ref[h] / total_ref[h]).T.astype(BF16)


def attention_forward(offsets, bounds, query_raw, cosine, sine, stream, first, kv_a, kv_b):
    rows = query_raw.shape[0]
    kv_shape = (2 * kv_a.shape[0], kv_a.shape[1])
    return pl.pallas_call(
        forward_kernel,
        out_shape=(
            jax.ShapeDtypeStruct((HEADS, rows, HD), BF16),
            jax.ShapeDtypeStruct((rows, HEADS * HD), BF16),
            jax.ShapeDtypeStruct((HEADS, 1, rows), F32),
        ),
        in_specs=[smem(), smem()] + [vmem()] * 5 + [anywhere()] * 2,
        out_specs=[vmem()] * 3,
        scratch_shapes=[
            pltpu.VMEM((HEADS, 1, rows), F32),
            pltpu.VMEM((HEADS, 1, rows), F32),
            pltpu.VMEM((HEADS, HD, rows), F32),
            pltpu.VMEM((TILE, rows), F32),
            pltpu.VMEM((KV, HD, TILE), BF16),
            pltpu.VMEM(kv_shape, BF16),
            pltpu.SemaphoreType.DMA((2,)),
        ],
        compiler_params=pltpu.CompilerParams(vmem_limit_bytes=48 << 20),
        cost_estimate=pl.CostEstimate(
            flops=4 * HEADS * rows * HD * 2048,
            transcendentals=HEADS * rows * 2048,
            bytes_accessed=kv_a.size * 4 + query_raw.size * 8,
        ),
        name="attention_forward",
    )(offsets, bounds, query_raw, cosine, sine, stream, first, kv_a, kv_b)


def backward_kernel(
    offset_ref, bound_ref, query_ref, cos_ref, sin_ref, stream_ref, first_ref,
    mixed_ref, grad_ref, lse_ref, half_a_ref, half_b_ref,
    d_query_ref, d_half_a_ref, d_half_b_ref,
    delta_ref, head_grad_ref, sum_ref, bias_ref, turned_ref, d_tile_ref, kv_ref, sem_ref,
):
    copies = fetch(half_a_ref, half_b_ref, kv_ref, sem_ref)
    half = half_a_ref.shape[0]
    for h in range(HEADS):
        part = grad_ref[:, h * HD : (h + 1) * HD]
        head_grad_ref[h] = part
        product = part.astype(F32) * mixed_ref[:, h * HD : (h + 1) * HD].astype(F32)
        delta_ref[h] = lax.dot_general(
            jnp.ones((8, HD), F32),
            product,
            (((1,), (1,)), ((), ())),
            precision=lax.Precision.HIGHEST,
            preferred_element_type=F32,
        )[:1]
    sum_ref[...] = jnp.zeros(sum_ref.shape, F32)
    d_half_a_ref[...] = jnp.zeros(d_half_a_ref.shape, BF16)
    d_half_b_ref[...] = jnp.zeros(d_half_b_ref.shape, BF16)
    for copy in copies:
        copy.wait()

    def visit(tile, carry):
        start = pl.multiple_of(offset_ref[tile], TILE)
        bias_ref[...] = allowed_bias(tile, stream_ref[...], first_ref[...], bias_ref.shape)
        d_tile_ref[...] = jnp.zeros(d_tile_ref.shape, F32)
        for g in range(KV):
            turned_ref[g] = kv_ref[pl.ds(start, TILE), g * HD : (g + 1) * HD].T
        for g in range(KV):
            keys = kv_ref[pl.ds(start, TILE), g * HD : (g + 1) * HD]
            values = kv_ref[pl.ds(start, TILE), (KV + g) * HD : (KV + g + 1) * HD]

            def some(i, carry):
                heads = [g * GROUP + i * BATCH + b for b in range(BATCH)]
                query = [query_ref[h] for h in heads]
                head_grad = [head_grad_ref[h] for h in heads]
                summed = [sum_ref[h] for h in heads]
                bias = bias_ref[...]
                turned = turned_ref[g]
                d_keys, d_values = d_tile_ref[g], d_tile_ref[KV + g]
                for b, h in enumerate(heads):
                    scores = contract(keys, query[b], 1, 1) * (SCALE * LOG2E) + bias
                    weights = jnp.exp2(scores - lse_ref[h])
                    d_weights = contract(values, head_grad[b], 1, 1)
                    d_scores = (weights * (d_weights - delta_ref[h])).astype(BF16)
                    d_keys += contract(d_scores, query[b], 1, 0)
                    d_values += contract(weights.astype(BF16), head_grad[b], 1, 0)
                    summed[b] += contract(turned, d_scores, 1, 0)
                for b, h in enumerate(heads):
                    sum_ref[h] = summed[b]
                d_tile_ref[g] = d_keys
                d_tile_ref[KV + g] = d_values
                return carry

            lax.fori_loop(0, GROUP // BATCH, some, 0)
        for i, d_ref in enumerate((d_half_a_ref, d_half_b_ref)):

            @pl.when(start // half == i)
            def _():
                at = pl.ds(pl.multiple_of(start - i * half, TILE), TILE)
                for g in range(KV):
                    d_ref[at, g * HD : (g + 1) * HD] = (d_tile_ref[g] * SCALE).astype(BF16)
                    d_ref[at, (KV + g) * HD : (KV + g + 1) * HD] = d_tile_ref[KV + g].astype(BF16)

        return carry

    lax.fori_loop(bound_ref[0], bound_ref[1] + 1, visit, 0)
    cosine, sine = cos_ref[...], -sin_ref[...]
    for h in range(HEADS):
        d_query_ref[:, h * HD : (h + 1) * HD] = turn(
            sum_ref[h].T * SCALE, cosine, sine
        ).astype(BF16)


def attention_backward(
    offsets, bounds, queries, cosine, sine, stream, first, mixed, d_mixed, lse, kv_a, kv_b
):
    rows = mixed.shape[0]
    kv_shape = (2 * kv_a.shape[0], kv_a.shape[1])
    return pl.pallas_call(
        backward_kernel,
        out_shape=(
            jax.ShapeDtypeStruct((rows, HEADS * HD), BF16),
            jax.ShapeDtypeStruct(kv_a.shape, BF16),
            jax.ShapeDtypeStruct(kv_b.shape, BF16),
        ),
        in_specs=[smem(), smem()] + [vmem()] * 8 + [anywhere()] * 2,
        out_specs=[vmem()] * 3,
        scratch_shapes=[
            pltpu.VMEM((HEADS, 1, rows), F32),
            pltpu.VMEM((HEADS, rows, HD), BF16),
            pltpu.VMEM((HEADS, HD, rows), F32),
            pltpu.VMEM((TILE, rows), F32),
            pltpu.VMEM((KV, HD, TILE), BF16),
            pltpu.VMEM((2 * KV, TILE, HD), F32),
            pltpu.VMEM(kv_shape, BF16),
            pltpu.SemaphoreType.DMA((2,)),
        ],
        compiler_params=pltpu.CompilerParams(vmem_limit_bytes=56 << 20),
        cost_estimate=pl.CostEstimate(
            flops=10 * HEADS * rows * HD * 2048,
            transcendentals=HEADS * rows * 2048,
            bytes_accessed=kv_a.size * 8 + mixed.size * 8,
        ),
        name="attention_backward",
    )(offsets, bounds, queries, cosine, sine, stream, first, mixed, d_mixed, lse, kv_a, kv_b)


def side_by_side(order_ref, weight_ref):
    return jnp.concatenate([weight_ref[order_ref[p]] for p in range(weight_ref.shape[0])], axis=1)


def ffn_kernel(
    order_ref, normed_ref, grad_ref, gate_ref, up_ref, down_a_ref, down_b_ref,
    act_ref, d_gate_ref, d_up_ref,
):
    step = ROWS

    def chunk(i, carry):
        at = pl.ds(pl.multiple_of(i * step, step), step)
        normed = normed_ref[at, :]
        gate = contract(normed, side_by_side(order_ref, gate_ref), 1, 1)
        up = contract(normed, side_by_side(order_ref, up_ref), 1, 1)
        down = [ref[p] for ref in (down_a_ref, down_b_ref) for p in range(ref.shape[0])]
        d_act = contract(grad_ref[at, :], jnp.concatenate(down, axis=1), 1, 1)
        sigmoid = jax.nn.sigmoid(gate)
        silu = gate * sigmoid
        act_ref[at, :] = (silu * up).astype(BF16)
        d_up_ref[at, :] = (d_act * silu).astype(BF16)
        d_gate_ref[at, :] = (d_act * up * (sigmoid + silu * (1.0 - sigmoid))).astype(BF16)
        return carry

    lax.fori_loop(0, normed_ref.shape[0] // step, chunk, 0)


def ffn_middle(order, normed, grad, gate, up, down_a, down_b):
    rows, depth = normed.shape
    pieces, units, piece = gate.shape
    width = UNITS
    whole = pl.BlockSpec((rows, depth), lambda i, order_ref: (0, 0), pipeline_mode=pl.Buffered(1))
    weight = pl.BlockSpec((pieces, width, piece), lambda i, order_ref: (0, i, 0))
    half = pl.BlockSpec((pieces // 2, width, piece), lambda i, order_ref: (0, i, 0))
    return pl.pallas_call(
        ffn_kernel,
        out_shape=(jax.ShapeDtypeStruct((rows, units), BF16),) * 3,
        grid_spec=pltpu.PrefetchScalarGridSpec(
            num_scalar_prefetch=1,
            grid=(pl.cdiv(units, width),),
            in_specs=[whole, whole, weight, weight, half, half],
            out_specs=[pl.BlockSpec((rows, width), lambda i, order_ref: (0, i))] * 3,
        ),
        compiler_params=pltpu.CompilerParams(vmem_limit_bytes=48 << 20),
        cost_estimate=pl.CostEstimate(
            flops=6 * rows * depth * units,
            transcendentals=rows * units,
            bytes_accessed=2 * (3 * depth * units + 3 * rows * units + 2 * rows * depth),
        ),
        name="ffn_middle",
    )(order, normed, grad, gate, up, down_a, down_b)


def back_kernel(order_ref, d_gate_ref, d_up_ref, gate_ref, up_ref, out_ref):
    out_ref[...] = (
        contract(d_gate_ref[...], gate_ref[0], 1, 0) + contract(d_up_ref[...], up_ref[0], 1, 0)
    ).astype(BF16)


def ffn_back(order, d_gate, d_up, gate, up):
    rows, units = d_gate.shape
    pieces, _, piece = gate.shape
    whole = pl.BlockSpec((rows, units), lambda i, order_ref: (0, 0), pipeline_mode=pl.Buffered(1))
    part = pl.BlockSpec((1, units, piece), lambda i, order_ref: (order_ref[i], 0, 0))
    return pl.pallas_call(
        back_kernel,
        out_shape=jax.ShapeDtypeStruct((rows, pieces * piece), BF16),
        grid_spec=pltpu.PrefetchScalarGridSpec(
            num_scalar_prefetch=1,
            grid=(pieces,),
            in_specs=[whole, whole, part, part],
            out_specs=pl.BlockSpec((rows, piece), lambda i, order_ref: (0, i)),
        ),
        compiler_params=pltpu.CompilerParams(vmem_limit_bytes=48 << 20),
        cost_estimate=pl.CostEstimate(
            flops=4 * rows * pieces * piece * units,
            transcendentals=0,
            bytes_accessed=2 * (2 * pieces * piece * units + 2 * rows * units),
        ),
        name="ffn_back",
    )(order, d_gate, d_up, gate, up)


def forth_kernel(act_ref, down_a_ref, down_b_ref, out_ref):
    count = pl.num_programs(0) // 2
    for i, down_ref in enumerate((down_a_ref, down_b_ref)):

        @pl.when(pl.program_id(0) // count == i)
        def _():
            out_ref[...] = contract(act_ref[...], down_ref[0], 1, 0).astype(BF16)


def ffn_forth(act, down_a, down_b):
    rows, units = act.shape
    count, _, piece = down_a.shape
    return pl.pallas_call(
        forth_kernel,
        out_shape=jax.ShapeDtypeStruct((rows, 2 * count * piece), BF16),
        grid=(2 * count,),
        in_specs=[
            pl.BlockSpec((rows, units), lambda i: (0, 0), pipeline_mode=pl.Buffered(1)),
            pl.BlockSpec((1, units, piece), lambda i: (jnp.minimum(i, count - 1), 0, 0)),
            pl.BlockSpec((1, units, piece), lambda i: (jnp.maximum(i - count, 0), 0, 0)),
        ],
        out_specs=pl.BlockSpec((rows, piece), lambda i: (0, i)),
        compiler_params=pltpu.CompilerParams(vmem_limit_bytes=48 << 20),
        cost_estimate=pl.CostEstimate(
            flops=4 * rows * count * piece * units,
            transcendentals=0,
            bytes_accessed=2 * (2 * count * piece * units + rows * units),
        ),
        name="ffn_forth",
    )(act, down_a, down_b)


def unit_grad_kernel(count, shift, added, stacked, order_ref, left_ref, right_ref, *refs):
    outs = refs[added:]
    piece = outs[0].shape[-1]
    turned = left_ref[...].T
    for p in range(count):
        at = pl.ds(pl.multiple_of(order_ref[shift + p] * piece, piece), piece)
        term = contract(turned, right_ref[:, at], 1, 0)
        if added:
            term = term + refs[0][p].astype(F32)
        if stacked:
            outs[0][p] = term.astype(BF16)
        else:
            outs[p][...] = term.astype(BF16)


def unit_grad(left, right, order, shift, count, piece, received=None, apart=False):
    rows, units = left.shape
    columns = right.shape[1]
    width = GRAD_UNITS if count <= 4 else UNITS
    stack = pl.BlockSpec((count, width, piece), lambda i, order_ref: (0, i, 0))
    single = pl.BlockSpec((width, piece), lambda i, order_ref: (i, 0))
    extra = [] if received is None else [received]
    if apart:
        out_shape = [jax.ShapeDtypeStruct((units, piece), BF16)] * count
        out_specs = [single] * count
    else:
        out_shape = jax.ShapeDtypeStruct((count, units, piece), BF16)
        out_specs = stack
    return pl.pallas_call(
        functools.partial(unit_grad_kernel, count, shift, len(extra), not apart),
        out_shape=out_shape,
        grid_spec=pltpu.PrefetchScalarGridSpec(
            num_scalar_prefetch=1,
            grid=(pl.cdiv(units, width),),
            in_specs=[
                pl.BlockSpec((rows, width), lambda i, order_ref: (0, i)),
                pl.BlockSpec(
                    (rows, columns), lambda i, order_ref: (0, 0), pipeline_mode=pl.Buffered(1)
                ),
            ]
            + [stack] * len(extra),
            out_specs=out_specs,
        ),
        compiler_params=pltpu.CompilerParams(vmem_limit_bytes=48 << 20),
        cost_estimate=pl.CostEstimate(
            flops=2 * rows * units * count * piece,
            transcendentals=0,
            bytes_accessed=2
            * (rows * units + rows * columns + (1 + len(extra)) * units * count * piece),
        ),
        name="unit_grad",
    )(order, left, right, *extra)


def rope_tables(position):
    half_width = HD // 2
    inverse = ROPE_BASE ** (-(jnp.arange(half_width, dtype=F32) * 2.0 / HD))
    angles = position.astype(F32)[:, None] * inverse[None, :]
    cosine, sine = jnp.cos(angles), jnp.sin(angles)
    return (
        jnp.concatenate([cosine, cosine], axis=1),
        jnp.concatenate([-sine, sine], axis=1),
    )


def rotate(values, cosine, sine):
    half_width = values.shape[-1] // 2
    swapped = jnp.concatenate([values[..., half_width:], values[..., :half_width]], axis=-1)
    return values * cosine + swapped * sine


def norm_forward(values, gain_vector):
    rms_scale = lax.rsqrt(jnp.mean(values * values, axis=1, keepdims=True) + EPSILON)
    return (values * rms_scale * gain_vector, rms_scale)


def norm_backward(values, rms_scale, gain_vector, gradient):
    weighted = gradient * gain_vector
    gain_grad = jnp.sum(gradient * values * rms_scale, axis=0)
    inner_mean = jnp.mean(weighted * values, axis=1, keepdims=True)
    return (rms_scale * weighted - values * rms_scale**3 * inner_mean, gain_grad)


def local(
    inputs,
    out_grad,
    q_weight,
    q_bias,
    kv_weight,
    kv_bias,
    out_weight,
    attn_gain,
    ffn_gain,
    gate_weight,
    up_weight,
    down_weight,
    block_order,
    long_docs,
    short_docs,
):
    seq, head = SeqAxis(), HeadAxis()
    local_rows, depth = inputs.shape
    span_rows = local_rows * head.size
    wide = KV * HD * 2
    half = depth // 2
    pieces = seq.size // 2

    inputs16, cotangent16 = shuffle(seq.order, inputs, out_grad)
    gate_all = lax.all_gather(gate_weight.T, "seq", axis=0, tiled=False)
    q_span = head.gather_small(q_weight, 1)
    out_span = head.gather_small(out_weight, 0)
    q_a, q_b = seq.gather(q_span)
    out_a, out_b = seq.gather(out_span, axis=1)

    kv_rows_each = kv_weight.shape[0]
    sizes = [q_bias.shape[0], kv_bias.shape[0], attn_gain.shape[0], ffn_gain.shape[0]]
    cuts = [sum(sizes[:i]) for i in range(5)]
    padded = -(-(kv_rows_each + 1) // 16) * 16
    strip = jnp.concatenate([q_bias, kv_bias, attn_gain, ffn_gain])
    strip = jnp.pad(strip[None, :], ((0, padded - kv_rows_each - 1), (0, wide - strip.shape[0])))
    pack = jnp.concatenate([kv_weight, strip], axis=0)
    pack_all = jnp.concatenate(seq.gather(head.gather_small(pack, 0), ordered=False), axis=0)
    pack_all = pack_all.reshape(seq.size, head.size, padded, wide)
    kv_full = pack_all[:, :, :kv_rows_each].reshape(depth, wide)
    strips = pack_all[:, :, kv_rows_each].astype(F32)

    def part_of(i):
        return strips[:, :, cuts[i] : cuts[i + 1]].reshape(seq.size, -1)

    q_bias_full = part_of(0)[seq.place].reshape(1, -1)
    kv_bias_full = part_of(1)[seq.place].reshape(1, -1)
    attn_gain32 = part_of(2).reshape(1, -1)
    ffn_gain32 = part_of(3).reshape(1, -1)

    lengths = jnp.concatenate([long_docs, short_docs])
    index = jnp.arange(lengths.shape[0], dtype=jnp.int32)
    starts = jnp.sum(jnp.where(index[None, :] < index[:, None], lengths[None, :], 0), axis=1)
    long_total = starts[long_docs.shape[0]]
    row_start = (seq.me * head.size + head.me) * local_rows
    stream = (
        block_order[row_start // BLK] * BLK
        + row_start % BLK
        + jnp.arange(local_rows, dtype=jnp.int32)
    )
    position = jnp.where(stream >= long_total, stream - long_total, stream)
    first = jnp.max(jnp.where(starts[None, :] <= stream[:, None], starts[None, :], 0), axis=1)
    cosine, sine = rope_tables(position)
    blocks = jnp.arange(block_order.shape[0], dtype=jnp.int32)
    storage = jnp.sum(
        jnp.where(block_order[:, None] == blocks[None, :], blocks[:, None], 0), axis=0
    )
    span_blocks = span_rows // BLK
    base = seq.place[storage // span_blocks] * span_rows + storage % span_blocks * BLK
    per_block = BLK // TILE
    offsets = (base[:, None] + jnp.arange(per_block, dtype=jnp.int32)[None, :] * TILE).reshape(-1)
    bounds = jnp.stack([first[0] // TILE, stream[-1] // TILE]).astype(jnp.int32)
    where = (offsets.astype(jnp.int32), bounds)
    tables = (cosine, sine, stream[None, :], first[None, :])

    residual = inputs16.astype(F32)
    normed32, attn_scale = norm_forward(residual, attn_gain32)
    normed = normed32.astype(BF16)
    kv_raw = jnp.dot(normed, kv_full, preferred_element_type=F32) + kv_bias_full
    key_part = rotate(
        kv_raw[:, : KV * HD].reshape(local_rows, KV, HD), cosine[:, None, :], sine[:, None, :]
    )
    kv_rows = jnp.concatenate(
        [key_part.reshape(local_rows, KV * HD), kv_raw[:, KV * HD :]], axis=1
    ).astype(BF16)
    query_raw = (
        jnp.dot(normed[:, :half], q_a, preferred_element_type=F32)
        + jnp.dot(normed[:, half:], q_b, preferred_element_type=F32)
        + q_bias_full
    )
    kv_span = head.gather_small(after(kv_rows, q_a, out_span), 0)
    cotangent_late = after(cotangent16, kv_span, gate_all)
    kv_halves = seq.gather(after(kv_span, cotangent_late))
    grad_all = lax.all_gather(cotangent_late, "head", axis=0, tiled=True)
    up_all = lax.all_gather(after(up_weight.T, kv_halves[0]), "seq", axis=0, tiled=False)
    queries, mixed, lse = attention_forward(*where, query_raw, *tables, *kv_halves)
    hidden = residual + jnp.concatenate(
        [jnp.dot(mixed, part, preferred_element_type=F32) for part in (out_a, out_b)], axis=1
    )
    normed2_32, ffn_scale = norm_forward(hidden, ffn_gain32)
    normed2 = normed2_32.astype(BF16)

    straight = jnp.arange(seq.size, dtype=jnp.int32)
    normed2_all, first_step = head.gather(normed2)
    down_begun = seq.begin(after(down_weight, *first_step))
    down_begun = [after(item, normed2_all) for item in down_begun]
    down = [
        half_of.reshape(pieces, -1, depth // seq.size) for half_of in seq.finish(down_begun)
    ]
    act, d_gate, d_up = ffn_middle(seq.order, normed2_all, grad_all, gate_all, up_all, *down)
    d_normed2_terms = ffn_back(seq.order, d_gate, d_up, gate_all, up_all)

    def total(parts):
        return sum(part.astype(F32) for part in parts)

    piece = depth // seq.size

    def by_lane(left, right):
        def mine(received):
            return unit_grad(left, right, straight, 0, pieces, piece, received, True)

        return seq.reduce(mine, unit_grad(left, right, straight, pieces, pieces, piece))

    def whole_grad(left, right):
        return unit_grad(after(left, d_normed2_terms), right, seq.place, 0, seq.size, piece)

    def scattered(whole):
        return lax.psum_scatter(whole, "seq", scatter_dimension=0, tiled=False).astype(F32)

    terms = [
        whole_grad(act, grad_all), whole_grad(d_gate, normed2_all), whole_grad(d_up, normed2_all)
    ]
    d_normed2 = total(head.reduce(d_normed2_terms, terms))
    gates = [*(head.steps or [d_normed2] * 2), d_normed2]
    down_grad, gate_grad, up_grad = (
        scattered(after(whole, step)) for whole, step in zip(terms, gates, strict=True)
    )
    gate_grad, up_grad = gate_grad.T, up_grad.T

    d_hidden_norm, ffn_gain_grad = norm_backward(hidden, ffn_scale, ffn_gain32, d_normed2)
    d_hidden = cotangent16.astype(F32) + d_hidden_norm
    d_attn = d_hidden.astype(BF16)
    d_mixed = (
        contract(d_attn[:, :half], out_a, 1, 1) + contract(d_attn[:, half:], out_b, 1, 1)
    ).astype(BF16)
    d_queries, d_kv_a, d_kv_b = attention_backward(
        *where, queries, *tables, mixed, d_mixed, lse, *kv_halves
    )

    def stacked(value):
        return value.reshape(pieces, value.shape[0] // pieces, value.shape[1])

    def adding(value):
        def add(received):
            return list(value if received is None else value + received)

        return add

    d_kv_span = seq.reduce(adding(stacked(d_kv_a)), stacked(d_kv_b))
    ffn_terms = ffn_forth(after(act, d_kv_span), *down)
    beside = (d_kv_span, d_kv_span, d_kv_span)
    (output,) = shuffle(seq.place, hidden + total(head.reduce(ffn_terms, beside)))
    d_kv_own = head.reduce_small(d_kv_span.astype(BF16), 0)
    key_back = rotate(
        d_kv_own[:, : KV * HD].reshape(local_rows, KV, HD), cosine[:, None, :], -sine[:, None, :]
    )
    d_kv = jnp.concatenate(
        [key_back.reshape(local_rows, KV * HD), d_kv_own[:, KV * HD :]], axis=1
    ).astype(BF16)
    d_normed = jnp.concatenate(
        [contract(d_queries, part, 1, 1) for part in (q_a, q_b)], axis=1
    ) + contract(d_kv, kv_full, 1, 1)
    d_input_norm, attn_gain_grad = norm_backward(residual, attn_scale, attn_gain32, d_normed)
    (input_grad,) = shuffle(seq.place, d_hidden + d_input_norm)

    out_span = by_lane(mixed, d_attn)
    out_weight_grad = head.reduce_small(out_span.astype(BF16), 0)
    rest = (straight, 0, 1, d_queries.shape[1])

    def q_part(i, received):
        columns = normed[:, i * half : (i + 1) * half]
        if received is not None:
            received = received.reshape(1, half, -1)
        return stacked(unit_grad(columns, d_queries, *rest, received)[0])

    q_span = seq.reduce(lambda received: list(q_part(0, received)), q_part(1, None))
    q_weight_grad = head.reduce_small(q_span.astype(BF16), 1)
    kv_part = contract(normed, d_kv, 0, 0).reshape(seq.size, head.size, kv_rows_each, wide)
    q_bias_part = jnp.sum(d_queries.astype(F32), axis=0).reshape(seq.size, -1)[seq.order]
    kv_bias_part = jnp.sum(d_kv.astype(F32), axis=0).reshape(seq.size, -1)[seq.order]
    strips = jnp.concatenate(
        [
            item.reshape(seq.size, head.size, 1, -1)
            for item in (q_bias_part, kv_bias_part, attn_gain_grad, ffn_gain_grad)
        ],
        axis=3,
    )
    strips = jnp.pad(
        strips,
        ((0, 0), (0, 0), (0, padded - kv_rows_each - 1), (0, wide - strips.shape[3])),
    )
    small = jnp.concatenate([kv_part, strips], axis=2).astype(BF16)
    small = small.reshape(seq.size, head.size * padded, wide)
    small = seq.reduce(adding(small[:pieces]), small[pieces:])
    small = head.reduce_small(small.astype(BF16), 0)
    kv_weight_grad = small[:kv_rows_each]
    tail = small[kv_rows_each]
    q_bias_grad, kv_bias_grad, attn_grad, ffn_grad = (
        tail[cuts[i] : cuts[i + 1]] for i in range(4)
    )
    return (
        output,
        input_grad,
        q_weight_grad,
        q_bias_grad,
        kv_weight_grad,
        kv_bias_grad,
        out_weight_grad,
        attn_grad,
        ffn_grad,
        gate_grad,
        up_grad,
        down_grad,
    )


def solution(mesh):
    in_specs = (
        P(("seq", "head"), None),
        P(("seq", "head"), None),
        P("seq", "head"),
        P(("seq", "head")),
        P(("seq", "head"), None),
        P(("seq", "head")),
        P("head", "seq"),
        P(("seq", "head")),
        P(("seq", "head")),
        P("seq", "head"),
        P("seq", "head"),
        P("head", "seq"),
        P(),
        P(),
        P(),
    )
    out_specs = (
        P(("seq", "head"), None),
        P(("seq", "head"), None),
        P("seq", "head"),
        P(("seq", "head")),
        P(("seq", "head"), None),
        P(("seq", "head")),
        P("head", "seq"),
        P(("seq", "head")),
        P(("seq", "head")),
        P("seq", "head"),
        P("seq", "head"),
        P("head", "seq"),
    )
    return jax.shard_map(local, mesh=mesh, in_specs=in_specs, out_specs=out_specs, check_vma=False)
```

```python
import functools

import jax
import jax.numpy as jnp
from jax import lax
from jax.experimental import pallas as pl
from jax.experimental.pallas import tpu as pltpu
from jax.sharding import PartitionSpec as P

HEADS = 16
KV = 2
HD = 128
BLK = 512
GROUP = HEADS // KV
TILE = 512
BATCH = 8
ROWS = 1024
UNITS = 256
GRAD_UNITS = 512

EPSILON = 1e-06
ROPE_BASE = 1000000.0
NEGATIVE = -1e30
SCALE = HD**-0.5
LOG2E = 1.4426950408889634

F32 = jnp.float32
BF16 = jnp.bfloat16

ORDER = ((0, 2, 4, 6, 1, 5, 3, 7), (0, 4, 2, 6, 1, 3, 5, 7))
RELAY = ((0, 1, 2, 3), (1, 0, 2, 3), (2, 3, 1, 0), (3, 2, 1, 0))


def contract(left_side, right_side, left_dim, right_dim):
    return lax.dot_general(
        left_side,
        right_side,
        (((left_dim,), (right_dim,)), ((), ())),
        preferred_element_type=F32,
    )


def after(value, *others):
    return lax.optimization_barrier((value, *others))[0]


class Lane:
    def __init__(self, depth):
        self.depth = depth
        self.done = []

    def __call__(self, send, value):
        if len(self.done) >= self.depth:
            value = after(value, self.done[-self.depth])
        self.done.append(send(value))
        return self.done[-1]


class SeqAxis:
    def __init__(self):
        self.size = lax.axis_size("seq")
        self.me = lax.axis_index("seq")
        self.fast = self.size == 8
        self.lane = Lane(2)
        places = jnp.arange(self.size, dtype=jnp.int32)
        if self.fast:
            odd = self.me % 2 == 1
            self.order = self.me ^ jnp.where(odd, jnp.array(ORDER[1]), jnp.array(ORDER[0]))
        else:
            self.order = places
        self.place = jnp.sum(
            jnp.where(self.order[:, None] == places[None, :], places[:, None], 0), axis=0
        )

    def swap(self, value, even, odd, ordered=True):
        pairs = [(i, i ^ (odd if i % 2 else even)) for i in range(self.size)]

        def send(item):
            return lax.ppermute(item, "seq", pairs)

        return self.lane(send, value) if ordered else send(value)

    def begin(self, value, ordered=True, corner=False):
        if not self.fast:
            return [value]
        begun = [value, self.swap(value, 2, 4, ordered), self.swap(value, 4, 2, ordered)]
        return begun + [self.swap(value, 6, 6, ordered)] if corner else begun

    def finish(self, begun, axis=0, ordered=True):
        if not self.fast:
            whole = lax.all_gather(begun[0], "seq", axis=axis, tiled=True)
            half = whole.shape[axis] // 2
            return [
                lax.slice_in_dim(whole, i * half, (i + 1) * half, axis=axis) for i in range(2)
            ]
        if len(begun) == 3:
            begun = [*begun, self.swap(begun[1], 4, 2, ordered)]
        mine = jnp.concatenate(begun, axis=axis)
        return [mine, self.swap(mine, 1, 1, False)]

    def gather(self, value, axis=0, ordered=True):
        return self.finish(self.begin(value, ordered), axis, ordered)

    def reduce(self, mine, other):
        if not self.fast:
            whole = jnp.concatenate([jnp.stack(mine(None)), other], axis=0)
            return lax.psum_scatter(whole, "seq", scatter_dimension=0, tiled=False).astype(F32)
        here, one, two, corner = mine(self.swap(other, 1, 1, False))
        corner = self.swap(corner, 4, 2)
        two = self.swap(two, 4, 2)
        one = self.swap(one + corner, 2, 4)
        return here.astype(F32) + two.astype(F32) + one.astype(F32)


class HeadAxis:
    def __init__(self):
        self.size = lax.axis_size("head")
        self.me = lax.axis_index("head")
        self.fast = self.size == 4
        self.inner = (self.me == 1) | (self.me == 2)
        self.steps = None
        self.relay = jnp.array(RELAY, jnp.int32)[self.me] if self.fast else None
        self.direct = self.me ^ jnp.arange(self.size, dtype=jnp.int32)

    def send(self, value, pairs):
        return lax.ppermute(value, "head", pairs)

    def gather(self, value):
        if not self.fast:
            return lax.all_gather(value, "head", axis=0, tiled=True), (value,)
        pair = [(0, 1), (1, 0), (2, 3), (3, 2)]
        middle = [(1, 2), (2, 1)]
        outward = [(1, 0), (2, 3)]
        slot1 = self.send(value, pair)
        near = self.send(value, middle)
        far = self.send(slot1, middle)
        slot2 = jnp.where(self.inner, near, self.send(near, outward))
        slot3 = jnp.where(self.inner, far, self.send(far, outward))
        return place([value, slot1, slot2, slot3], self.relay, 0), (slot1, near)

    def reduce(self, whole, beside):
        if not self.fast:
            return [lax.psum_scatter(whole, "head", scatter_dimension=0, tiled=True)]
        pair = [(0, 1), (1, 0), (2, 3), (3, 2)]
        middle = [(1, 2), (2, 1)]
        inward = [(0, 1), (3, 2)]
        rows = whole.shape[0] // self.size
        own, slot1, slot2, slot3 = (
            lax.dynamic_slice_in_dim(whole, self.relay[k] * rows, rows, 0) for k in range(4)
        )
        far = slot3 + after(self.send(slot3, inward), beside[0])
        near = self.send(after(slot2, far), inward)
        next_door = slot1 + after(self.send(far, middle), near, beside[1])
        near = slot2 + near
        self.steps = [far, next_door]
        return [own, after(self.send(next_door, pair), beside[2]), self.send(near, middle)]

    def gather_small(self, value, axis):
        if not self.fast:
            return lax.all_gather(value, "head", axis=axis, tiled=True)
        pieces = [value] + [
            self.send(value, [(i, i ^ k) for i in range(self.size)]) for k in range(1, 4)
        ]
        return place(pieces, self.direct, axis)

    def reduce_small(self, value, axis):
        if not self.fast:
            return lax.psum_scatter(value, "head", scatter_dimension=axis, tiled=True).astype(F32)
        width = value.shape[axis] // self.size
        total = None
        for k in range(self.size):
            part = lax.dynamic_slice_in_dim(value, (self.me ^ k) * width, width, axis)
            if k:
                part = self.send(part, [(i, i ^ k) for i in range(self.size)])
            total = part.astype(F32) if total is None else total + part.astype(F32)
        return total


def vmem():
    return pl.BlockSpec(memory_space=pltpu.VMEM)


def anywhere():
    return pl.BlockSpec(memory_space=pl.ANY)


def smem():
    return pl.BlockSpec(memory_space=pltpu.SMEM)


def place_kernel(axis, order_ref, *refs):
    out_ref = refs[-1]
    for k, piece_ref in enumerate(refs[:-1]):
        width = piece_ref.shape[axis]
        at = pl.ds(pl.multiple_of(order_ref[k] * width, width), width)
        if axis:
            out_ref[:, at] = piece_ref[...]
        else:
            out_ref[at, :] = piece_ref[...]


def place(pieces, order, axis):
    shape = list(pieces[0].shape)
    shape[axis] *= len(pieces)
    return pl.pallas_call(
        functools.partial(place_kernel, axis),
        out_shape=jax.ShapeDtypeStruct(shape, pieces[0].dtype),
        in_specs=[smem()] + [vmem()] * len(pieces),
        out_specs=vmem(),
        name="place",
    )(order, *pieces)


def shuffle_kernel(count, order_ref, *refs):
    for i in range(len(refs) // 2):
        in_ref, out_ref = refs[i], refs[len(refs) // 2 + i]
        width = in_ref.shape[1] // count
        for p in range(count):
            at = pl.ds(pl.multiple_of(order_ref[p] * width, width), width)
            out_ref[:, p * width : (p + 1) * width] = in_ref[:, at]


def shuffle(order, *values):
    return pl.pallas_call(
        functools.partial(shuffle_kernel, order.shape[0]),
        out_shape=[jax.ShapeDtypeStruct(v.shape, v.dtype) for v in values],
        in_specs=[smem()] + [vmem()] * len(values),
        out_specs=[vmem()] * len(values),
        name="shuffle",
    )(order, *values)


def turn(values, cosine, sine):
    return values * cosine + pltpu.roll(values, HD // 2, 1) * sine


def allowed_bias(tile, stream, first, shape):
    key = tile * TILE + lax.broadcasted_iota(jnp.int32, shape, 0)
    return jnp.where((key >= first) & (key <= stream), 0.0, NEGATIVE)


def fetch(half_a_ref, half_b_ref, whole_ref, sem_ref):
    half = half_a_ref.shape[0]
    copies = [
        pltpu.make_async_copy(ref, whole_ref.at[pl.ds(i * half, half)], sem_ref.at[i])
        for i, ref in enumerate((half_a_ref, half_b_ref))
    ]
    for copy in copies:
        copy.start()
    return copies


def forward_kernel(
    offset_ref, bound_ref, raw_ref, cos_ref, sin_ref, stream_ref, first_ref, half_a_ref, half_b_ref,
    query_ref, mixed_ref, lse_ref,
    top_ref, total_ref, sum_ref, bias_ref, turned_ref, kv_ref, sem_ref,
):
    copies = fetch(half_a_ref, half_b_ref, kv_ref, sem_ref)
    cosine, sine = cos_ref[...], sin_ref[...]
    for h in range(HEADS):
        query_ref[h] = turn(raw_ref[:, h * HD : (h + 1) * HD], cosine, sine).astype(BF16)
    top_ref[...] = jnp.full(top_ref.shape, NEGATIVE, F32)
    total_ref[...] = jnp.zeros(total_ref.shape, F32)
    sum_ref[...] = jnp.zeros(sum_ref.shape, F32)
    for copy in copies:
        copy.wait()

    def visit(tile, carry):
        start = pl.multiple_of(offset_ref[tile], TILE)
        bias_ref[...] = allowed_bias(tile, stream_ref[...], first_ref[...], bias_ref.shape)
        for g in range(KV):
            turned_ref[g] = kv_ref[pl.ds(start, TILE), (KV + g) * HD : (KV + g + 1) * HD].T
        for g in range(KV):
            keys = kv_ref[pl.ds(start, TILE), g * HD : (g + 1) * HD]

            def some(i, carry):
                heads = [g * GROUP + i * BATCH + b for b in range(BATCH)]
                old = [top_ref[h] for h in heads]
                total = [total_ref[h] for h in heads]
                summed = [sum_ref[h] for h in heads]
                scores = [contract(keys, query_ref[h], 1, 1) for h in heads]
                bias = bias_ref[...]
                turned = turned_ref[g]
                new, fresh, fades = [], [], []
                for b in range(BATCH):
                    score = scores[b] * (SCALE * LOG2E) + bias
                    peak = jnp.maximum(old[b], jnp.max(score, axis=0, keepdims=True))
                    weights = jnp.exp2(score - peak)
                    fade = jnp.exp2(old[b] - peak)
                    new.append(peak)
                    fades.append(fade)
                    total[b] = total[b] * fade + jnp.sum(weights, axis=0, keepdims=True)
                    fresh.append(contract(turned, weights.astype(BF16), 1, 0))
                for b, h in enumerate(heads):
                    top_ref[h] = new[b]
                    total_ref[h] = total[b]
                    sum_ref[h] = summed[b] * fades[b] + fresh[b]
                return carry

            lax.fori_loop(0, GROUP // BATCH, some, 0)
        return carry

    lax.fori_loop(bound_ref[0], bound_ref[1] + 1, visit, 0)
    for h in range(HEADS):
        lse_ref[h] = top_ref[h] + jnp.log2(total_ref[h])
        mixed_ref[:, h * HD : (h + 1) * HD] = (sum_ref[h] / total_ref[h]).T.astype(BF16)


def attention_forward(offsets, bounds, query_raw, cosine, sine, stream, first, kv_a, kv_b):
    rows = query_raw.shape[0]
    kv_shape = (2 * kv_a.shape[0], kv_a.shape[1])
    return pl.pallas_call(
        forward_kernel,
        out_shape=(
            jax.ShapeDtypeStruct((HEADS, rows, HD), BF16),
            jax.ShapeDtypeStruct((rows, HEADS * HD), BF16),
            jax.ShapeDtypeStruct((HEADS, 1, rows), F32),
        ),
        in_specs=[smem(), smem()] + [vmem()] * 5 + [anywhere()] * 2,
        out_specs=[vmem()] * 3,
        scratch_shapes=[
            pltpu.VMEM((HEADS, 1, rows), F32),
            pltpu.VMEM((HEADS, 1, rows), F32),
            pltpu.VMEM((HEADS, HD, rows), F32),
            pltpu.VMEM((TILE, rows), F32),
            pltpu.VMEM((KV, HD, TILE), BF16),
            pltpu.VMEM(kv_shape, BF16),
            pltpu.SemaphoreType.DMA((2,)),
        ],
        compiler_params=pltpu.CompilerParams(vmem_limit_bytes=48 << 20),
        cost_estimate=pl.CostEstimate(
            flops=4 * HEADS * rows * HD * 2048,
            transcendentals=HEADS * rows * 2048,
            bytes_accessed=kv_a.size * 4 + query_raw.size * 8,
        ),
        name="attention_forward",
    )(offsets, bounds, query_raw, cosine, sine, stream, first, kv_a, kv_b)


def backward_kernel(
    offset_ref, bound_ref, query_ref, cos_ref, sin_ref, stream_ref, first_ref,
    mixed_ref, grad_ref, lse_ref, half_a_ref, half_b_ref,
    d_query_ref, d_half_a_ref, d_half_b_ref,
    delta_ref, head_grad_ref, sum_ref, bias_ref, turned_ref, d_tile_ref, kv_ref, sem_ref,
):
    copies = fetch(half_a_ref, half_b_ref, kv_ref, sem_ref)
    half = half_a_ref.shape[0]
    for h in range(HEADS):
        part = grad_ref[:, h * HD : (h + 1) * HD]
        head_grad_ref[h] = part
        product = part.astype(F32) * mixed_ref[:, h * HD : (h + 1) * HD].astype(F32)
        delta_ref[h] = lax.dot_general(
            jnp.ones((8, HD), F32),
            product,
            (((1,), (1,)), ((), ())),
            precision=lax.Precision.HIGHEST,
            preferred_element_type=F32,
        )[:1]
    sum_ref[...] = jnp.zeros(sum_ref.shape, F32)
    d_half_a_ref[...] = jnp.zeros(d_half_a_ref.shape, BF16)
    d_half_b_ref[...] = jnp.zeros(d_half_b_ref.shape, BF16)
    for copy in copies:
        copy.wait()

    def visit(tile, carry):
        start = pl.multiple_of(offset_ref[tile], TILE)
        bias_ref[...] = allowed_bias(tile, stream_ref[...], first_ref[...], bias_ref.shape)
        d_tile_ref[...] = jnp.zeros(d_tile_ref.shape, F32)
        for g in range(KV):
            turned_ref[g] = kv_ref[pl.ds(start, TILE), g * HD : (g + 1) * HD].T
        for g in range(KV):
            keys = kv_ref[pl.ds(start, TILE), g * HD : (g + 1) * HD]
            values = kv_ref[pl.ds(start, TILE), (KV + g) * HD : (KV + g + 1) * HD]

            def some(i, carry):
                heads = [g * GROUP + i * BATCH + b for b in range(BATCH)]
                query = [query_ref[h] for h in heads]
                head_grad = [head_grad_ref[h] for h in heads]
                summed = [sum_ref[h] for h in heads]
                bias = bias_ref[...]
                turned = turned_ref[g]
                d_keys, d_values = d_tile_ref[g], d_tile_ref[KV + g]
                for b, h in enumerate(heads):
                    scores = contract(keys, query[b], 1, 1) * (SCALE * LOG2E) + bias
                    weights = jnp.exp2(scores - lse_ref[h])
                    d_weights = contract(values, head_grad[b], 1, 1)
                    d_scores = (weights * (d_weights - delta_ref[h])).astype(BF16)
                    d_keys += contract(d_scores, query[b], 1, 0)
                    d_values += contract(weights.astype(BF16), head_grad[b], 1, 0)
                    summed[b] += contract(turned, d_scores, 1, 0)
                for b, h in enumerate(heads):
                    sum_ref[h] = summed[b]
                d_tile_ref[g] = d_keys
                d_tile_ref[KV + g] = d_values
                return carry

            lax.fori_loop(0, GROUP // BATCH, some, 0)
        for i, d_ref in enumerate((d_half_a_ref, d_half_b_ref)):

            @pl.when(start // half == i)
            def _():
                at = pl.ds(pl.multiple_of(start - i * half, TILE), TILE)
                for g in range(KV):
                    d_ref[at, g * HD : (g + 1) * HD] = (d_tile_ref[g] * SCALE).astype(BF16)
                    d_ref[at, (KV + g) * HD : (KV + g + 1) * HD] = d_tile_ref[KV + g].astype(BF16)

        return carry

    lax.fori_loop(bound_ref[0], bound_ref[1] + 1, visit, 0)
    cosine, sine = cos_ref[...], -sin_ref[...]
    for h in range(HEADS):
        d_query_ref[:, h * HD : (h + 1) * HD] = turn(
            sum_ref[h].T * SCALE, cosine, sine
        ).astype(BF16)


def attention_backward(
    offsets, bounds, queries, cosine, sine, stream, first, mixed, d_mixed, lse, kv_a, kv_b
):
    rows = mixed.shape[0]
    kv_shape = (2 * kv_a.shape[0], kv_a.shape[1])
    return pl.pallas_call(
        backward_kernel,
        out_shape=(
            jax.ShapeDtypeStruct((rows, HEADS * HD), BF16),
            jax.ShapeDtypeStruct(kv_a.shape, BF16),
            jax.ShapeDtypeStruct(kv_b.shape, BF16),
        ),
        in_specs=[smem(), smem()] + [vmem()] * 8 + [anywhere()] * 2,
        out_specs=[vmem()] * 3,
        scratch_shapes=[
            pltpu.VMEM((HEADS, 1, rows), F32),
            pltpu.VMEM((HEADS, rows, HD), BF16),
            pltpu.VMEM((HEADS, HD, rows), F32),
            pltpu.VMEM((TILE, rows), F32),
            pltpu.VMEM((KV, HD, TILE), BF16),
            pltpu.VMEM((2 * KV, TILE, HD), F32),
            pltpu.VMEM(kv_shape, BF16),
            pltpu.SemaphoreType.DMA((2,)),
        ],
        compiler_params=pltpu.CompilerParams(vmem_limit_bytes=56 << 20),
        cost_estimate=pl.CostEstimate(
            flops=10 * HEADS * rows * HD * 2048,
            transcendentals=HEADS * rows * 2048,
            bytes_accessed=kv_a.size * 8 + mixed.size * 8,
        ),
        name="attention_backward",
    )(offsets, bounds, queries, cosine, sine, stream, first, mixed, d_mixed, lse, kv_a, kv_b)


def side_by_side(order_ref, weight_ref):
    return jnp.concatenate([weight_ref[order_ref[p]] for p in range(weight_ref.shape[0])], axis=1)


def ffn_kernel(
    order_ref, normed_ref, grad_ref, gate_ref, up_ref, down_a_ref, down_b_ref,
    act_ref, d_gate_ref, d_up_ref,
):
    step = ROWS

    def chunk(i, carry):
        at = pl.ds(pl.multiple_of(i * step, step), step)
        normed = normed_ref[at, :]
        gate = contract(normed, side_by_side(order_ref, gate_ref), 1, 1)
        up = contract(normed, side_by_side(order_ref, up_ref), 1, 1)
        down = [ref[p] for ref in (down_a_ref, down_b_ref) for p in range(ref.shape[0])]
        d_act = contract(grad_ref[at, :], jnp.concatenate(down, axis=1), 1, 1)
        sigmoid = jax.nn.sigmoid(gate)
        silu = gate * sigmoid
        act_ref[at, :] = (silu * up).astype(BF16)
        d_up_ref[at, :] = (d_act * silu).astype(BF16)
        d_gate_ref[at, :] = (d_act * up * (sigmoid + silu * (1.0 - sigmoid))).astype(BF16)
        return carry

    lax.fori_loop(0, normed_ref.shape[0] // step, chunk, 0)


def ffn_middle(order, normed, grad, gate, up, down_a, down_b):
    rows, depth = normed.shape
    pieces, units, piece = gate.shape
    width = UNITS
    whole = pl.BlockSpec((rows, depth), lambda i, order_ref: (0, 0), pipeline_mode=pl.Buffered(1))
    weight = pl.BlockSpec((pieces, width, piece), lambda i, order_ref: (0, i, 0))
    half = pl.BlockSpec((pieces // 2, width, piece), lambda i, order_ref: (0, i, 0))
    return pl.pallas_call(
        ffn_kernel,
        out_shape=(jax.ShapeDtypeStruct((rows, units), BF16),) * 3,
        grid_spec=pltpu.PrefetchScalarGridSpec(
            num_scalar_prefetch=1,
            grid=(pl.cdiv(units, width),),
            in_specs=[whole, whole, weight, weight, half, half],
            out_specs=[pl.BlockSpec((rows, width), lambda i, order_ref: (0, i))] * 3,
        ),
        compiler_params=pltpu.CompilerParams(vmem_limit_bytes=48 << 20),
        cost_estimate=pl.CostEstimate(
            flops=6 * rows * depth * units,
            transcendentals=rows * units,
            bytes_accessed=2 * (3 * depth * units + 3 * rows * units + 2 * rows * depth),
        ),
        name="ffn_middle",
    )(order, normed, grad, gate, up, down_a, down_b)


def back_kernel(order_ref, d_gate_ref, d_up_ref, gate_ref, up_ref, out_ref):
    out_ref[...] = (
        contract(d_gate_ref[...], gate_ref[0], 1, 0) + contract(d_up_ref[...], up_ref[0], 1, 0)
    ).astype(BF16)


def ffn_back(order, d_gate, d_up, gate, up):
    rows, units = d_gate.shape
    pieces, _, piece = gate.shape
    whole = pl.BlockSpec((rows, units), lambda i, order_ref: (0, 0), pipeline_mode=pl.Buffered(1))
    part = pl.BlockSpec((1, units, piece), lambda i, order_ref: (order_ref[i], 0, 0))
    return pl.pallas_call(
        back_kernel,
        out_shape=jax.ShapeDtypeStruct((rows, pieces * piece), BF16),
        grid_spec=pltpu.PrefetchScalarGridSpec(
            num_scalar_prefetch=1,
            grid=(pieces,),
            in_specs=[whole, whole, part, part],
            out_specs=pl.BlockSpec((rows, piece), lambda i, order_ref: (0, i)),
        ),
        compiler_params=pltpu.CompilerParams(vmem_limit_bytes=48 << 20),
        cost_estimate=pl.CostEstimate(
            flops=4 * rows * pieces * piece * units,
            transcendentals=0,
            bytes_accessed=2 * (2 * pieces * piece * units + 2 * rows * units),
        ),
        name="ffn_back",
    )(order, d_gate, d_up, gate, up)


def forth_kernel(act_ref, down_a_ref, down_b_ref, out_ref):
    count = pl.num_programs(0) // 2
    for i, down_ref in enumerate((down_a_ref, down_b_ref)):

        @pl.when(pl.program_id(0) // count == i)
        def _():
            out_ref[...] = contract(act_ref[...], down_ref[0], 1, 0).astype(BF16)


def ffn_forth(act, down_a, down_b):
    rows, units = act.shape
    count, _, piece = down_a.shape
    return pl.pallas_call(
        forth_kernel,
        out_shape=jax.ShapeDtypeStruct((rows, 2 * count * piece), BF16),
        grid=(2 * count,),
        in_specs=[
            pl.BlockSpec((rows, units), lambda i: (0, 0), pipeline_mode=pl.Buffered(1)),
            pl.BlockSpec((1, units, piece), lambda i: (jnp.minimum(i, count - 1), 0, 0)),
            pl.BlockSpec((1, units, piece), lambda i: (jnp.maximum(i - count, 0), 0, 0)),
        ],
        out_specs=pl.BlockSpec((rows, piece), lambda i: (0, i)),
        compiler_params=pltpu.CompilerParams(vmem_limit_bytes=48 << 20),
        cost_estimate=pl.CostEstimate(
            flops=4 * rows * count * piece * units,
            transcendentals=0,
            bytes_accessed=2 * (2 * count * piece * units + rows * units),
        ),
        name="ffn_forth",
    )(act, down_a, down_b)


def unit_grad_kernel(count, shift, added, stacked, order_ref, left_ref, right_ref, *refs):
    outs = refs[added:]
    piece = outs[0].shape[-1]
    turned = left_ref[...].T
    for p in range(count):
        at = pl.ds(pl.multiple_of(order_ref[shift + p] * piece, piece), piece)
        term = contract(turned, right_ref[:, at], 1, 0)
        if added:
            term = term + refs[0][p].astype(F32)
        if stacked:
            outs[0][p] = term.astype(BF16)
        else:
            outs[p][...] = term.astype(BF16)


def unit_grad(left, right, order, shift, count, piece, received=None, apart=False):
    rows, units = left.shape
    columns = right.shape[1]
    width = GRAD_UNITS if count <= 4 else UNITS
    stack = pl.BlockSpec((count, width, piece), lambda i, order_ref: (0, i, 0))
    single = pl.BlockSpec((width, piece), lambda i, order_ref: (i, 0))
    extra = [] if received is None else [received]
    if apart:
        out_shape = [jax.ShapeDtypeStruct((units, piece), BF16)] * count
        out_specs = [single] * count
    else:
        out_shape = jax.ShapeDtypeStruct((count, units, piece), BF16)
        out_specs = stack
    return pl.pallas_call(
        functools.partial(unit_grad_kernel, count, shift, len(extra), not apart),
        out_shape=out_shape,
        grid_spec=pltpu.PrefetchScalarGridSpec(
            num_scalar_prefetch=1,
            grid=(pl.cdiv(units, width),),
            in_specs=[
                pl.BlockSpec((rows, width), lambda i, order_ref: (0, i)),
                pl.BlockSpec(
                    (rows, columns), lambda i, order_ref: (0, 0), pipeline_mode=pl.Buffered(1)
                ),
            ]
            + [stack] * len(extra),
            out_specs=out_specs,
        ),
        compiler_params=pltpu.CompilerParams(vmem_limit_bytes=48 << 20),
        cost_estimate=pl.CostEstimate(
            flops=2 * rows * units * count * piece,
            transcendentals=0,
            bytes_accessed=2
            * (rows * units + rows * columns + (1 + len(extra)) * units * count * piece),
        ),
        name="unit_grad",
    )(order, left, right, *extra)


def rope_tables(position):
    half_width = HD // 2
    inverse = ROPE_BASE ** (-(jnp.arange(half_width, dtype=F32) * 2.0 / HD))
    angles = position.astype(F32)[:, None] * inverse[None, :]
    cosine, sine = jnp.cos(angles), jnp.sin(angles)
    return (
        jnp.concatenate([cosine, cosine], axis=1),
        jnp.concatenate([-sine, sine], axis=1),
    )


def rotate(values, cosine, sine):
    half_width = values.shape[-1] // 2
    swapped = jnp.concatenate([values[..., half_width:], values[..., :half_width]], axis=-1)
    return values * cosine + swapped * sine


def norm_forward(values, gain_vector):
    rms_scale = lax.rsqrt(jnp.mean(values * values, axis=1, keepdims=True) + EPSILON)
    return (values * rms_scale * gain_vector, rms_scale)


def norm_backward(values, rms_scale, gain_vector, gradient):
    weighted = gradient * gain_vector
    gain_grad = jnp.sum(gradient * values * rms_scale, axis=0)
    inner_mean = jnp.mean(weighted * values, axis=1, keepdims=True)
    return (rms_scale * weighted - values * rms_scale**3 * inner_mean, gain_grad)


def local(
    inputs,
    out_grad,
    q_weight,
    q_bias,
    kv_weight,
    kv_bias,
    out_weight,
    attn_gain,
    ffn_gain,
    gate_weight,
    up_weight,
    down_weight,
    block_order,
    long_docs,
    short_docs,
):
    seq, head = SeqAxis(), HeadAxis()
    local_rows, depth = inputs.shape
    span_rows = local_rows * head.size
    wide = KV * HD * 2
    half = depth // 2
    pieces = seq.size // 2

    inputs16, cotangent16 = shuffle(seq.order, inputs, out_grad)
    gate_all = lax.all_gather(gate_weight.T, "seq", axis=0, tiled=False)
    q_span = head.gather_small(q_weight, 1)
    out_span = head.gather_small(out_weight, 0)
    q_a, q_b = seq.gather(q_span)
    out_a, out_b = seq.gather(out_span, axis=1)

    kv_rows_each = kv_weight.shape[0]
    sizes = [q_bias.shape[0], kv_bias.shape[0], attn_gain.shape[0], ffn_gain.shape[0]]
    cuts = [sum(sizes[:i]) for i in range(5)]
    padded = -(-(kv_rows_each + 1) // 16) * 16
    strip = jnp.concatenate([q_bias, kv_bias, attn_gain, ffn_gain])
    strip = jnp.pad(strip[None, :], ((0, padded - kv_rows_each - 1), (0, wide - strip.shape[0])))
    pack = jnp.concatenate([kv_weight, strip], axis=0)
    pack_all = jnp.concatenate(seq.gather(head.gather_small(pack, 0), ordered=False), axis=0)
    pack_all = pack_all.reshape(seq.size, head.size, padded, wide)
    kv_full = pack_all[:, :, :kv_rows_each].reshape(depth, wide)
    strips = pack_all[:, :, kv_rows_each].astype(F32)

    def part_of(i):
        return strips[:, :, cuts[i] : cuts[i + 1]].reshape(seq.size, -1)

    q_bias_full = part_of(0)[seq.place].reshape(1, -1)
    kv_bias_full = part_of(1)[seq.place].reshape(1, -1)
    attn_gain32 = part_of(2).reshape(1, -1)
    ffn_gain32 = part_of(3).reshape(1, -1)

    lengths = jnp.concatenate([long_docs, short_docs])
    index = jnp.arange(lengths.shape[0], dtype=jnp.int32)
    starts = jnp.sum(jnp.where(index[None, :] < index[:, None], lengths[None, :], 0), axis=1)
    long_total = starts[long_docs.shape[0]]
    row_start = (seq.me * head.size + head.me) * local_rows
    stream = (
        block_order[row_start // BLK] * BLK
        + row_start % BLK
        + jnp.arange(local_rows, dtype=jnp.int32)
    )
    position = jnp.where(stream >= long_total, stream - long_total, stream)
    first = jnp.max(jnp.where(starts[None, :] <= stream[:, None], starts[None, :], 0), axis=1)
    cosine, sine = rope_tables(position)
    blocks = jnp.arange(block_order.shape[0], dtype=jnp.int32)
    storage = jnp.sum(
        jnp.where(block_order[:, None] == blocks[None, :], blocks[:, None], 0), axis=0
    )
    span_blocks = span_rows // BLK
    base = seq.place[storage // span_blocks] * span_rows + storage % span_blocks * BLK
    per_block = BLK // TILE
    offsets = (base[:, None] + jnp.arange(per_block, dtype=jnp.int32)[None, :] * TILE).reshape(-1)
    bounds = jnp.stack([first[0] // TILE, stream[-1] // TILE]).astype(jnp.int32)
    where = (offsets.astype(jnp.int32), bounds)
    tables = (cosine, sine, stream[None, :], first[None, :])

    residual = inputs16.astype(F32)
    normed32, attn_scale = norm_forward(residual, attn_gain32)
    normed = normed32.astype(BF16)
    kv_raw = jnp.dot(normed, kv_full, preferred_element_type=F32) + kv_bias_full
    key_part = rotate(
        kv_raw[:, : KV * HD].reshape(local_rows, KV, HD), cosine[:, None, :], sine[:, None, :]
    )
    kv_rows = jnp.concatenate(
        [key_part.reshape(local_rows, KV * HD), kv_raw[:, KV * HD :]], axis=1
    ).astype(BF16)
    query_raw = (
        jnp.dot(normed[:, :half], q_a, preferred_element_type=F32)
        + jnp.dot(normed[:, half:], q_b, preferred_element_type=F32)
        + q_bias_full
    )
    kv_span = head.gather_small(after(kv_rows, q_a, out_span), 0)
    cotangent_late = after(cotangent16, kv_span, gate_all)
    kv_halves = seq.gather(after(kv_span, cotangent_late))
    grad_all = lax.all_gather(cotangent_late, "head", axis=0, tiled=True)
    up_all = lax.all_gather(after(up_weight.T, kv_halves[0]), "seq", axis=0, tiled=False)
    queries, mixed, lse = attention_forward(*where, query_raw, *tables, *kv_halves)
    hidden = residual + jnp.concatenate(
        [jnp.dot(mixed, part, preferred_element_type=F32) for part in (out_a, out_b)], axis=1
    )
    normed2_32, ffn_scale = norm_forward(hidden, ffn_gain32)
    normed2 = normed2_32.astype(BF16)

    straight = jnp.arange(seq.size, dtype=jnp.int32)
    normed2_all, first_step = head.gather(normed2)
    down_begun = seq.begin(after(down_weight, *first_step), corner=True)
    down_begun = [after(item, normed2_all) for item in down_begun]
    down = [
        half_of.reshape(pieces, -1, depth // seq.size) for half_of in seq.finish(down_begun)
    ]
    act, d_gate, d_up = ffn_middle(seq.order, normed2_all, grad_all, gate_all, up_all, *down)
    d_normed2_terms = ffn_back(seq.order, d_gate, d_up, gate_all, up_all)

    def total(parts):
        return sum(part.astype(F32) for part in parts)

    piece = depth // seq.size

    def by_lane(left, right):
        def mine(received):
            return unit_grad(left, right, straight, 0, pieces, piece, received, True)

        return seq.reduce(mine, unit_grad(left, right, straight, pieces, pieces, piece))

    def whole_grad(left, right):
        return unit_grad(after(left, d_normed2_terms), right, seq.place, 0, seq.size, piece)

    def scattered(whole):
        return lax.psum_scatter(whole, "seq", scatter_dimension=0, tiled=False).astype(F32)

    terms = [
        whole_grad(act, grad_all), whole_grad(d_gate, normed2_all), whole_grad(d_up, normed2_all)
    ]
    d_normed2 = total(head.reduce(d_normed2_terms, terms))
    gates = [*(head.steps or [d_normed2] * 2), d_normed2]
    down_grad, gate_grad, up_grad = (
        scattered(after(whole, step)) for whole, step in zip(terms, gates, strict=True)
    )
    gate_grad, up_grad = gate_grad.T, up_grad.T

    d_hidden_norm, ffn_gain_grad = norm_backward(hidden, ffn_scale, ffn_gain32, d_normed2)
    d_hidden = cotangent16.astype(F32) + d_hidden_norm
    d_attn = d_hidden.astype(BF16)
    d_mixed = (
        contract(d_attn[:, :half], out_a, 1, 1) + contract(d_attn[:, half:], out_b, 1, 1)
    ).astype(BF16)
    d_queries, d_kv_a, d_kv_b = attention_backward(
        *where, queries, *tables, mixed, d_mixed, lse, *kv_halves
    )

    def stacked(value):
        return value.reshape(pieces, value.shape[0] // pieces, value.shape[1])

    def adding(value):
        def add(received):
            return list(value if received is None else value + received)

        return add

    d_kv_span = seq.reduce(adding(stacked(d_kv_a)), stacked(d_kv_b))
    ffn_terms = ffn_forth(after(act, d_kv_span), *down)
    beside = (d_kv_span, d_kv_span, d_kv_span)
    (output,) = shuffle(seq.place, hidden + total(head.reduce(ffn_terms, beside)))
    d_kv_own = head.reduce_small(d_kv_span.astype(BF16), 0)
    key_back = rotate(
        d_kv_own[:, : KV * HD].reshape(local_rows, KV, HD), cosine[:, None, :], -sine[:, None, :]
    )
    d_kv = jnp.concatenate(
        [key_back.reshape(local_rows, KV * HD), d_kv_own[:, KV * HD :]], axis=1
    ).astype(BF16)
    d_normed = jnp.concatenate(
        [contract(d_queries, part, 1, 1) for part in (q_a, q_b)], axis=1
    ) + contract(d_kv, kv_full, 1, 1)
    d_input_norm, attn_gain_grad = norm_backward(residual, attn_scale, attn_gain32, d_normed)
    (input_grad,) = shuffle(seq.place, d_hidden + d_input_norm)

    out_span = by_lane(mixed, d_attn)
    out_weight_grad = head.reduce_small(out_span.astype(BF16), 0)
    rest = (straight, 0, 1, d_queries.shape[1])

    def q_part(i, received):
        columns = normed[:, i * half : (i + 1) * half]
        if received is not None:
            received = received.reshape(1, half, -1)
        return stacked(unit_grad(columns, d_queries, *rest, received)[0])

    q_span = seq.reduce(lambda received: list(q_part(0, received)), q_part(1, None))
    q_weight_grad = head.reduce_small(q_span.astype(BF16), 1)
    kv_part = contract(normed, d_kv, 0, 0).reshape(seq.size, head.size, kv_rows_each, wide)
    q_bias_part = jnp.sum(d_queries.astype(F32), axis=0).reshape(seq.size, -1)[seq.order]
    kv_bias_part = jnp.sum(d_kv.astype(F32), axis=0).reshape(seq.size, -1)[seq.order]
    strips = jnp.concatenate(
        [
            item.reshape(seq.size, head.size, 1, -1)
            for item in (q_bias_part, kv_bias_part, attn_gain_grad, ffn_gain_grad)
        ],
        axis=3,
    )
    strips = jnp.pad(
        strips,
        ((0, 0), (0, 0), (0, padded - kv_rows_each - 1), (0, wide - strips.shape[3])),
    )
    small = jnp.concatenate([kv_part, strips], axis=2).astype(BF16)
    small = small.reshape(seq.size, head.size * padded, wide)
    small = seq.reduce(adding(small[:pieces]), small[pieces:])
    small = head.reduce_small(small.astype(BF16), 0)
    kv_weight_grad = small[:kv_rows_each]
    tail = small[kv_rows_each]
    q_bias_grad, kv_bias_grad, attn_grad, ffn_grad = (
        tail[cuts[i] : cuts[i + 1]] for i in range(4)
    )
    return (
        output,
        input_grad,
        q_weight_grad,
        q_bias_grad,
        kv_weight_grad,
        kv_bias_grad,
        out_weight_grad,
        attn_grad,
        ffn_grad,
        gate_grad,
        up_grad,
        down_grad,
    )


def solution(mesh):
    in_specs = (
        P(("seq", "head"), None),
        P(("seq", "head"), None),
        P("seq", "head"),
        P(("seq", "head")),
        P(("seq", "head"), None),
        P(("seq", "head")),
        P("head", "seq"),
        P(("seq", "head")),
        P(("seq", "head")),
        P("seq", "head"),
        P("seq", "head"),
        P("head", "seq"),
        P(),
        P(),
        P(),
    )
    out_specs = (
        P(("seq", "head"), None),
        P(("seq", "head"), None),
        P("seq", "head"),
        P(("seq", "head")),
        P(("seq", "head"), None),
        P(("seq", "head")),
        P("head", "seq"),
        P(("seq", "head")),
        P(("seq", "head")),
        P("seq", "head"),
        P("seq", "head"),
        P("head", "seq"),
    )
    return jax.shard_map(local, mesh=mesh, in_specs=in_specs, out_specs=out_specs, check_vma=False)
```
